32 devices in a mesh: dp: 2 (over x), node: 4 (over z), local: 4 (over y, core).
Axes of the slice: x: 2, y: 2, z: 4, core: 2. Of those that a mesh axis runs over, the one named last changes fastest.
Arguments:
- tokens: bfloat16 [6144, 2048], P(('dp', 'node', 'local')), may hold values from -6 to 6
- cotangent: bfloat16 [6144, 2048], P(('dp', 'node', 'local')), may hold values from -6 to 6
- expert_of: int32 [6144, 1], P(('dp', 'node', 'local')), may hold values from 0 to 3; in each aligned block of 192 rows (0 to 191, 192 to 383, ...) at most 60 rows name the same one
- w1_codes: bfloat16 [4, 2048, 512], P('local', 'node'), may hold values from -4 to 4
- w1_scales: bfloat16 [4, 64, 512], P('local', 'node'), may hold values from 0.010986328 to 0.044921875
Outputs:
- grad_w2: bfloat16 [4, 2048, 512], P('local', 'node')
The draws below stay inside these ranges and needn't reach their ends.
Inputs may be any that keep to these rules, and one draw needn't show every extreme that they name: `expert_of`: within the rows of one device (aligned blocks of 192 rows) no expert is named by more than 60 rows, a bound that some block reaches.
All inputs are finite; a program needn't handle non-finite values.
Results may differ from the reference program's by a relative error of at most 0.018.
Values may be sent and summed in bfloat16 or wider, within the bound.
No kernel may reach another device: no remote copies, remote signals or barrier semaphores. Data moves between devices by JAX's collectives and lax.ppermute only.
A program may use at most 64 MiB of HBM per device.

```python
import math
import jax
import jax.numpy as jnp
import numpy as np
from jax import lax

D = 2048
FF = 512
QB = 32
TOK_DEV = 192
EXPERTS = 4
CAP = 60
TOKENS = 6144
N_DP = 2
N_NODE = 4
N_LOCAL = 4


def with_spikes(values, own_key, source, target, shards_of, factor):
    owner, partner = [(jnp.arange(values.shape[dim]) // (values.shape[dim] // shards_of)).reshape([-1 if axis == dim else 1 for axis in range(values.ndim)]) for dim in (source, target)]
    chosen = jax.random.permutation(own_key, shards_of)[partner]
    strong = (owner == chosen) | (owner == (partner + shards_of // 2) % shards_of)
    return jnp.where(strong, factor * values, values)


def level_of(stream_key, shape, pieces, least, largest):
    loudness = 1.0
    for axis_at, parts in pieces:
        draws = jax.random.uniform(jax.random.fold_in(jax.random.fold_in(stream_key, 6), axis_at), (parts,), jnp.float32, least / len(pieces), largest / len(pieces))
        loudness = loudness * jnp.repeat(jnp.exp(draws), shape[axis_at] // parts).reshape((-1,) + (1,) * (len(shape) - 1 - axis_at))
    return loudness


def routed_block(stream_key, own, number, rows, amount, top, reach, slope):
    order = jax.random.permutation(stream_key, amount)
    crowded, common = shares(amount, rows * top, reach, slope, True), shares(amount, rows * top, reach, slope, False)
    places = jnp.arange(amount)

    def named(tallies, turn):
        used = int((tallies > 0).sum())
        fixed = max(1, used // 4)
        moved = fixed + (places - fixed + turn * (used - fixed)) % max(1, amount - fixed)
        return jnp.zeros((amount,), jnp.int32).at[order[jnp.where(places < fixed, places, moved)]].set(jnp.asarray(tallies, jnp.int32))

    tallies = jnp.where(number % 4 == 0, named(crowded, number // 4), named(common, number - number // 4 - 1))
    mixed = jax.random.permutation(jax.random.fold_in(own, 3), amount)
    donor, sink = mixed[0:amount // 2 * 2:2], mixed[1:amount // 2 * 2:2]
    slack = jnp.minimum(tallies[donor] - 1, reach - tallies[sink]) // 2
    slack = jnp.where((donor == order[0]) | (sink == order[0]) | (tallies[sink] == 0), 0, jnp.maximum(slack, 0))
    moved = jax.random.randint(jax.random.fold_in(own, 4), (amount // 2,), 0, 1 << 20) % (slack + 1)
    tallies = tallies.at[donor].add(-moved).at[sink].add(moved)
    members = jnp.searchsorted(jnp.cumsum(tallies), jnp.arange(rows * top), side="right").astype(jnp.int32)
    table = members.reshape(top, rows).T
    table = table[jax.random.permutation(jax.random.fold_in(own, 1), rows)]
    turn = jax.random.randint(jax.random.fold_in(own, 2), (rows, 1), 0, top)
    return jnp.take_along_axis(table, (jnp.arange(top)[None, :] + turn) % top, axis=1)


def shares(count, total, limit, slope, full):
    loads = [(1 << 20) // math.isqrt(grade ** slope) + 1 for grade in range(1, count + 1)]
    largest = limit if full else min(limit, max(-(-total // count), total * loads[0] // sum(loads)))
    least = 1 if total - largest >= count - 1 else 0
    holding, spare = [largest] + [least] * (count - 1), total - largest - least * (count - 1)
    while spare > 0:
        movable = [i for i in range(1, count) if holding[i] < largest] or [i for i in range(1, count) if holding[i] < limit]
        pool, left = sum([loads[i] for i in movable]), spare
        for i in movable:
            more = min(limit - holding[i], max(1, left * loads[i] // pool), spare)
            holding[i] = holding[i] + more
            spare = spare - more
    return np.array(holding)


def scatter_about(rng, shape, scale, bound, split=(), kind=jnp.bfloat16):
    drawn = scale * jax.random.normal(rng, shape, jnp.float32)
    if split:
        drawn = drawn * level_of(rng, shape, split, -0.22, 0.18)
    return jnp.clip(drawn, -bound, bound).astype(kind)


def gaussian_with(rng, shape, spread, bound, shards, heavy, held_as=jnp.bfloat16):
    drawn = spread * jax.random.normal(rng, shape, jnp.float32)
    if shards:
        drawn = drawn * level_of(rng, shape, shards, -0.22, 0.18)
    return jnp.clip(with_spikes(drawn, jax.random.fold_in(rng, 3), *heavy), -bound, bound).astype(held_as)


def setup_inputs(seed: int = 0) -> dict:
    key_list = jax.random.split(jax.random.key(seed), 6)
    tokens = scatter_about(key_list[0], (TOKENS, D), 1.0, 6.0, ((0, 32),))
    cotangent = gaussian_with(key_list[1], (TOKENS, D), 1.0, 6.0, ((0, 32),), (0, 1, 32, 2.75))
    expert_of_keys = jax.random.split(jax.random.fold_in(key_list[2], 1), TOKENS // TOK_DEV)
    expert_of_turns = jax.random.permutation(jax.random.fold_in(key_list[2], 3), TOKENS // TOK_DEV)
    expert_of = jax.vmap(lambda own, number: routed_block(jax.random.fold_in(key_list[2], 2), own, number, TOK_DEV, EXPERTS, 1, CAP, 2))(expert_of_keys, expert_of_turns).reshape((TOKENS, 1))
    w1_codes = scatter_about(key_list[3], (EXPERTS, D, FF), 1.0, 4.0, ((0, 4), (1, 4)))
    w1_scales = jnp.clip(jnp.exp(math.log(0.044921875) - 1.40827327 * jax.random.uniform(key_list[4], (EXPERTS, D // QB, FF), jnp.float32) ** level_of(key_list[4], (EXPERTS, D // QB, FF), ((0, 4), (1, 4)), -0.2, 0.2)), 0.010986328, 0.044921875).astype(jnp.bfloat16)
    return dict(tokens=tokens, cotangent=cotangent, expert_of=expert_of, w1_codes=w1_codes, w1_scales=w1_scales)


def slot_of(expert_ids, experts, capacity):
    chosen = expert_ids[:, 0].astype(jnp.int32)
    onehot = (chosen[:, None] == jnp.arange(experts, dtype=jnp.int32)[None, :]).astype(jnp.int32)
    ranking = jnp.sum((jnp.cumsum(onehot, axis=0) - 1) * onehot, axis=1).astype(jnp.int32)
    return (chosen * capacity + ranking).astype(jnp.int32)


def place(row_data, slots, experts, capacity):
    blank_rows = jnp.zeros((experts * capacity, row_data.shape[1]), row_data.dtype)
    return blank_rows.at[slots].set(row_data).reshape(experts, capacity, row_data.shape[1])


def dequantize(weight_codes, block_scales):
    shaped = weight_codes.reshape(weight_codes.shape[:-2] + (block_scales.shape[-2], QB, weight_codes.shape[-1]))
    product = shaped.astype(jnp.float32) * block_scales[..., None, :].astype(jnp.float32)
    return product.astype(jnp.bfloat16).reshape(weight_codes.shape)


def reference(tokens, cotangent, expert_of, w1_codes, w1_scales):
    up_weight = dequantize(w1_codes, w1_scales).astype(jnp.float32)
    groups = N_DP * N_NODE
    x_groups = tokens.reshape(groups, N_LOCAL, TOK_DEV, D)
    dy_groups = cotangent.reshape(groups, N_LOCAL, TOK_DEV, D)
    id_groups = expert_of.reshape(groups, N_LOCAL, TOK_DEV, 1)
    factor = float(TOKENS // EXPERTS) ** -0.5

    def group_term(running, inputs):
        x_group, dy_group, id_group = inputs
        slots = jax.vmap(lambda ids: slot_of(ids, EXPERTS, CAP))(id_group)
        x_buffer = jax.vmap(lambda rows_in, where: place(rows_in, where, EXPERTS, CAP))(x_group, slots)
        dy_buffer = jax.vmap(lambda rows_in, where: place(rows_in, where, EXPERTS, CAP))(dy_group, slots)
        x_expert = jnp.swapaxes(x_buffer, 0, 1).reshape(EXPERTS, N_LOCAL * CAP, D).astype(jnp.float32)
        dy_expert = jnp.swapaxes(dy_buffer, 0, 1).reshape(EXPERTS, N_LOCAL * CAP, D).astype(jnp.float32)
        pre = jnp.einsum("emd,edf->emf", x_expert, up_weight)
        act = jax.nn.silu(pre).astype(jnp.bfloat16)
        second = jnp.einsum("emd,emf->edf", dy_expert, act.astype(jnp.float32))
        rounded = (second * factor).astype(jnp.bfloat16)
        rounded = lax.optimization_barrier(rounded)
        return running + rounded.astype(jnp.float32), None

    initial = jnp.zeros((EXPERTS, D, FF), jnp.float32)
    summed, _ = lax.scan(group_term, initial, (x_groups, dy_groups, id_groups))
    return summed.astype(jnp.bfloat16)
```

```python
import functools
import jax
import jax.numpy as jnp
from jax import lax
from jax.experimental import pallas as pl
from jax.experimental.pallas import tpu as pltpu
from jax.sharding import PartitionSpec as P

QB = 32
CHUNKS = 1
F32 = jnp.float32
BF16 = jnp.bfloat16


def mate(i, k, size):
    return i ^ k if size & (size - 1) == 0 else (i + k) % size


def origin(i, k, size):
    return i ^ k if size & (size - 1) == 0 else (i + size - k) % size


def traced_mate(i, k, size):
    return lax.bitwise_xor(i, jnp.int32(k)) if size & (size - 1) == 0 else lax.rem(i + k, size)


def traced_origin(i, k, size):
    if size & (size - 1) == 0:
        return lax.bitwise_xor(i, jnp.int32(k))
    return lax.rem(i + (size - k), size)


def call(body, outs, scalars, args, scratch=(), flops=0):
    moved = sum(a.size * a.dtype.itemsize for a in args)
    moved += sum(o.size * o.dtype.itemsize for o in outs)
    room = 2 * moved + (8 << 20)
    return pl.pallas_call(
        body,
        out_shape=outs,
        in_specs=[pl.BlockSpec(memory_space=pltpu.SMEM)]
        + [pl.BlockSpec(memory_space=pltpu.VMEM)] * len(args),
        out_specs=[pl.BlockSpec(memory_space=pltpu.VMEM)] * len(outs),
        scratch_shapes=list(scratch),
        compiler_params=pltpu.CompilerParams(vmem_limit_bytes=min(room, 60 << 20)),
        cost_estimate=pl.CostEstimate(flops=flops, bytes_accessed=moved, transcendentals=0),
    )(scalars, *args)


def shape(rows, cols, dtype):
    return jax.ShapeDtypeStruct((rows, cols), dtype)


def dequant_body(dims, pos, codes, scales, *refs):
    outs, full = refs[:-1], refs[-1]
    rows, ff = codes.shape
    mine = rows // dims[0]
    wide = codes[...].astype(F32).reshape(rows // QB, QB, ff)
    product = wide * scales[...].astype(F32)[:, None, :]
    full[...] = product.astype(BF16).reshape(rows, ff)
    kept = full[pl.ds(pl.multiple_of(pos[0] * mine, 16), mine), :]
    width = ff // len(outs)
    for i, out in enumerate(outs):
        out[...] = kept[:, i * width : (i + 1) * width]


def route_body(dims, cap, blocks, pos, ids, rows, *outs):
    copies, nodes, locals_ = dims
    count = rows.shape[0]
    lane = lax.broadcasted_iota(jnp.int32, (count, 128), 1)
    chosen = ids[...]
    onehot = chosen == lane
    before = lax.broadcasted_iota(jnp.int32, (count, count), 0)
    after = lax.broadcasted_iota(jnp.int32, (count, count), 1)
    lower = (after < before).astype(F32).astype(BF16)
    ranks = jnp.dot(lower, onehot.astype(F32).astype(BF16), preferred_element_type=F32)
    rank = jnp.sum(jnp.where(onehot, ranks, 0.0), axis=1, keepdims=True).astype(jnp.int32)
    if locals_ & (locals_ - 1) == 0:
        relative = lax.bitwise_xor(chosen, pos[2])
    else:
        relative = lax.rem(chosen - pos[2] + locals_, locals_)
    slot = relative * cap + rank
    places = lax.broadcasted_iota(jnp.int32, (count, locals_ * cap), 1)
    pick = jnp.transpose((slot == places).astype(F32)).astype(BF16)
    width = rows.shape[1] // (copies * blocks)
    for j in range(copies):
        which = traced_mate(pos[0], j, copies)
        for b in range(blocks):
            at = pl.multiple_of((b * copies + which) * width, 128)
            got = jnp.dot(pick, rows[:, pl.ds(at, width)], preferred_element_type=F32)
            got = got.astype(BF16)
            for k in range(locals_):
                out = outs[j * locals_ + k]
                out[:, b * width : (b + 1) * width] = got[k * cap : (k + 1) * cap]


def join_body(dims, pos, *refs):
    copies, nodes, locals_ = dims
    pieces, out = refs[:-1], refs[-1]
    cap = pieces[0].shape[0]
    for j in range(copies):
        base = traced_origin(pos[0], j, copies) * (locals_ * cap)
        for k in range(locals_):
            at = pl.multiple_of(base + k * cap, 16)
            out[pl.ds(at, cap), :] = pieces[j * locals_ + k][...]


def turn_body(dims, pos, *refs):
    pieces, out, held = refs[:-2], refs[-2], refs[-1]
    join_body(dims, pos, *pieces, held)
    out[...] = jnp.transpose(held[...])


def up_body(dims, pos, rows, *refs):
    copies, nodes, locals_ = dims
    weights, (kept, sent), held = refs[:nodes], refs[nodes : nodes + 2], refs[-1]
    mine = weights[0].shape[0]
    for s in range(nodes):
        at = pl.multiple_of(lax.rem(pos[1] + (nodes - s), nodes) * mine, 16)
        held[pl.ds(at, mine), :] = weights[s][...]
    pre = jnp.dot(rows[...], held[...], preferred_element_type=F32)
    kept[...] = pre
    sent[...] = pre.astype(BF16)


def down_body(dims, factor, pos, turned, kept, *refs):
    copies, nodes, locals_ = dims
    got, outs, act = refs[: -nodes - 1], refs[-nodes - 1 : -1], refs[-1]
    pre = kept[...]
    for part in got:
        pre = pre + part[...].astype(F32)
    act[...] = (pre * jax.nn.sigmoid(pre)).astype(BF16)
    mine = outs[0].shape[0]
    for s in reversed(range(nodes)):
        at = pl.multiple_of(lax.rem(pos[1] + s, nodes) * mine, 16)
        term = jnp.dot(turned[pl.ds(at, mine), :], act[...], preferred_element_type=F32)
        outs[s][...] = (term * factor).astype(outs[s].dtype)


def sum_body(pos, own, *refs):
    total = own[...]
    for part in refs[:-1]:
        total = total + part[...].astype(F32)
    refs[-1][...] = total.astype(BF16)


def lay_body(dims, chunks, pos, *refs):
    copies = dims[0]
    parts, out = refs[:-1], refs[-1]
    mine, width = parts[0].shape
    for j in range(copies):
        at = pl.multiple_of(traced_origin(pos[0], j, copies) * mine, 16)
        for i in range(chunks):
            out[pl.ds(at, mine), i * width : (i + 1) * width] = parts[i * copies + j][...]


def on_device(tokens, cotangent, expert_of, w1_codes, w1_scales):
    copies, nodes, locals_ = (lax.axis_size(a) for a in ("dp", "node", "local"))
    dims = (copies, nodes, locals_)
    count, features = tokens.shape
    capacity = 5 * count // (4 * locals_)
    cap = -(-capacity // 16) * 16
    shard, hidden = w1_codes.shape[1:]
    mine = shard // copies
    part = features // copies
    width = hidden // CHUNKS
    everyone = copies * locals_ * cap
    pos = jnp.stack([lax.axis_index(a) for a in ("dp", "node", "local")]).astype(jnp.int32)

    weights = call(
        functools.partial(dequant_body, dims),
        [shape(mine, width, BF16)] * CHUNKS,
        pos,
        [w1_codes[0], w1_scales[0]],
        [pltpu.VMEM((shard, hidden), BF16)],
    )
    order = [s for s in (2, 1, 3) if s < nodes] + list(range(4, nodes))
    held = []
    for chunk in weights:
        got = {0: chunk}
        for s in order:
            got[s] = lax.ppermute(chunk, "node", [(i, (i + s) % nodes) for i in range(nodes)])
        held.append([got[s] for s in range(nodes)])

    blocks = nodes
    if mine % 128:
        blocks = 1
        tokens, cotangent = (
            a.reshape(count, nodes, copies, mine).swapaxes(1, 2).reshape(count, features)
            for a in (tokens, cotangent)
        )

    def exchange(rows):
        pieces = call(
            functools.partial(route_body, dims, cap, blocks),
            [shape(cap, part, BF16)] * (copies * locals_),
            pos,
            [expert_of, rows],
            flops=2 * locals_ * cap * count * features,
        )
        moved = list(pieces)
        for k in reversed(range(locals_)):
            for j in reversed(range(copies)):
                if j or k:
                    pairs = [
                        (a * locals_ + b, mate(a, j, copies) * locals_ + mate(b, k, locals_))
                        for a in range(copies)
                        for b in range(locals_)
                    ]
                    at = j * locals_ + k
                    moved[at] = lax.ppermute(pieces[at], ("dp", "local"), pairs)
        return moved

    got_x = exchange(tokens)
    got_dy = exchange(cotangent)
    (rows_x,) = call(
        functools.partial(join_body, dims), [shape(everyone, part, BF16)], pos, got_x
    )
    (turned,) = call(
        functools.partial(turn_body, dims),
        [shape(part, everyone, BF16)],
        pos,
        got_dy,
        [pltpu.VMEM((everyone, part), BF16)],
    )
    factor = float(count * copies * nodes) ** (-0.5)
    finished = []
    for i in range(CHUNKS):
        kept, sent = call(
            functools.partial(up_body, dims),
            [shape(everyone, width, F32), shape(everyone, width, BF16)],
            pos,
            [rows_x] + held[i],
            [pltpu.VMEM((part, width), BF16)],
            flops=2 * everyone * part * width,
        )
        if copies == 2:
            others = [lax.ppermute(sent, "dp", [(0, 1), (1, 0)])]
        else:
            kept, others = lax.psum(kept, "dp"), []
        terms = call(
            functools.partial(down_body, dims, factor),
            [shape(mine, width, F32)] + [shape(mine, width, BF16)] * (nodes - 1),
            pos,
            [turned, kept] + others,
            [pltpu.VMEM((everyone, width), BF16)],
            flops=2 * everyone * part * width,
        )
        arrived = [
            lax.ppermute(terms[s], "node", [(a, (a + s) % nodes) for a in range(nodes)])
            for s in order
        ]
        (summed,) = call(sum_body, [shape(mine, width, BF16)], pos, [terms[0]] + arrived)
        finished.append(summed)
        for j in range(1, copies):
            finished.append(
                lax.ppermute(summed, "dp", [(a, mate(a, j, copies)) for a in range(copies)])
            )
    (result,) = call(
        functools.partial(lay_body, dims, CHUNKS), [shape(shard, hidden, BF16)], pos, finished
    )
    return result[None]


def solution(mesh):
    rows = P(("dp", "node", "local"), None)
    weights = P("local", "node", None)
    return jax.shard_map(
        on_device,
        mesh=mesh,
        in_specs=(rows, rows, rows, weights, weights),
        out_specs=weights,
        check_vma=False,
    )
```

```python
import functools
import jax
import jax.numpy as jnp
from jax import lax
from jax.experimental import pallas as pl
from jax.experimental.pallas import tpu as pltpu
from jax.sharding import PartitionSpec as P

QB = 32
CHUNKS = 2
F32 = jnp.float32
BF16 = jnp.bfloat16


def mate(i, k, size):
    return i ^ k if size & (size - 1) == 0 else (i + k) % size


def traced_mate(i, k, size):
    return lax.bitwise_xor(i, jnp.int32(k)) if size & (size - 1) == 0 else lax.rem(i + k, size)


def traced_origin(i, k, size):
    if size & (size - 1) == 0:
        return lax.bitwise_xor(i, jnp.int32(k))
    return lax.rem(i + (size - k), size)


def call(body, outs, scalars, args, scratch=(), flops=0, space=pltpu.VMEM):
    moved = sum(a.size * a.dtype.itemsize for a in args)
    moved += sum(o.size * o.dtype.itemsize for o in outs)
    room = 2 * moved + (8 << 20)
    return pl.pallas_call(
        body,
        out_shape=outs,
        in_specs=[pl.BlockSpec(memory_space=pltpu.SMEM)]
        + [pl.BlockSpec(memory_space=space)] * len(args),
        out_specs=[pl.BlockSpec(memory_space=pltpu.VMEM)] * len(outs),
        scratch_shapes=list(scratch),
        compiler_params=pltpu.CompilerParams(vmem_limit_bytes=min(room, 60 << 20)),
        cost_estimate=pl.CostEstimate(flops=flops, bytes_accessed=moved, transcendentals=0),
    )(scalars, *args)


def fence_body(pos, out):
    for i in range(pos.shape[0]):
        out[i] = pos[i]


def fence(pos):
    spec = pl.BlockSpec(memory_space=pltpu.SMEM)
    kind = jax.ShapeDtypeStruct(pos.shape, pos.dtype)
    return pl.pallas_call(fence_body, out_shape=kind, in_specs=[spec], out_specs=spec)(pos)


def shape(rows, cols, dtype):
    return jax.ShapeDtypeStruct((rows, cols), dtype)


def dequant_body(pos, codes, scales, *refs):
    outs, (raw, steps, wide, sems) = refs[:-4], refs[-4:]
    mine, ff = raw.shape
    at = pl.multiple_of(pos[0] * mine, 16)
    first = pltpu.make_async_copy(codes.at[pl.ds(at, mine), :], raw, sems.at[0])
    second = pltpu.make_async_copy(scales, steps, sems.at[1])
    first.start()
    second.start()
    second.wait()
    wide[...] = steps[...].astype(F32)
    used = max(1, mine // QB)
    begin = lax.div(pos[0] * mine, jnp.int32(QB))
    if used % 8 == 0:
        begin = pl.multiple_of(begin, 8)
    factors = wide[pl.ds(begin, used), :]
    first.wait()
    blocks = raw[...].astype(F32).reshape(used, mine // used, ff)
    kept = (blocks * factors[:, None, :]).astype(BF16).reshape(mine, ff)
    width = ff // len(outs)
    for i, out in enumerate(outs):
        out[...] = kept[:, i * width : (i + 1) * width]


def route_body(dims, cap, blocks, pos, ids, rows_x, rows_dy, *outs):
    copies, _, locals_ = dims
    count = rows_x.shape[0]
    high = max(16, locals_)
    if locals_ & (locals_ - 1) == 0:
        relative = lax.bitwise_xor(ids[...], pos[2])
    else:
        relative = lax.rem(ids[...] - pos[2] + locals_, locals_)
    onehot = relative == lax.broadcasted_iota(jnp.int32, (high, count), 0)
    first = lax.broadcasted_iota(jnp.int32, (count, count), 0)
    second = lax.broadcasted_iota(jnp.int32, (count, count), 1)
    earlier = (first < second).astype(F32).astype(BF16)
    ranks = jnp.dot(onehot.astype(F32).astype(BF16), earlier, preferred_element_type=F32)
    rank = jnp.sum(jnp.where(onehot, ranks, 0.0), axis=0, keepdims=True).astype(jnp.int32)
    slot = relative * cap + rank
    places = lax.broadcasted_iota(jnp.int32, (locals_ * cap, count), 0)
    pick = (slot == places).astype(F32).astype(BF16)
    width = rows_x.shape[1] // (copies * blocks)
    for half, rows in enumerate((rows_x, rows_dy)):
        for j in range(copies):
            which = traced_mate(pos[0], j, copies)
            for b in range(blocks):
                at = pl.multiple_of((b * copies + which) * width, 128)
                got = jnp.dot(pick, rows[:, pl.ds(at, width)], preferred_element_type=F32)
                got = got.astype(BF16)
                for k in range(locals_):
                    out = outs[(half * copies + j) * locals_ + k]
                    out[:, b * width : (b + 1) * width] = got[k * cap : (k + 1) * cap]


def join_body(dims, pos, *refs):
    copies, _, locals_ = dims
    pieces, out = refs[:-1], refs[-1]
    cap = pieces[0].shape[0]
    for j in range(copies):
        base = traced_origin(pos[0], j, copies) * (locals_ * cap)
        for k in range(locals_):
            at = pl.multiple_of(base + k * cap, 16)
            out[pl.ds(at, cap), :] = pieces[j * locals_ + k][...]


def turn_body(dims, pos, *refs):
    pieces, out, held = refs[:-2], refs[-2], refs[-1]
    join_body(dims, pos, *pieces, held)
    out[...] = jnp.transpose(held[...])


def up_body(dims, pos, rows, *refs):
    _, nodes, _ = dims
    weights, (kept, sent), held = refs[:nodes], refs[nodes : nodes + 2], refs[-1]
    mine = weights[0].shape[0]
    for s in range(nodes):
        at = pl.multiple_of(lax.rem(pos[1] + (nodes - s), nodes) * mine, 16)
        held[pl.ds(at, mine), :] = weights[s][...]
    pre = jnp.dot(rows[...], held[...], preferred_element_type=F32)
    kept[...] = pre
    sent[...] = pre.astype(BF16)


def down_body(dims, factor, pos, turned, kept, *refs):
    _, nodes, _ = dims
    got, outs, act = refs[: -nodes - 1], refs[-nodes - 1 : -1], refs[-1]
    pre = kept[...]
    for part in got:
        pre = pre + part[...].astype(F32)
    act[...] = (pre * jax.nn.sigmoid(pre)).astype(BF16)
    mine = outs[0].shape[0]
    for s in reversed(range(nodes)):
        at = pl.multiple_of(lax.rem(pos[1] + s, nodes) * mine, 16)
        term = jnp.dot(turned[pl.ds(at, mine), :], act[...], preferred_element_type=F32)
        outs[s][...] = (term * factor).astype(outs[s].dtype)


def sum_body(pos, own, *refs):
    total = own[...]
    for part in refs[:-1]:
        total = total + part[...].astype(F32)
    refs[-1][...] = total.astype(BF16)


def lay_body(dims, chunks, pos, *refs):
    copies = dims[0]
    parts, out = refs[:-1], refs[-1]
    mine, width = parts[0].shape
    for j in range(copies):
        at = pl.multiple_of(traced_origin(pos[0], j, copies) * mine, 16)
        for i in range(chunks):
            out[pl.ds(at, mine), i * width : (i + 1) * width] = parts[i * copies + j][...]


def on_device(tokens, cotangent, expert_of, w1_codes, w1_scales):
    copies, nodes, locals_ = (lax.axis_size(a) for a in ("dp", "node", "local"))
    dims = (copies, nodes, locals_)
    count, features = tokens.shape
    capacity = 5 * count // (4 * locals_)
    cap = -(-capacity // 16) * 16
    shard, hidden = w1_codes.shape[1:]
    mine = shard // copies
    part = features // copies
    width = hidden // CHUNKS
    everyone = copies * locals_ * cap
    pos = jnp.stack([lax.axis_index(a) for a in ("dp", "node", "local")]).astype(jnp.int32)

    weights = call(
        dequant_body,
        [shape(mine, width, BF16)] * CHUNKS,
        pos,
        [w1_codes[0], w1_scales[0]],
        [
            pltpu.VMEM((mine, hidden), BF16),
            pltpu.VMEM((shard // QB, hidden), BF16),
            pltpu.VMEM((shard // QB, hidden), F32),
            pltpu.SemaphoreType.DMA((2,)),
        ],
        space=pltpu.HBM,
    )
    order = [s for s in (2, 1, 3) if s < nodes] + list(range(4, nodes))
    held = []
    for chunk in weights:
        got = {0: chunk}
        for s in order:
            got[s] = lax.ppermute(chunk, "node", [(a, (a + s) % nodes) for a in range(nodes)])
        held.append([got[s] for s in range(nodes)])

    blocks = nodes
    if mine % 128:
        blocks = 1
        tokens, cotangent = (
            a.reshape(count, nodes, copies, mine).swapaxes(1, 2).reshape(count, features)
            for a in (tokens, cotangent)
        )

    pieces = call(
        functools.partial(route_body, dims, cap, blocks),
        [shape(cap, part, BF16)] * (2 * copies * locals_),
        pos,
        [expert_of.reshape(1, count), tokens, cotangent],
        flops=4 * locals_ * cap * count * features,
    )

    def exchange(pieces):
        moved = list(pieces)
        for k in reversed(range(locals_)):
            for j in reversed(range(copies)):
                if j or k:
                    pairs = [
                        (a * locals_ + b, mate(a, j, copies) * locals_ + mate(b, k, locals_))
                        for a in range(copies)
                        for b in range(locals_)
                    ]
                    at = j * locals_ + k
                    moved[at] = lax.ppermute(pieces[at], ("dp", "local"), pairs)
        return moved

    got_x = exchange(pieces[: copies * locals_])
    got_dy = exchange(pieces[copies * locals_ :])
    late = fence(pos)
    (rows_x,) = call(functools.partial(join_body, dims), [shape(everyone, part, BF16)], late, got_x)
    (turned,) = call(
        functools.partial(turn_body, dims),
        [shape(part, everyone, BF16)],
        pos,
        got_dy,
        [pltpu.VMEM((everyone, part), BF16)],
    )
    factor = float(count * copies * nodes) ** (-0.5)
    finished = []
    for i in range(CHUNKS):
        kept, sent = call(
            functools.partial(up_body, dims),
            [shape(everyone, width, F32), shape(everyone, width, BF16)],
            pos,
            [rows_x] + held[i],
            [pltpu.VMEM((part, width), BF16)],
            flops=2 * everyone * part * width,
        )
        if copies == 2:
            others = [lax.ppermute(sent, "dp", [(0, 1), (1, 0)])]
        else:
            kept, others = lax.psum(kept, "dp"), []
        terms = call(
            functools.partial(down_body, dims, factor),
            [shape(mine, width, F32)] + [shape(mine, width, BF16)] * (nodes - 1),
            pos,
            [turned, kept] + others,
            [pltpu.VMEM((everyone, width), BF16)],
            flops=2 * everyone * part * width,
        )
        arrived = []
        for s in order:
            pairs = [(a, (a + s) % nodes) for a in range(nodes)]
            arrived.append(lax.ppermute(terms[s], "node", pairs))
        (summed,) = call(sum_body, [shape(mine, width, BF16)], pos, [terms[0]] + arrived)
        finished.append(summed)
        for j in range(1, copies):
            pairs = [(a, mate(a, j, copies)) for a in range(copies)]
            finished.append(lax.ppermute(summed, "dp", pairs))
    (result,) = call(
        functools.partial(lay_body, dims, CHUNKS), [shape(shard, hidden, BF16)], pos, finished
    )
    return result[None]


def solution(mesh):
    rows = P(("dp", "node", "local"), None)
    weights = P("local", "node", None)
    return jax.shard_map(
        on_device,
        mesh=mesh,
        in_specs=(rows, rows, rows, weights, weights),
        out_specs=weights,
        check_vma=False,
    )
```

```python
import functools
import jax
import jax.numpy as jnp
from jax import lax
from jax.experimental import pallas as pl
from jax.experimental.pallas import tpu as pltpu
from jax.sharding import PartitionSpec as P

QB = 32
CHUNKS = 2
F32 = jnp.float32
BF16 = jnp.bfloat16


def mate(i, k, size):
    return i ^ k if size & (size - 1) == 0 else (i + k) % size


def traced_mate(i, k, size):
    return lax.bitwise_xor(i, jnp.int32(k)) if size & (size - 1) == 0 else lax.rem(i + k, size)


def traced_origin(i, k, size):
    if size & (size - 1) == 0:
        return lax.bitwise_xor(i, jnp.int32(k))
    return lax.rem(i + (size - k), size)


def call(body, outs, scalars, args, scratch=(), flops=0, space=pltpu.VMEM):
    moved = sum(a.size * a.dtype.itemsize for a in args)
    moved += sum(o.size * o.dtype.itemsize for o in outs)
    room = 2 * moved + (8 << 20)
    return pl.pallas_call(
        body,
        out_shape=outs,
        in_specs=[pl.BlockSpec(memory_space=pltpu.SMEM)]
        + [pl.BlockSpec(memory_space=space)] * len(args),
        out_specs=[pl.BlockSpec(memory_space=pltpu.VMEM)] * len(outs),
        scratch_shapes=list(scratch),
        compiler_params=pltpu.CompilerParams(vmem_limit_bytes=min(room, 60 << 20)),
        cost_estimate=pl.CostEstimate(flops=flops, bytes_accessed=moved, transcendentals=0),
    )(scalars, *args)


def partition(values):
    return values[0], values[1], values[2:]


def slots_of(copies, pairs):
    slots = [(j, k) for k in reversed(range(pairs)) for j in reversed(range(copies))]
    return [slot for slot in slots if slot != (0, 0)]


def shape(rows, cols, dtype):
    return jax.ShapeDtypeStruct((rows, cols), dtype)


def dequant_body(pos, codes, scales, *refs):
    outs, (raw, steps, wide, sems) = refs[:-4], refs[-4:]
    mine, ff = raw.shape
    at = pl.multiple_of(pos[0] * mine, 16)
    first = pltpu.make_async_copy(codes.at[pl.ds(at, mine), :], raw, sems.at[0])
    second = pltpu.make_async_copy(scales, steps, sems.at[1])
    first.start()
    second.start()
    second.wait()
    wide[...] = steps[...].astype(F32)
    used = max(1, mine // QB)
    begin = lax.div(pos[0] * mine, jnp.int32(QB))
    if used % 8 == 0:
        begin = pl.multiple_of(begin, 8)
    factors = wide[pl.ds(begin, used), :]
    first.wait()
    blocks = raw[...].astype(F32).reshape(used, mine // used, ff)
    kept = (blocks * factors[:, None, :]).astype(BF16).reshape(mine, ff)
    width = ff // len(outs)
    for i, out in enumerate(outs):
        out[...] = kept[:, i * width : (i + 1) * width]


def select_body(dims, stride, pos, ids, ids_pair, *picks):
    _, _, locals_ = dims
    pairs = locals_ // 2
    count = ids.shape[1]
    high = max(16, pairs)
    first = lax.broadcasted_iota(jnp.int32, (count, count), 0)
    second = lax.broadcasted_iota(jnp.int32, (count, count), 1)
    earlier = (first < second).astype(F32).astype(BF16)
    places = lax.broadcasted_iota(jnp.int32, (pairs * stride, count), 0)
    owner = lax.shift_right_logical(pos[2], 1)
    held = jnp.zeros((high, 1), F32)
    for chosen, pick in zip((ids[...], ids_pair[...]), picks):
        group = lax.shift_right_logical(chosen, 1)
        if pairs & (pairs - 1) == 0:
            relative = lax.bitwise_xor(group, owner)
        else:
            relative = lax.rem(group - owner + pairs, pairs)
        mine = lax.bitwise_and(chosen, 1) == lax.bitwise_and(pos[2], 1)
        relative = jnp.where(mine, relative, high)
        onehot = relative == lax.broadcasted_iota(jnp.int32, (high, count), 0)
        marks = onehot.astype(F32)
        ranks = held + jnp.dot(marks.astype(BF16), earlier, preferred_element_type=F32)
        rank = jnp.sum(jnp.where(onehot, ranks, 0.0), axis=0, keepdims=True)
        slot = jnp.where(mine, relative * stride + rank.astype(jnp.int32), -1)
        pick[...] = (slot == places).astype(F32).astype(BF16)
        held = held + jnp.sum(marks, axis=1, keepdims=True)


def place_rows(dims, stride, blocks, pos, picks, sources, outs):
    copies, _, locals_ = dims
    pairs = locals_ // 2
    rows = outs[0].shape[0]
    width = sources[0].shape[1] // (copies * blocks)
    for j in reversed(range(copies)):
        which = traced_mate(pos[0], j, copies)
        for b in range(blocks):
            at = pl.multiple_of((b * copies + which) * width, 128)
            got = sum(
                jnp.dot(pick[...], source[:, pl.ds(at, width)], preferred_element_type=F32)
                for pick, source in zip(picks, sources)
            ).astype(BF16)
            for k in range(pairs):
                out = outs[j * pairs + k]
                out[:, b * width : (b + 1) * width] = got[k * stride : k * stride + rows]


def first_body(dims, stride, blocks, pos, ids, ids_pair, rows, rows_pair, *outs):
    select_body(dims, stride, pos, ids, ids_pair, *outs[:2])
    place_rows(dims, stride, blocks, pos, outs[:2], (rows, rows_pair), outs[2:])


def later_body(dims, stride, blocks, pos, pick, pick_pair, rows, rows_pair, *outs):
    place_rows(dims, stride, blocks, pos, (pick, pick_pair), (rows, rows_pair), outs)


def join_body(dims, stride, pos, *refs):
    copies, _, locals_ = dims
    pairs = locals_ // 2
    pieces, out = refs[:-1], refs[-1]
    rows, width = pieces[0].shape
    for j in range(copies):
        base = traced_origin(pos[0], j, copies) * (pairs * stride)
        for k in range(pairs):
            at = pl.multiple_of(base + k * stride, 16)
            block = pieces[j * pairs + k][...]
            if rows < stride:
                blank = jnp.zeros((stride - rows, width), block.dtype)
                block = jnp.concatenate([block, blank], axis=0)
            out[pl.ds(at, stride), :] = block


def turn_body(dims, stride, pos, *refs):
    pieces, out, held = refs[:-2], refs[-2], refs[-1]
    join_body(dims, stride, pos, *pieces, held)
    out[...] = jnp.transpose(held[...])


def up_body(dims, pos, rows, *refs):
    _, nodes, _ = dims
    weights, (kept, sent), held = refs[:nodes], refs[nodes : nodes + 2], refs[-1]
    mine = weights[0].shape[0]
    for s in range(nodes):
        at = pl.multiple_of(lax.rem(pos[1] + (nodes - s), nodes) * mine, 16)
        held[pl.ds(at, mine), :] = weights[s][...]
    pre = jnp.dot(rows[...], held[...], preferred_element_type=F32)
    kept[...] = pre
    sent[...] = pre.astype(BF16)


def down_body(dims, factor, pos, turned, kept, *refs):
    _, nodes, _ = dims
    got, outs, act = refs[: -nodes - 1], refs[-nodes - 1 : -1], refs[-1]
    pre = kept[...]
    for part in got:
        pre = pre + part[...].astype(F32)
    act[...] = (pre * jax.nn.sigmoid(pre)).astype(BF16)
    mine = outs[0].shape[0]
    for s in reversed(range(nodes)):
        at = pl.multiple_of(lax.rem(pos[1] + s, nodes) * mine, 16)
        term = jnp.dot(turned[pl.ds(at, mine), :], act[...], preferred_element_type=F32)
        outs[s][...] = (term * factor).astype(outs[s].dtype)


def sum_body(pos, own, *refs):
    total = own[...]
    for part in refs[:-1]:
        total = total + part[...].astype(F32)
    refs[-1][...] = total.astype(BF16)


def lay_body(dims, chunks, pos, *refs):
    copies = dims[0]
    parts, out = refs[:-1], refs[-1]
    mine, width = parts[0].shape
    for j in range(copies):
        at = pl.multiple_of(traced_origin(pos[0], j, copies) * mine, 16)
        for i in range(chunks):
            out[pl.ds(at, mine), i * width : (i + 1) * width] = parts[i * copies + j][...]


def on_device(tokens, cotangent, expert_of, w1_codes, w1_scales):
    copies, nodes, locals_ = (lax.axis_size(a) for a in ("dp", "node", "local"))
    dims = (copies, nodes, locals_)
    count, features = tokens.shape
    capacity = 5 * count // (4 * locals_)
    pairs = locals_ // 2
    sent_rows = -(-2 * capacity // 8) * 8
    stride = -(-sent_rows // 16) * 16
    shard, hidden = w1_codes.shape[1:]
    mine = shard // copies
    part = features // copies
    width = hidden // CHUNKS
    everyone = copies * pairs * stride
    pos = jnp.stack([lax.axis_index(a) for a in ("dp", "node", "local")]).astype(jnp.int32)

    blocks = nodes
    if mine % 128:
        blocks = 1
        tokens, cotangent = (
            a.reshape(count, nodes, copies, mine).swapaxes(1, 2).reshape(count, features)
            for a in (tokens, cotangent)
        )
    chosen = expert_of.reshape(1, count)
    swap = [(i, i ^ 1) for i in range(locals_)]
    chosen_pair = lax.ppermute(chosen, "local", swap)
    tokens_pair = lax.ppermute(tokens, "local", swap)
    cotangent_pair = lax.ppermute(cotangent, "local", swap)

    weights = call(
        dequant_body,
        [shape(mine, width, BF16)] * CHUNKS,
        pos,
        [w1_codes[0], w1_scales[0]],
        [
            pltpu.VMEM((mine, hidden), BF16),
            pltpu.VMEM((shard // QB, hidden), BF16),
            pltpu.VMEM((shard // QB, hidden), F32),
            pltpu.SemaphoreType.DMA((2,)),
        ],
        space=pltpu.HBM,
    )
    order = [s for s in (2, 1, 3) if s < nodes] + list(range(4, nodes))
    held = []
    for chunk in weights:
        got = {0: chunk}
        for s in order:
            got[s] = lax.ppermute(chunk, "node", [(a, (a + s) % nodes) for a in range(nodes)])
        held.append([got[s] for s in range(nodes)])

    flops = 4 * pairs * stride * count * features
    sent = [shape(sent_rows, part, BF16)] * (copies * pairs)
    *picks, pieces_x = partition(
        call(
            functools.partial(first_body, dims, stride, blocks),
            [shape(pairs * stride, count, BF16)] * 2 + sent,
            pos,
            [chosen, chosen_pair, tokens, tokens_pair],
            flops=flops,
        )
    )
    pieces_y = call(
        functools.partial(later_body, dims, stride, blocks),
        sent,
        pos,
        [*picks, cotangent, cotangent_pair],
        flops=flops,
    )

    def exchange(pieces):
        moved = list(pieces)
        for j, k in slots_of(copies, pairs):
            links = [
                (a * locals_ + b, mate(a, j, copies) * locals_ + 2 * mate(b // 2, k, pairs) + b % 2)
                for a in range(copies)
                for b in range(locals_)
            ]
            at = j * pairs + k
            moved[at] = lax.ppermute(pieces[at], ("dp", "local"), links)
        return moved

    got_x = exchange(pieces_x)
    got_dy = exchange(pieces_y)
    (rows_x,) = call(
        functools.partial(join_body, dims, stride), [shape(everyone, part, BF16)], pos, got_x
    )
    (turned,) = call(
        functools.partial(turn_body, dims, stride),
        [shape(part, everyone, BF16)],
        pos,
        got_dy,
        [pltpu.VMEM((everyone, part), BF16)],
    )
    factor = float(count * copies * nodes) ** (-0.5)
    finished = []
    for i in range(CHUNKS):
        kept, sent = call(
            functools.partial(up_body, dims),
            [shape(everyone, width, F32), shape(everyone, width, BF16)],
            pos,
            [rows_x] + held[i],
            [pltpu.VMEM((part, width), BF16)],
            flops=2 * everyone * part * width,
        )
        if copies == 2:
            others = [lax.ppermute(sent, "dp", [(0, 1), (1, 0)])]
        else:
            kept, others = lax.psum(kept, "dp"), []
        terms = call(
            functools.partial(down_body, dims, factor),
            [shape(mine, width, F32)] + [shape(mine, width, BF16)] * (nodes - 1),
            pos,
            [turned, kept] + others,
            [pltpu.VMEM((everyone, width), BF16)],
            flops=2 * everyone * part * width,
        )
        arrived = []
        for s in order:
            pairs = [(a, (a + s) % nodes) for a in range(nodes)]
            arrived.append(lax.ppermute(terms[s], "node", pairs))
        (summed,) = call(sum_body, [shape(mine, width, BF16)], pos, [terms[0]] + arrived)
        finished.append(summed)
        for j in range(1, copies):
            pairs = [(a, mate(a, j, copies)) for a in range(copies)]
            finished.append(lax.ppermute(summed, "dp", pairs))
    (result,) = call(
        functools.partial(lay_body, dims, CHUNKS), [shape(shard, hidden, BF16)], pos, finished
    )
    return result[None]


def solution(mesh):
    rows = P(("dp", "node", "local"), None)
    weights = P("local", "node", None)
    return jax.shard_map(
        on_device,
        mesh=mesh,
        in_specs=(rows, rows, rows, weights, weights),
        out_specs=weights,
        check_vma=False,
    )
```

```python
import functools
import jax
import jax.numpy as jnp
from jax import lax
from jax.experimental import pallas as pl
from jax.experimental.pallas import tpu as pltpu
from jax.sharding import PartitionSpec as P

QB = 32
CHUNKS = 2
F32 = jnp.float32
BF16 = jnp.bfloat16


def mate(i, k, size):
    return i ^ k if size & (size - 1) == 0 else (i + k) % size


def traced_mate(i, k, size):
    return lax.bitwise_xor(i, jnp.int32(k)) if size & (size - 1) == 0 else lax.rem(i + k, size)


def traced_origin(i, k, size):
    if size & (size - 1) == 0:
        return lax.bitwise_xor(i, jnp.int32(k))
    return lax.rem(i + (size - k), size)


def call(body, outs, scalars, args, scratch=(), flops=0, space=pltpu.VMEM, target=pltpu.VMEM):
    moved = sum(a.size * a.dtype.itemsize for a in args)
    moved += sum(o.size * o.dtype.itemsize for o in outs)
    room = 2 * moved + (8 << 20)
    return pl.pallas_call(
        body,
        out_shape=outs,
        in_specs=[pl.BlockSpec(memory_space=pltpu.SMEM)]
        + [pl.BlockSpec(memory_space=space)] * len(args),
        out_specs=[pl.BlockSpec(memory_space=target)] * len(outs),
        scratch_shapes=list(scratch),
        compiler_params=pltpu.CompilerParams(vmem_limit_bytes=min(room, 60 << 20)),
        cost_estimate=pl.CostEstimate(flops=flops, bytes_accessed=moved, transcendentals=0),
    )(scalars, *args)


def partition(values):
    return values[0], values[1], values[2:]


def node_order(nodes):
    return [s for s in (2, 3, 1) if s < nodes] + list(range(4, nodes))


def slots_of(copies, pairs):
    slots = [(j, k) for k in reversed(range(pairs)) for j in reversed(range(copies))]
    return [slot for slot in slots if slot != (0, 0)]


def shape(rows, cols, dtype):
    return jax.ShapeDtypeStruct((rows, cols), dtype)


def dequant_body(pos, codes, scales, *refs):
    outs, (raw, steps, wide, sems) = refs[:-4], refs[-4:]
    mine, ff = raw.shape
    at = pl.multiple_of(pos[0] * mine, 16)
    first = pltpu.make_async_copy(codes.at[pl.ds(at, mine), :], raw, sems.at[0])
    second = pltpu.make_async_copy(scales, steps, sems.at[1])
    first.start()
    second.start()
    second.wait()
    wide[...] = steps[...].astype(F32)
    used = max(1, mine // QB)
    begin = lax.div(pos[0] * mine, jnp.int32(QB))
    if used % 8 == 0:
        begin = pl.multiple_of(begin, 8)
    factors = wide[pl.ds(begin, used), :]
    first.wait()
    blocks = raw[...].astype(F32).reshape(used, mine // used, ff)
    kept = (blocks * factors[:, None, :]).astype(BF16).reshape(mine, ff)
    width = ff // len(outs)
    for i, out in enumerate(outs):
        out[...] = kept[:, i * width : (i + 1) * width]


def select_body(dims, stride, pos, ids, ids_pair, *picks):
    _, _, locals_ = dims
    pairs = locals_ // 2
    count = ids.shape[1]
    high = max(16, pairs)
    first = lax.broadcasted_iota(jnp.int32, (count, count), 0)
    second = lax.broadcasted_iota(jnp.int32, (count, count), 1)
    earlier = (first < second).astype(F32).astype(BF16)
    places = lax.broadcasted_iota(jnp.int32, (pairs * stride, count), 0)
    owner = lax.shift_right_logical(pos[2], 1)
    held = jnp.zeros((high, 1), F32)
    for chosen, pick in zip((ids[...], ids_pair[...]), picks):
        group = lax.shift_right_logical(chosen, 1)
        if pairs & (pairs - 1) == 0:
            relative = lax.bitwise_xor(group, owner)
        else:
            relative = lax.rem(group - owner + pairs, pairs)
        mine = lax.bitwise_and(chosen, 1) == lax.bitwise_and(pos[2], 1)
        relative = jnp.where(mine, relative, high)
        onehot = relative == lax.broadcasted_iota(jnp.int32, (high, count), 0)
        marks = onehot.astype(F32)
        ranks = held + jnp.dot(marks.astype(BF16), earlier, preferred_element_type=F32)
        rank = jnp.sum(jnp.where(onehot, ranks, 0.0), axis=0, keepdims=True)
        slot = jnp.where(mine, relative * stride + rank.astype(jnp.int32), -1)
        pick[...] = (slot == places).astype(F32).astype(BF16)
        held = held + jnp.sum(marks, axis=1, keepdims=True)


def place_rows(dims, stride, blocks, pos, picks, sources, outs):
    copies, _, locals_ = dims
    pairs = locals_ // 2
    rows = outs[0].shape[0]
    width = sources[0].shape[1] // (copies * blocks)
    for j in reversed(range(copies)):
        which = traced_mate(pos[0], j, copies)
        for b in range(blocks):
            at = pl.multiple_of((b * copies + which) * width, 128)
            got = sum(
                jnp.dot(pick[...], source[:, pl.ds(at, width)], preferred_element_type=F32)
                for pick, source in zip(picks, sources)
            ).astype(BF16)
            for k in range(pairs):
                out = outs[j * pairs + k]
                out[:, b * width : (b + 1) * width] = got[k * stride : k * stride + rows]


def first_body(dims, stride, blocks, pos, ids, ids_pair, rows, rows_pair, *outs):
    select_body(dims, stride, pos, ids, ids_pair, *outs[:2])
    place_rows(dims, stride, blocks, pos, outs[:2], (rows, rows_pair), outs[2:])


def later_body(dims, stride, blocks, pos, pick, pick_pair, rows, rows_pair, *outs):
    place_rows(dims, stride, blocks, pos, (pick, pick_pair), (rows, rows_pair), outs)


def join_body(dims, stride, pos, *refs):
    copies, _, locals_ = dims
    pairs = locals_ // 2
    pieces, out = refs[:-1], refs[-1]
    rows, width = pieces[0].shape
    for j in range(copies):
        base = traced_origin(pos[0], j, copies) * (pairs * stride)
        for k in range(pairs):
            at = pl.multiple_of(base + k * stride, 16)
            block = pieces[j * pairs + k][...]
            if rows < stride:
                blank = jnp.zeros((stride - rows, width), block.dtype)
                block = jnp.concatenate([block, blank], axis=0)
            out[pl.ds(at, stride), :] = block


def turn_body(dims, stride, pos, *refs):
    pieces, out, held = refs[:-2], refs[-2], refs[-1]
    join_body(dims, stride, pos, *pieces, held)
    out[...] = jnp.transpose(held[...])


def up_body(dims, pos, rows, *refs):
    _, nodes, _ = dims
    weights, (kept, sent), held = refs[:nodes], refs[nodes : nodes + 2], refs[-1]
    mine = weights[0].shape[0]
    for s in range(nodes):
        at = pl.multiple_of(traced_origin(pos[1], s, nodes) * mine, 16)
        held[pl.ds(at, mine), :] = weights[s][...]
    pre = jnp.dot(rows[...], held[...], preferred_element_type=F32)
    kept[...] = pre
    sent[...] = pre.astype(BF16)


def down_body(dims, factor, pos, turned, kept, *refs):
    _, nodes, _ = dims
    got, outs, act = refs[: -nodes - 1], refs[-nodes - 1 : -1], refs[-1]
    pre = kept[...]
    for part in got:
        pre = pre + part[...].astype(F32)
    act[...] = (pre * jax.nn.sigmoid(pre)).astype(BF16)
    mine = outs[0].shape[0]
    for s in reversed(range(nodes)):
        at = pl.multiple_of(traced_mate(pos[1], s, nodes) * mine, 16)
        term = jnp.dot(turned[pl.ds(at, mine), :], act[...], preferred_element_type=F32)
        outs[s][...] = (term * factor).astype(outs[s].dtype)


def sum_body(pos, own, *refs):
    total = own[...]
    for part in refs[:-1]:
        total = total + part[...].astype(F32)
    refs[-1][...] = total.astype(BF16)


def lay_body(dims, chunks, pos, *refs):
    copies = dims[0]
    parts, out, sems = refs[:-2], refs[-2], refs[-1]
    mine, width = parts[0].shape
    moves = []
    for j in range(copies):
        at = pl.multiple_of(traced_origin(pos[0], j, copies) * mine, 16)
        for i in range(chunks):
            spot = out.at[pl.ds(at, mine), pl.ds(i * width, width)]
            moves.append(pltpu.make_async_copy(parts[i * copies + j], spot, sems.at[i * copies + j]))
    for move in moves:
        move.start()
    for move in moves:
        move.wait()


def on_device(tokens, cotangent, expert_of, w1_codes, w1_scales):
    copies, nodes, locals_ = (lax.axis_size(a) for a in ("dp", "node", "local"))
    dims = (copies, nodes, locals_)
    count, features = tokens.shape
    capacity = 5 * count // (4 * locals_)
    pairs = locals_ // 2
    sent_rows = -(-2 * capacity // 8) * 8
    stride = -(-sent_rows // 16) * 16
    shard, hidden = w1_codes.shape[1:]
    mine = shard // copies
    part = features // copies
    width = hidden // CHUNKS
    everyone = copies * pairs * stride
    pos = jnp.stack([lax.axis_index(a) for a in ("dp", "node", "local")]).astype(jnp.int32)

    blocks = nodes
    if mine % 128:
        blocks = 1
        tokens, cotangent = (
            a.reshape(count, nodes, copies, mine).swapaxes(1, 2).reshape(count, features)
            for a in (tokens, cotangent)
        )
    chosen = expert_of.reshape(1, count)
    swap = [(i, i ^ 1) for i in range(locals_)]
    chosen_pair = lax.ppermute(chosen, "local", swap)
    tokens_pair = lax.ppermute(tokens, "local", swap)
    cotangent_pair = lax.ppermute(cotangent, "local", swap)

    weights = call(
        dequant_body,
        [shape(mine, width, BF16)] * CHUNKS,
        pos,
        [w1_codes[0], w1_scales[0]],
        [
            pltpu.VMEM((mine, hidden), BF16),
            pltpu.VMEM((shard // QB, hidden), BF16),
            pltpu.VMEM((shard // QB, hidden), F32),
            pltpu.SemaphoreType.DMA((2,)),
        ],
        space=pltpu.HBM,
    )
    order = node_order(nodes)
    held = []
    for chunk in weights:
        got = {0: chunk}
        for s in order:
            got[s] = lax.ppermute(chunk, "node", [(a, mate(a, s, nodes)) for a in range(nodes)])
        held.append([got[s] for s in range(nodes)])

    flops = 4 * pairs * stride * count * features
    sent = [shape(sent_rows, part, BF16)] * (copies * pairs)
    *picks, pieces_x = partition(
        call(
            functools.partial(first_body, dims, stride, blocks),
            [shape(pairs * stride, count, BF16)] * 2 + sent,
            pos,
            [chosen, chosen_pair, tokens, tokens_pair],
            flops=flops,
        )
    )
    pieces_y = call(
        functools.partial(later_body, dims, stride, blocks),
        sent,
        pos,
        [*picks, cotangent, cotangent_pair],
        flops=flops,
    )

    def exchange(pieces):
        moved = list(pieces)
        for j, k in slots_of(copies, pairs):
            links = [
                (a * locals_ + b, mate(a, j, copies) * locals_ + 2 * mate(b // 2, k, pairs) + b % 2)
                for a in range(copies)
                for b in range(locals_)
            ]
            at = j * pairs + k
            moved[at] = lax.ppermute(pieces[at], ("dp", "local"), links)
        return moved

    got_x = exchange(pieces_x)
    got_dy = exchange(pieces_y)
    (rows_x,) = call(
        functools.partial(join_body, dims, stride), [shape(everyone, part, BF16)], pos, got_x
    )
    (turned,) = call(
        functools.partial(turn_body, dims, stride),
        [shape(part, everyone, BF16)],
        pos,
        got_dy,
        [pltpu.VMEM((everyone, part), BF16)],
    )
    factor = float(count * copies * nodes) ** (-0.5)
    finished = []
    for i in range(CHUNKS):
        kept, sent = call(
            functools.partial(up_body, dims),
            [shape(everyone, width, F32), shape(everyone, width, BF16)],
            pos,
            [rows_x] + held[i],
            [pltpu.VMEM((part, width), BF16)],
            flops=2 * everyone * part * width,
        )
        if copies == 2:
            others = [lax.ppermute(sent, "dp", [(0, 1), (1, 0)])]
        else:
            kept, others = lax.psum(kept, "dp"), []
        terms = call(
            functools.partial(down_body, dims, factor),
            [shape(mine, width, F32)] + [shape(mine, width, BF16)] * (nodes - 1),
            pos,
            [turned, kept] + others,
            [pltpu.VMEM((everyone, width), BF16)],
            flops=2 * everyone * part * width,
        )
        arrived = []
        for s in order:
            links = [(a, mate(a, s, nodes)) for a in range(nodes)]
            arrived.append(lax.ppermute(terms[s], "node", links))
        (summed,) = call(sum_body, [shape(mine, width, BF16)], pos, [terms[0]] + arrived)
        finished.append(summed)
        for j in range(1, copies):
            links = [(a, mate(a, j, copies)) for a in range(copies)]
            finished.append(lax.ppermute(summed, "dp", links))
    (result,) = call(
        functools.partial(lay_body, dims, CHUNKS),
        [shape(shard, hidden, BF16)],
        pos,
        finished,
        [pltpu.SemaphoreType.DMA((CHUNKS * copies,))],
        target=pltpu.HBM,
    )
    return result[None]


def solution(mesh):
    rows = P(("dp", "node", "local"), None)
    weights = P("local", "node", None)
    return jax.shard_map(
        on_device,
        mesh=mesh,
        in_specs=(rows, rows, rows, weights, weights),
        out_specs=weights,
        check_vma=False,
    )
```

```python
import functools
import jax
import jax.numpy as jnp
from jax import lax
from jax.experimental import pallas as pl
from jax.experimental.pallas import tpu as pltpu
from jax.sharding import PartitionSpec as P

QB = 32
SPLITS = ((1, 1), (2,))
F32 = jnp.float32
BF16 = jnp.bfloat16


def mate(i, k, size):
    return i ^ k if size & (size - 1) == 0 else (i + k) % size


def traced_mate(i, k, size):
    return lax.bitwise_xor(i, jnp.int32(k)) if size & (size - 1) == 0 else lax.rem(i + k, size)


def traced_origin(i, k, size):
    if size & (size - 1) == 0:
        return lax.bitwise_xor(i, jnp.int32(k))
    return lax.rem(i + (size - k), size)


def call(body, outs, scalars, args, scratch=(), flops=0, space=pltpu.VMEM, target=pltpu.VMEM):
    moved = sum(a.size * a.dtype.itemsize for a in args)
    moved += sum(o.size * o.dtype.itemsize for o in outs)
    spaces = space if isinstance(space, list) else [space] * len(args)
    room = 2 * moved + (8 << 20)
    return pl.pallas_call(
        body,
        out_shape=outs,
        in_specs=[pl.BlockSpec(memory_space=pltpu.SMEM)]
        + [pl.BlockSpec(memory_space=kind) for kind in spaces],
        out_specs=[pl.BlockSpec(memory_space=target)] * len(outs),
        scratch_shapes=list(scratch),
        compiler_params=pltpu.CompilerParams(vmem_limit_bytes=min(room, 60 << 20)),
        cost_estimate=pl.CostEstimate(flops=flops, bytes_accessed=moved, transcendentals=0),
    )(scalars, *args)


def node_order(nodes):
    return [s for s in (2, 3, 1) if s < nodes] + list(range(4, nodes))


def slots_of(copies, pairs):
    slots = [(j, k) for k in reversed(range(pairs)) for j in reversed(range(copies))]
    return [slot for slot in slots if slot != (0, 0)]


def shape(rows, cols, dtype):
    return jax.ShapeDtypeStruct((rows, cols), dtype)


def dequant_body(pos, codes, scales, *refs):
    outs, (raw, steps, wide, sems) = refs[:-4], refs[-4:]
    mine, ff = raw.shape
    at = pl.multiple_of(pos[0] * mine, 16)
    first = pltpu.make_async_copy(codes.at[pl.ds(at, mine), :], raw, sems.at[0])
    second = pltpu.make_async_copy(scales, steps, sems.at[1])
    first.start()
    second.start()
    second.wait()
    wide[...] = steps[...].astype(F32)
    used = max(1, mine // QB)
    begin = lax.div(pos[0] * mine, jnp.int32(QB))
    if used % 8 == 0:
        begin = pl.multiple_of(begin, 8)
    factors = wide[pl.ds(begin, used), :]
    first.wait()
    blocks = raw[...].astype(F32).reshape(used, mine // used, ff)
    kept = (blocks * factors[:, None, :]).astype(BF16).reshape(mine, ff)
    width = ff // len(outs)
    for i, out in enumerate(outs):
        out[...] = kept[:, i * width : (i + 1) * width]


def select_body(dims, stride, pos, ids, ids_pair, *picks):
    _, _, locals_ = dims
    pairs = locals_ // 2
    count = ids.shape[1]
    high = max(16, pairs)
    first = lax.broadcasted_iota(jnp.int32, (count, count), 0)
    second = lax.broadcasted_iota(jnp.int32, (count, count), 1)
    earlier = (first < second).astype(F32).astype(BF16)
    places = lax.broadcasted_iota(jnp.int32, (pairs * stride, count), 0)
    owner = lax.shift_right_logical(pos[2], 1)
    held = jnp.zeros((high, 1), F32)
    for chosen, pick in zip((ids[...], ids_pair[...]), picks):
        group = lax.shift_right_logical(chosen, 1)
        if pairs & (pairs - 1) == 0:
            relative = lax.bitwise_xor(group, owner)
        else:
            relative = lax.rem(group - owner + pairs, pairs)
        mine = lax.bitwise_and(chosen, 1) == lax.bitwise_and(pos[2], 1)
        relative = jnp.where(mine, relative, high)
        onehot = relative == lax.broadcasted_iota(jnp.int32, (high, count), 0)
        marks = onehot.astype(F32)
        ranks = held + jnp.dot(marks.astype(BF16), earlier, preferred_element_type=F32)
        rank = jnp.sum(jnp.where(onehot, ranks, 0.0), axis=0, keepdims=True)
        slot = jnp.where(mine, relative * stride + rank.astype(jnp.int32), -1)
        pick[...] = (slot == places).astype(F32).astype(BF16)
        held = held + jnp.sum(marks, axis=1, keepdims=True)


def place_rows(dims, stride, blocks, pos, picks, sources, outs):
    copies, _, locals_ = dims
    pairs = locals_ // 2
    rows = outs[0].shape[0]
    width = sources[0].shape[1] // (copies * blocks)
    for j in reversed(range(copies)):
        which = traced_mate(pos[0], j, copies)
        for b in range(blocks):
            at = pl.multiple_of((b * copies + which) * width, 128)
            got = sum(
                jnp.dot(pick[...], source[:, pl.ds(at, width)], preferred_element_type=F32)
                for pick, source in zip(picks, sources)
            ).astype(BF16)
            for k in range(pairs):
                out = outs[j * pairs + k]
                out[:, b * width : (b + 1) * width] = got[k * stride : k * stride + rows]


def choose_body(dims, stride, pos, ids, ids_pair, rows, *refs):
    picks, near, sem = refs[:2], refs[2], refs[3]
    move = pltpu.make_async_copy(rows, near, sem)
    move.start()
    select_body(dims, stride, pos, ids, ids_pair, *picks)
    move.wait()


def route_body(dims, stride, blocks, pos, pick, pick_pair, rows, rows_pair, *outs):
    place_rows(dims, stride, blocks, pos, (pick, pick_pair), (rows, rows_pair), outs)


def join_body(dims, stride, pos, *refs):
    copies, _, locals_ = dims
    pairs = locals_ // 2
    pieces, out = refs[:-1], refs[-1]
    rows, width = pieces[0].shape
    for j in range(copies):
        base = traced_origin(pos[0], j, copies) * (pairs * stride)
        for k in range(pairs):
            at = pl.multiple_of(base + k * stride, 16)
            block = pieces[j * pairs + k][...]
            if rows < stride:
                blank = jnp.zeros((stride - rows, width), block.dtype)
                block = jnp.concatenate([block, blank], axis=0)
            out[pl.ds(at, stride), :] = block


def turn_body(dims, stride, pos, *refs):
    pieces, out, held = refs[:-2], refs[-2], refs[-1]
    join_body(dims, stride, pos, *pieces, held)
    out[...] = jnp.transpose(held[...])


def up_body(dims, pos, rows, *refs):
    _, nodes, _ = dims
    weights, outs, held = refs[:nodes], refs[nodes:-1], refs[-1]
    mine = weights[0].shape[0]
    for s in range(nodes):
        at = pl.multiple_of(traced_origin(pos[1], s, nodes) * mine, 16)
        held[pl.ds(at, mine), :] = weights[s][...]
    begin = 0
    for kept, sent in zip(outs[::2], outs[1::2]):
        end = begin + kept.shape[1]
        pre = jnp.dot(rows[...], held[:, begin:end], preferred_element_type=F32)
        kept[...] = pre
        sent[...] = pre.astype(BF16)
        begin = end


def down_body(dims, factor, pos, turned, kept, *refs):
    _, nodes, _ = dims
    got, outs, act = refs[: -nodes - 1], refs[-nodes - 1 : -1], refs[-1]
    pre = kept[...]
    for part in got:
        pre = pre + part[...].astype(F32)
    act[...] = (pre * jax.nn.sigmoid(pre)).astype(BF16)
    mine = outs[0].shape[0]
    for s in reversed(range(nodes)):
        at = pl.multiple_of(traced_mate(pos[1], s, nodes) * mine, 16)
        term = jnp.dot(turned[pl.ds(at, mine), :], act[...], preferred_element_type=F32)
        outs[s][...] = (term * factor).astype(outs[s].dtype)


def sum_body(pos, own, *refs):
    total = own[...]
    for part in refs[:-1]:
        total = total + part[...].astype(F32)
    refs[-1][...] = total.astype(BF16)


def lay_body(dims, pos, *refs):
    copies = dims[0]
    parts, out, sems = refs[:-2], refs[-2], refs[-1]
    moves = []
    begin = 0
    for i in range(len(parts) // copies):
        mine, width = parts[i * copies].shape
        for j in range(copies):
            at = pl.multiple_of(traced_origin(pos[0], j, copies) * mine, 16)
            spot = out.at[pl.ds(at, mine), pl.ds(begin, width)]
            moves.append(pltpu.make_async_copy(parts[i * copies + j], spot, sems.at[i * copies + j]))
        begin += width
    for move in moves:
        move.start()
    for move in moves:
        move.wait()


def on_device(tokens, cotangent, expert_of, w1_codes, w1_scales):
    copies, nodes, locals_ = (lax.axis_size(a) for a in ("dp", "node", "local"))
    dims = (copies, nodes, locals_)
    count, features = tokens.shape
    capacity = 5 * count // (4 * locals_)
    pairs = locals_ // 2
    sent_rows = -(-2 * capacity // 8) * 8
    stride = -(-sent_rows // 16) * 16
    shard, hidden = w1_codes.shape[1:]
    mine = shard // copies
    part = features // copies
    width = hidden // len(SPLITS)
    everyone = copies * pairs * stride
    pos = jnp.stack([lax.axis_index(a) for a in ("dp", "node", "local")]).astype(jnp.int32)

    blocks = nodes
    if mine % 128:
        blocks = 1
        tokens, cotangent = (
            a.reshape(count, nodes, copies, mine).swapaxes(1, 2).reshape(count, features)
            for a in (tokens, cotangent)
        )
    chosen = expert_of.reshape(1, count)
    swap = [(i, i ^ 1) for i in range(locals_)]
    tokens_pair = lax.ppermute(tokens, "local", swap)
    chosen_pair = lax.ppermute(chosen, "local", swap)
    cotangent_pair = lax.ppermute(cotangent, "local", swap)

    weights = call(
        dequant_body,
        [shape(mine, width, BF16)] * len(SPLITS),
        pos,
        [pltpu.with_memory_space_constraint(a[0], pltpu.HBM) for a in (w1_codes, w1_scales)],
        [
            pltpu.VMEM((mine, hidden), BF16),
            pltpu.VMEM((shard // QB, hidden), BF16),
            pltpu.VMEM((shard // QB, hidden), F32),
            pltpu.SemaphoreType.DMA((2,)),
        ],
        space=pltpu.HBM,
    )
    order = node_order(nodes)
    held = []
    for chunk in weights:
        got = {0: chunk}
        for s in order:
            got[s] = lax.ppermute(chunk, "node", [(a, mate(a, s, nodes)) for a in range(nodes)])
        held.append([got[s] for s in range(nodes)])

    *picks, tokens = call(
        functools.partial(choose_body, dims, stride),
        [shape(pairs * stride, count, BF16)] * 2 + [shape(count, features, BF16)],
        pos,
        [chosen, chosen_pair, pltpu.with_memory_space_constraint(tokens, pltpu.HBM)],
        [pltpu.SemaphoreType.DMA],
        space=[pltpu.VMEM, pltpu.VMEM, pltpu.HBM],
    )

    def route(rows, rows_pair):
        return call(
            functools.partial(route_body, dims, stride, blocks),
            [shape(sent_rows, part, BF16)] * (copies * pairs),
            pos,
            [*picks, rows, rows_pair],
            flops=4 * pairs * stride * count * features,
        )

    pieces_x = route(tokens, tokens_pair)
    pieces_y = route(cotangent, cotangent_pair)

    def exchange(pieces):
        moved = list(pieces)
        for j, k in slots_of(copies, pairs):
            links = [
                (a * locals_ + b, mate(a, j, copies) * locals_ + 2 * mate(b // 2, k, pairs) + b % 2)
                for a in range(copies)
                for b in range(locals_)
            ]
            at = j * pairs + k
            moved[at] = lax.ppermute(pieces[at], ("dp", "local"), links)
        return moved

    got_x = exchange(pieces_x)
    got_dy = exchange(pieces_y)
    (rows_x,) = call(
        functools.partial(join_body, dims, stride), [shape(everyone, part, BF16)], pos, got_x
    )
    (turned,) = call(
        functools.partial(turn_body, dims, stride),
        [shape(part, everyone, BF16)],
        pos,
        got_dy,
        [pltpu.VMEM((everyone, part), BF16)],
    )
    factor = float(count * copies * nodes) ** (-0.5)
    groups = []
    for i, split in enumerate(SPLITS):
        widths = [width * share // sum(split) for share in split]
        parts = call(
            functools.partial(up_body, dims),
            [shape(everyone, w, kind) for w in widths for kind in (F32, BF16)],
            pos,
            [rows_x] + held[i],
            [pltpu.VMEM((part, width), BF16)],
            flops=2 * everyone * part * width,
        )
        groups += list(zip(widths, parts[::2], parts[1::2]))
    finished = []
    for wide, kept, sent in groups:
        if copies == 2:
            others = [lax.ppermute(sent, "dp", [(0, 1), (1, 0)])]
        else:
            kept, others = lax.psum(kept, "dp"), []
        terms = call(
            functools.partial(down_body, dims, factor),
            [shape(mine, wide, F32)] + [shape(mine, wide, BF16)] * (nodes - 1),
            pos,
            [turned, kept] + others,
            [pltpu.VMEM((everyone, wide), BF16)],
            flops=2 * everyone * part * wide,
        )
        arrived = []
        for s in order:
            links = [(a, mate(a, s, nodes)) for a in range(nodes)]
            arrived.append(lax.ppermute(terms[s], "node", links))
        (summed,) = call(sum_body, [shape(mine, wide, BF16)], pos, [terms[0]] + arrived)
        finished.append(summed)
        for j in range(1, copies):
            links = [(a, mate(a, j, copies)) for a in range(copies)]
            finished.append(lax.ppermute(summed, "dp", links))
    (result,) = call(
        functools.partial(lay_body, dims),
        [shape(shard, hidden, BF16)],
        pos,
        finished,
        [pltpu.SemaphoreType.DMA((len(finished),))],
        target=pltpu.HBM,
    )
    return result[None]


def solution(mesh):
    rows = P(("dp", "node", "local"), None)
    weights = P("local", "node", None)
    return jax.shard_map(
        on_device,
        mesh=mesh,
        in_specs=(rows, rows, rows, weights, weights),
        out_specs=weights,
        check_vma=False,
    )
```

```python
import functools
import jax
import jax.numpy as jnp
from jax import lax
from jax.experimental import pallas as pl
from jax.experimental.pallas import tpu as pltpu
from jax.sharding import PartitionSpec as P

QB = 32
SPLITS = ((1, 2), (1,))
F32 = jnp.float32
BF16 = jnp.bfloat16


def mate(i, k, size):
    return i ^ k if size & (size - 1) == 0 else (i + k) % size


def traced_mate(i, k, size):
    return lax.bitwise_xor(i, jnp.int32(k)) if size & (size - 1) == 0 else lax.rem(i + k, size)


def traced_origin(i, k, size):
    if size & (size - 1) == 0:
        return lax.bitwise_xor(i, jnp.int32(k))
    return lax.rem(i + (size - k), size)


def call(body, outs, scalars, args, scratch=(), flops=0, space=pltpu.VMEM, target=pltpu.VMEM, aliases=None):
    moved = sum(a.size * a.dtype.itemsize for a in args)
    moved += sum(o.size * o.dtype.itemsize for o in outs)
    spaces = space if isinstance(space, list) else [space] * len(args)
    room = 2 * moved + (8 << 20)
    return pl.pallas_call(
        body,
        out_shape=outs,
        in_specs=[pl.BlockSpec(memory_space=pltpu.SMEM)]
        + [pl.BlockSpec(memory_space=kind) for kind in spaces],
        out_specs=[pl.BlockSpec(memory_space=target)] * len(outs),
        scratch_shapes=list(scratch),
        input_output_aliases=aliases or {},
        compiler_params=pltpu.CompilerParams(vmem_limit_bytes=min(room, 60 << 20)),
        cost_estimate=pl.CostEstimate(flops=flops, bytes_accessed=moved, transcendentals=0),
    )(scalars, *args)


def node_order(nodes):
    return [s for s in (3, 1, 2) if s < nodes] + list(range(4, nodes))


def slots_of(copies, pairs):
    slots = [(j, k) for k in reversed(range(pairs)) for j in reversed(range(copies))]
    return [slot for slot in slots if slot != (0, 0)]


def shape(rows, cols, dtype):
    return jax.ShapeDtypeStruct((rows, cols), dtype)


def dequant_body(pos, codes, scales, *refs):
    outs, (raw, steps, wide, sems) = refs[:-4], refs[-4:]
    mine, ff = raw.shape
    at = pl.multiple_of(pos[0] * mine, 16)
    first = pltpu.make_async_copy(codes.at[pl.ds(at, mine), :], raw, sems.at[0])
    second = pltpu.make_async_copy(scales, steps, sems.at[1])
    first.start()
    second.start()
    second.wait()
    wide[...] = steps[...].astype(F32)
    used = max(1, mine // QB)
    begin = lax.div(pos[0] * mine, jnp.int32(QB))
    if used % 8 == 0:
        begin = pl.multiple_of(begin, 8)
    factors = wide[pl.ds(begin, used), :]
    first.wait()
    blocks = raw[...].astype(F32).reshape(used, mine // used, ff)
    kept = (blocks * factors[:, None, :]).astype(BF16).reshape(mine, ff)
    begin = 0
    for out in outs:
        end = begin + out.shape[1]
        out[...] = kept[:, begin:end]
        begin = end


def select_body(dims, stride, pos, ids, ids_pair, *picks):
    _, _, locals_ = dims
    pairs = locals_ // 2
    count = ids.shape[1]
    high = max(16, pairs)
    first = lax.broadcasted_iota(jnp.int32, (count, count), 0)
    second = lax.broadcasted_iota(jnp.int32, (count, count), 1)
    earlier = (first < second).astype(F32).astype(BF16)
    places = lax.broadcasted_iota(jnp.int32, (pairs * stride, count), 0)
    owner = lax.shift_right_logical(pos[2], 1)
    held = jnp.zeros((high, 1), F32)
    for chosen, pick in zip((ids[...], ids_pair[...]), picks):
        group = lax.shift_right_logical(chosen, 1)
        if pairs & (pairs - 1) == 0:
            relative = lax.bitwise_xor(group, owner)
        else:
            relative = lax.rem(group - owner + pairs, pairs)
        mine = lax.bitwise_and(chosen, 1) == lax.bitwise_and(pos[2], 1)
        relative = jnp.where(mine, relative, high)
        onehot = relative == lax.broadcasted_iota(jnp.int32, (high, count), 0)
        marks = onehot.astype(F32)
        ranks = held + jnp.dot(marks.astype(BF16), earlier, preferred_element_type=F32)
        rank = jnp.sum(jnp.where(onehot, ranks, 0.0), axis=0, keepdims=True)
        slot = jnp.where(mine, relative * stride + rank.astype(jnp.int32), -1)
        pick[...] = (slot == places).astype(F32).astype(BF16)
        held = held + jnp.sum(marks, axis=1, keepdims=True)


def place_rows(dims, stride, blocks, pos, picks, sources, outs):
    copies, _, locals_ = dims
    pairs = locals_ // 2
    rows = outs[0].shape[0]
    width = sources[0].shape[1] // (copies * blocks)
    for j in reversed(range(copies)):
        which = traced_mate(pos[0], j, copies)
        for b in range(blocks):
            at = pl.multiple_of((b * copies + which) * width, 128)
            got = sum(
                jnp.dot(pick[...], source[:, pl.ds(at, width)], preferred_element_type=F32)
                for pick, source in zip(picks, sources)
            ).astype(BF16)
            for k in range(pairs):
                out = outs[j * pairs + k]
                out[:, b * width : (b + 1) * width] = got[k * stride : k * stride + rows]


def choose_body(dims, stride, pos, ids, ids_pair, rows, *refs):
    picks, near, sem = refs[:2], refs[2], refs[3]
    move = pltpu.make_async_copy(rows, near, sem)
    move.start()
    select_body(dims, stride, pos, ids, ids_pair, *picks)
    move.wait()


def route_body(dims, stride, blocks, pos, pick, pick_pair, rows, rows_pair, *outs):
    place_rows(dims, stride, blocks, pos, (pick, pick_pair), (rows, rows_pair), outs)


def join_body(dims, stride, pos, *refs):
    copies, _, locals_ = dims
    pairs = locals_ // 2
    pieces, out = refs[:-1], refs[-1]
    rows, width = pieces[0].shape
    for j in range(copies):
        base = traced_origin(pos[0], j, copies) * (pairs * stride)
        for k in range(pairs):
            at = pl.multiple_of(base + k * stride, 16)
            block = pieces[j * pairs + k][...]
            if rows < stride:
                blank = jnp.zeros((stride - rows, width), block.dtype)
                block = jnp.concatenate([block, blank], axis=0)
            out[pl.ds(at, stride), :] = block


def turn_body(dims, stride, pos, *refs):
    pieces, out, held = refs[:-2], refs[-2], refs[-1]
    join_body(dims, stride, pos, *pieces, held)
    out[...] = jnp.transpose(held[...])


def up_body(dims, pos, rows, *refs):
    _, nodes, _ = dims
    weights, outs, held = refs[:nodes], refs[nodes:-1], refs[-1]
    mine = weights[0].shape[0]
    for s in range(nodes):
        at = pl.multiple_of(traced_origin(pos[1], s, nodes) * mine, 16)
        held[pl.ds(at, mine), :] = weights[s][...]
    begin = 0
    for kept, sent in zip(outs[::2], outs[1::2]):
        end = begin + kept.shape[1]
        pre = jnp.dot(rows[...], held[:, begin:end], preferred_element_type=F32)
        kept[...] = pre
        sent[...] = pre.astype(BF16)
        begin = end


def down_body(dims, factor, pos, turned, kept, *refs):
    _, nodes, _ = dims
    got, outs, act = refs[: -nodes - 1], refs[-nodes - 1 : -1], refs[-1]
    pre = kept[...]
    for part in got:
        pre = pre + part[...].astype(F32)
    act[...] = (pre * jax.nn.sigmoid(pre)).astype(BF16)
    mine = outs[0].shape[0]
    for s in reversed(range(nodes)):
        at = pl.multiple_of(traced_mate(pos[1], s, nodes) * mine, 16)
        term = jnp.dot(turned[pl.ds(at, mine), :], act[...], preferred_element_type=F32)
        outs[s][...] = (term * factor).astype(outs[s].dtype)


def sum_body(pos, own, *refs):
    total = own[...]
    for part in refs[:-1]:
        total = total + part[...].astype(F32)
    refs[-1][...] = total.astype(BF16)


def lay_body(dims, spots, pos, *refs):
    copies = dims[0]
    parts, out, sems = refs[: len(spots)], refs[-2], refs[-1]
    moves = []
    for i, (part, (j, begin)) in enumerate(zip(parts, spots)):
        mine, width = part.shape
        at = pl.multiple_of(traced_origin(pos[0], j, copies) * mine, 16)
        spot = out.at[pl.ds(at, mine), pl.ds(begin, width)]
        moves.append(pltpu.make_async_copy(part, spot, sems.at[i]))
    for move in moves:
        move.start()
    for move in moves:
        move.wait()


def on_device(tokens, cotangent, expert_of, w1_codes, w1_scales):
    copies, nodes, locals_ = (lax.axis_size(a) for a in ("dp", "node", "local"))
    dims = (copies, nodes, locals_)
    count, features = tokens.shape
    capacity = 5 * count // (4 * locals_)
    pairs = locals_ // 2
    sent_rows = -(-2 * capacity // 8) * 8
    stride = -(-sent_rows // 16) * 16
    shard, hidden = w1_codes.shape[1:]
    mine = shard // copies
    part = features // copies
    unit = hidden // sum(sum(split) for split in SPLITS)
    gathered = [unit * sum(split) for split in SPLITS]
    everyone = copies * pairs * stride
    pos = jnp.stack([lax.axis_index(a) for a in ("dp", "node", "local")]).astype(jnp.int32)

    blocks = nodes
    if mine % 128:
        blocks = 1
        tokens, cotangent = (
            a.reshape(count, nodes, copies, mine).swapaxes(1, 2).reshape(count, features)
            for a in (tokens, cotangent)
        )
    chosen = expert_of.reshape(1, count)
    swap = [(i, i ^ 1) for i in range(locals_)]
    tokens_pair = lax.ppermute(tokens, "local", swap)
    chosen_pair = lax.ppermute(chosen, "local", swap)
    cotangent_pair = lax.ppermute(cotangent, "local", swap)

    weights = call(
        dequant_body,
        [shape(mine, w, BF16) for w in gathered],
        pos,
        [pltpu.with_memory_space_constraint(a[0], pltpu.HBM) for a in (w1_codes, w1_scales)],
        [
            pltpu.VMEM((mine, hidden), BF16),
            pltpu.VMEM((shard // QB, hidden), BF16),
            pltpu.VMEM((shard // QB, hidden), F32),
            pltpu.SemaphoreType.DMA((2,)),
        ],
        space=pltpu.HBM,
    )
    order = node_order(nodes)
    held = []
    for chunk in weights:
        got = {0: chunk}
        for s in order:
            got[s] = lax.ppermute(chunk, "node", [(a, mate(a, s, nodes)) for a in range(nodes)])
        held.append([got[s] for s in range(nodes)])

    *picks, tokens = call(
        functools.partial(choose_body, dims, stride),
        [shape(pairs * stride, count, BF16)] * 2 + [shape(count, features, BF16)],
        pos,
        [chosen, chosen_pair, pltpu.with_memory_space_constraint(tokens, pltpu.HBM)],
        [pltpu.SemaphoreType.DMA],
        space=[pltpu.VMEM, pltpu.VMEM, pltpu.HBM],
    )

    def route(rows, rows_pair):
        return call(
            functools.partial(route_body, dims, stride, blocks),
            [shape(sent_rows, part, BF16)] * (copies * pairs),
            pos,
            [*picks, rows, rows_pair],
            flops=4 * pairs * stride * count * features,
        )

    pieces_x = route(tokens, tokens_pair)
    pieces_y = route(cotangent, cotangent_pair)

    def exchange(pieces):
        moved = list(pieces)
        for j, k in slots_of(copies, pairs):
            links = [
                (a * locals_ + b, mate(a, j, copies) * locals_ + 2 * mate(b // 2, k, pairs) + b % 2)
                for a in range(copies)
                for b in range(locals_)
            ]
            at = j * pairs + k
            moved[at] = lax.ppermute(pieces[at], ("dp", "local"), links)
        return moved

    got_x = exchange(pieces_x)
    got_dy = exchange(pieces_y)
    (rows_x,) = call(
        functools.partial(join_body, dims, stride), [shape(everyone, part, BF16)], pos, got_x
    )
    (turned,) = call(
        functools.partial(turn_body, dims, stride),
        [shape(part, everyone, BF16)],
        pos,
        got_dy,
        [pltpu.VMEM((everyone, part), BF16)],
    )
    factor = float(count * copies * nodes) ** (-0.5)
    groups = []
    for i, split in enumerate(SPLITS):
        widths = [unit * share for share in split]
        parts = call(
            functools.partial(up_body, dims),
            [shape(everyone, w, kind) for w in widths for kind in (F32, BF16)],
            pos,
            [rows_x] + held[i],
            [pltpu.VMEM((part, gathered[i]), BF16)],
            flops=2 * everyone * part * gathered[i],
        )
        groups += list(zip(widths, parts[::2], parts[1::2]))
    finished = []
    for wide, kept, sent in groups:
        if copies == 2:
            others = [lax.ppermute(sent, "dp", [(0, 1), (1, 0)])]
        else:
            kept, others = lax.psum(kept, "dp"), []
        terms = call(
            functools.partial(down_body, dims, factor),
            [shape(mine, wide, F32)] + [shape(mine, wide, BF16)] * (nodes - 1),
            pos,
            [turned, kept] + others,
            [pltpu.VMEM((everyone, wide), BF16)],
            flops=2 * everyone * part * wide,
        )
        arrived = []
        for s in order:
            links = [(a, mate(a, s, nodes)) for a in range(nodes)]
            arrived.append(lax.ppermute(terms[s], "node", links))
        (summed,) = call(sum_body, [shape(mine, wide, BF16)], pos, [terms[0]] + arrived)
        finished.append(summed)
        for j in range(1, copies):
            links = [(a, mate(a, j, copies)) for a in range(copies)]
            finished.append(lax.ppermute(summed, "dp", links))
    spots = []
    begin = 0
    for wide, _, _ in groups:
        spots += [(j, begin) for j in range(copies)]
        begin += wide
    early = len(finished) - copies + 1
    last = copies - 1
    (result,) = call(
        functools.partial(lay_body, dims, spots[:early]),
        [shape(shard, hidden, BF16)],
        pos,
        finished[:early],
        [pltpu.SemaphoreType.DMA((early,))],
        target=pltpu.HBM,
    )
    (result,) = call(
        functools.partial(lay_body, dims, spots[early:]),
        [shape(shard, hidden, BF16)],
        pos,
        finished[early:] + [result],
        [pltpu.SemaphoreType.DMA((last,))],
        space=[pltpu.VMEM] * last + [pltpu.HBM],
        target=pltpu.HBM,
        aliases={last + 1: 0},
    )
    return result[None]


def solution(mesh):
    rows = P(("dp", "node", "local"), None)
    weights = P("local", "node", None)
    return jax.shard_map(
        on_device,
        mesh=mesh,
        in_specs=(rows, rows, rows, weights, weights),
        out_specs=weights,
        check_vma=False,
    )
```

```python
import functools
import jax
import jax.numpy as jnp
from jax import lax
from jax.experimental import pallas as pl
from jax.experimental.pallas import tpu as pltpu
from jax.sharding import PartitionSpec as P

QB = 32
SPLITS = ((1, 1), (1, 1))
F32 = jnp.float32
BF16 = jnp.bfloat16


def mate(i, k, size):
    return i ^ k if size & (size - 1) == 0 else (i + k) % size


def traced_mate(i, k, size):
    return lax.bitwise_xor(i, jnp.int32(k)) if size & (size - 1) == 0 else lax.rem(i + k, size)


def traced_origin(i, k, size):
    if size & (size - 1) == 0:
        return lax.bitwise_xor(i, jnp.int32(k))
    return lax.rem(i + (size - k), size)


def call(body, outs, scalars, args, scratch=(), flops=0, space=pltpu.VMEM, target=pltpu.VMEM, aliases=None):
    moved = sum(a.size * a.dtype.itemsize for a in args)
    moved += sum(o.size * o.dtype.itemsize for o in outs)
    spaces = space if isinstance(space, list) else [space] * len(args)
    room = 2 * moved + (8 << 20)
    return pl.pallas_call(
        body,
        out_shape=outs,
        in_specs=[pl.BlockSpec(memory_space=pltpu.SMEM)]
        + [pl.BlockSpec(memory_space=kind) for kind in spaces],
        out_specs=[pl.BlockSpec(memory_space=target)] * len(outs),
        scratch_shapes=list(scratch),
        input_output_aliases=aliases or {},
        compiler_params=pltpu.CompilerParams(vmem_limit_bytes=min(room, 60 << 20)),
        cost_estimate=pl.CostEstimate(flops=flops, bytes_accessed=moved, transcendentals=0),
    )(scalars, *args)


def node_order(nodes):
    return [s for s in (3, 1, 2) if s < nodes] + list(range(4, nodes))


def plan_of(nodes, aligned):
    order = node_order(nodes)
    every = order + [0]
    chunks = sum(len(split) for split in SPLITS)
    if not aligned:
        return [every], [([i], every) for i in range(chunks)], [[i] for i in range(chunks)]
    early, late = order[: nodes // 2], order[nodes // 2 :] + [0]
    jobs = [([0], early), ([1], early), ([0, 1], late)]
    jobs += [([i], every) for i in range(2, chunks)]
    return [early, late], jobs, [[0, 1]] + [[i] for i in range(2, chunks)]


def slots_of(copies, pairs):
    slots = [(j, k) for k in reversed(range(pairs)) for j in reversed(range(copies))]
    return [slot for slot in slots if slot != (0, 0)]


def shape(rows, cols, dtype):
    return jax.ShapeDtypeStruct((rows, cols), dtype)


def dequant_body(pos, codes, scales, *refs):
    outs, (raw, steps, wide, sems) = refs[:-4], refs[-4:]
    mine, ff = raw.shape
    at = pl.multiple_of(pos[0] * mine, 16)
    first = pltpu.make_async_copy(codes.at[pl.ds(at, mine), :], raw, sems.at[0])
    second = pltpu.make_async_copy(scales, steps, sems.at[1])
    first.start()
    second.start()
    second.wait()
    wide[...] = steps[...].astype(F32)
    used = max(1, mine // QB)
    begin = lax.div(pos[0] * mine, jnp.int32(QB))
    if used % 8 == 0:
        begin = pl.multiple_of(begin, 8)
    factors = wide[pl.ds(begin, used), :]
    first.wait()
    blocks = raw[...].astype(F32).reshape(used, mine // used, ff)
    kept = (blocks * factors[:, None, :]).astype(BF16).reshape(mine, ff)
    begin = 0
    for out in outs:
        end = begin + out.shape[1]
        out[...] = kept[:, begin:end]
        begin = end


def select_body(dims, stride, pos, ids, ids_pair, *picks):
    _, _, locals_ = dims
    pairs = locals_ // 2
    count = ids.shape[1]
    high = max(16, pairs)
    first = lax.broadcasted_iota(jnp.int32, (count, count), 0)
    second = lax.broadcasted_iota(jnp.int32, (count, count), 1)
    earlier = (first < second).astype(F32).astype(BF16)
    places = lax.broadcasted_iota(jnp.int32, (pairs * stride, count), 0)
    owner = lax.shift_right_logical(pos[2], 1)
    held = jnp.zeros((high, 1), F32)
    for chosen, pick in zip((ids[...], ids_pair[...]), picks):
        group = lax.shift_right_logical(chosen, 1)
        if pairs & (pairs - 1) == 0:
            relative = lax.bitwise_xor(group, owner)
        else:
            relative = lax.rem(group - owner + pairs, pairs)
        mine = lax.bitwise_and(chosen, 1) == lax.bitwise_and(pos[2], 1)
        relative = jnp.where(mine, relative, high)
        onehot = relative == lax.broadcasted_iota(jnp.int32, (high, count), 0)
        marks = onehot.astype(F32)
        ranks = held + jnp.dot(marks.astype(BF16), earlier, preferred_element_type=F32)
        rank = jnp.sum(jnp.where(onehot, ranks, 0.0), axis=0, keepdims=True)
        slot = jnp.where(mine, relative * stride + rank.astype(jnp.int32), -1)
        pick[...] = (slot == places).astype(F32).astype(BF16)
        held = held + jnp.sum(marks, axis=1, keepdims=True)


def place_rows(dims, stride, columns, pos, picks, sources, outs):
    copies, nodes, locals_ = dims
    pairs = locals_ // 2
    rows, width = outs[0].shape[0], outs[0].shape[1] // len(columns[0])
    for g, group in enumerate(columns):
        for j in reversed(range(copies)):
            which = traced_mate(pos[0], j, copies)
            for b, (relative, block) in enumerate(group):
                if relative:
                    block = traced_mate(pos[1], block, nodes)
                at = pl.multiple_of((block * copies + which) * width, 128)
                got = sum(
                    jnp.dot(pick[...], source[:, pl.ds(at, width)], preferred_element_type=F32)
                    for pick, source in zip(picks, sources)
                ).astype(BF16)
                for k in range(pairs):
                    out = outs[(g * copies + j) * pairs + k]
                    out[:, b * width : (b + 1) * width] = got[k * stride : k * stride + rows]


def choose_body(dims, stride, pos, ids, ids_pair, rows, *refs):
    picks, near, sem = refs[:2], refs[2], refs[3]
    move = pltpu.make_async_copy(rows, near, sem)
    move.start()
    select_body(dims, stride, pos, ids, ids_pair, *picks)
    move.wait()


def route_body(dims, stride, columns, pos, pick, pick_pair, rows, rows_pair, *outs):
    place_rows(dims, stride, columns, pos, (pick, pick_pair), (rows, rows_pair), outs)


def join_body(dims, stride, pos, *refs):
    copies, _, locals_ = dims
    pairs = locals_ // 2
    pieces, out = refs[:-1], refs[-1]
    rows, width = pieces[0].shape
    for j in range(copies):
        base = traced_origin(pos[0], j, copies) * (pairs * stride)
        for k in range(pairs):
            at = pl.multiple_of(base + k * stride, 16)
            block = pieces[j * pairs + k][...]
            if rows < stride:
                blank = jnp.zeros((stride - rows, width), block.dtype)
                block = jnp.concatenate([block, blank], axis=0)
            out[pl.ds(at, stride), :] = block


def turn_body(dims, stride, pos, *refs):
    pieces, out, held = refs[:-2], refs[-2], refs[-1]
    join_body(dims, stride, pos, *pieces, held)
    out[...] = jnp.transpose(held[...])


def up_body(dims, pos, rows, *refs):
    _, nodes, _ = dims
    weights, outs, held = refs[:nodes], refs[nodes:-1], refs[-1]
    mine = weights[0].shape[0]
    for s in range(nodes):
        at = pl.multiple_of(traced_origin(pos[1], s, nodes) * mine, 16)
        held[pl.ds(at, mine), :] = weights[s][...]
    begin = 0
    for kept, sent in zip(outs[::2], outs[1::2]):
        end = begin + kept.shape[1]
        pre = jnp.dot(rows[...], held[:, begin:end], preferred_element_type=F32)
        kept[...] = pre
        sent[...] = pre.astype(BF16)
        begin = end


def down_body(dims, factor, spots, sources, emits, pos, *refs):
    nodes = dims[1]
    tables = 1 + max(table for _, table, _ in spots)
    turned, rest, act = refs[:tables], list(refs[tables:-1]), refs[-1]
    begin = 0
    used = sum(sources)
    outs, kept_acts = rest[used : used + len(spots)], rest[used + len(spots) :]
    for held, emit in zip(sources, emits):
        if held and rest[0].dtype == F32:
            pre = rest[0][...]
            for part in rest[1:held]:
                pre = pre + part[...].astype(F32)
            value = (pre * jax.nn.sigmoid(pre)).astype(BF16)
        else:
            value = rest[0][...]
        rest = rest[held:]
        end = begin + value.shape[1]
        act[:, begin:end] = value
        if emit:
            kept_acts[0][...] = value
            kept_acts = kept_acts[1:]
        begin = end
    mine = outs[0].shape[0]
    for (s, table, place), out in zip(spots, outs):
        at = place * mine
        if place < 0:
            at = pl.multiple_of(traced_mate(pos[1], s, nodes) * mine, 16)
        term = jnp.dot(turned[table][pl.ds(at, mine), :], act[...], preferred_element_type=F32)
        out[...] = (term * factor).astype(out.dtype)


def sum_body(begins, pos, own, *refs):
    total, out = refs[-1], refs[-2]
    total[...] = own[...]
    for begin, part in zip(begins, refs[:-2]):
        end = begin + part.shape[1]
        total[:, begin:end] += part[...].astype(F32)
    out[...] = total[...].astype(BF16)


def lay_body(dims, spots, pos, *refs):
    copies = dims[0]
    parts, out, sems = refs[: len(spots)], refs[-2], refs[-1]
    moves = []
    for i, (part, (j, begin)) in enumerate(zip(parts, spots)):
        mine, width = part.shape
        at = pl.multiple_of(traced_origin(pos[0], j, copies) * mine, 16)
        spot = out.at[pl.ds(at, mine), pl.ds(begin, width)]
        moves.append(pltpu.make_async_copy(part, spot, sems.at[i]))
    for move in moves:
        move.start()
    for move in moves:
        move.wait()


def on_device(tokens, cotangent, expert_of, w1_codes, w1_scales):
    copies, nodes, locals_ = (lax.axis_size(a) for a in ("dp", "node", "local"))
    dims = (copies, nodes, locals_)
    count, features = tokens.shape
    capacity = 5 * count // (4 * locals_)
    pairs = locals_ // 2
    sent_rows = -(-2 * capacity // 8) * 8
    stride = -(-sent_rows // 16) * 16
    shard, hidden = w1_codes.shape[1:]
    mine = shard // copies
    part = features // copies
    unit = hidden // sum(sum(split) for split in SPLITS)
    gathered = [unit * sum(split) for split in SPLITS]
    everyone = copies * pairs * stride
    pos = jnp.stack([lax.axis_index(a) for a in ("dp", "node", "local")]).astype(jnp.int32)

    aligned = mine % 128 == 0
    halves, jobs, outputs = plan_of(nodes, aligned)
    if aligned:
        columns_x = [[(False, b) for b in range(nodes)]]
        columns_y = [[(True, s) for s in half] for half in halves]
    else:
        columns_x = columns_y = [[(False, 0)]]
        tokens, cotangent = (
            a.reshape(count, nodes, copies, mine).swapaxes(1, 2).reshape(count, features)
            for a in (tokens, cotangent)
        )
    chosen = expert_of.reshape(1, count)
    swap = [(i, i ^ 1) for i in range(locals_)]
    tokens_pair = lax.ppermute(tokens, "local", swap)
    chosen_pair = lax.ppermute(chosen, "local", swap)
    cotangent_pair = lax.ppermute(cotangent, "local", swap)

    weights = call(
        dequant_body,
        [shape(mine, w, BF16) for w in gathered],
        pos,
        [pltpu.with_memory_space_constraint(a[0], pltpu.HBM) for a in (w1_codes, w1_scales)],
        [
            pltpu.VMEM((mine, hidden), BF16),
            pltpu.VMEM((shard // QB, hidden), BF16),
            pltpu.VMEM((shard // QB, hidden), F32),
            pltpu.SemaphoreType.DMA((2,)),
        ],
        space=pltpu.HBM,
    )
    order = node_order(nodes)
    held = []
    for chunk in weights:
        got = {0: chunk}
        for s in order:
            got[s] = lax.ppermute(chunk, "node", [(a, mate(a, s, nodes)) for a in range(nodes)])
        held.append([got[s] for s in range(nodes)])

    *picks, tokens = call(
        functools.partial(choose_body, dims, stride),
        [shape(pairs * stride, count, BF16)] * 2 + [shape(count, features, BF16)],
        pos,
        [chosen, chosen_pair, pltpu.with_memory_space_constraint(tokens, pltpu.HBM)],
        [pltpu.SemaphoreType.DMA],
        space=[pltpu.VMEM, pltpu.VMEM, pltpu.HBM],
    )

    def route(columns, rows, rows_pair):
        pieces = call(
            functools.partial(route_body, dims, stride, columns),
            [shape(sent_rows, part // len(columns), BF16)] * (len(columns) * copies * pairs),
            pos,
            [*picks, rows, rows_pair],
            flops=4 * pairs * stride * count * features,
        )
        step = copies * pairs
        return [pieces[g * step : (g + 1) * step] for g in range(len(columns))]

    (pieces_x,) = route(columns_x, tokens, tokens_pair)
    pieces_y = route(columns_y, cotangent, cotangent_pair)

    def exchange(pieces):
        moved = list(pieces)
        for j, k in slots_of(copies, pairs):
            links = [
                (a * locals_ + b, mate(a, j, copies) * locals_ + 2 * mate(b // 2, k, pairs) + b % 2)
                for a in range(copies)
                for b in range(locals_)
            ]
            at = j * pairs + k
            moved[at] = lax.ppermute(pieces[at], ("dp", "local"), links)
        return moved

    (rows_x,) = call(
        functools.partial(join_body, dims, stride),
        [shape(everyone, part, BF16)],
        pos,
        exchange(pieces_x),
    )
    turned = []
    for h, pieces in enumerate(pieces_y):
        cols = part // len(pieces_y)
        got_dy = exchange(pieces)
        turned += call(
            functools.partial(turn_body, dims, stride),
            [shape(cols, everyone, BF16)],
            pos,
            got_dy,
            [pltpu.VMEM((everyone, cols), BF16)],
        )
    factor = float(count * copies * nodes) ** (-0.5)
    groups = []
    for i, split in enumerate(SPLITS):
        widths = [unit * share for share in split]
        parts = call(
            functools.partial(up_body, dims),
            [shape(everyone, w, kind) for w in widths for kind in (F32, BF16)],
            pos,
            [rows_x] + held[i],
            [pltpu.VMEM((part, gathered[i]), BF16)],
            flops=2 * everyone * part * gathered[i],
        )
        groups += list(zip(widths, parts[::2], parts[1::2]))
    acts = []
    for wide, kept, sent in groups:
        if copies == 2:
            acts.append([kept, lax.ppermute(sent, "dp", [(0, 1), (1, 0)])])
        else:
            acts.append([lax.psum(kept, "dp")])
    owns, arrived = {}, {}
    for n, (chunks, targets) in enumerate(jobs):
        wide = sum(groups[i][0] for i in chunks)
        tables = [h for h, half in enumerate(halves) if set(half) & set(targets)]
        spots = []
        for s in targets:
            (h,) = [h for h in tables if s in halves[h]]
            spots.append((s, tables.index(h), halves[h].index(s) if aligned else -1))
        again = [any(i in other for other, _ in jobs[n + 1 :]) for i in chunks]
        emits = [more and acts[i][0].dtype == F32 for i, more in zip(chunks, again)]
        kinds = [shape(mine, wide, BF16 if s else F32) for s in targets]
        kinds += [shape(everyone, groups[i][0], BF16) for i, emit in zip(chunks, emits) if emit]
        terms = call(
            functools.partial(down_body, dims, factor, spots, [len(acts[i]) for i in chunks], emits),
            kinds,
            pos,
            [turned[h] for h in tables] + sum((acts[i] for i in chunks), []),
            [pltpu.VMEM((everyone, wide), BF16)],
            flops=2 * everyone * len(targets) * mine * wide,
        )
        extra = list(terms[len(targets) :])
        for i, emit in zip(chunks, emits):
            if emit:
                acts[i] = [extra.pop(0)]
        (group,) = [g for g, members in enumerate(outputs) if chunks[0] in members]
        begin = sum(groups[i][0] for i in outputs[group] if i < chunks[0])
        for s, term in zip(targets, terms):
            if s == 0:
                owns[group] = term
                continue
            links = [(a, mate(a, s, nodes)) for a in range(nodes)]
            moved = lax.ppermute(term, "node", links)
            arrived.setdefault(group, []).append((begin, moved))
    finished = []
    for i in range(len(outputs)):
        wide = owns[i].shape[1]
        begins = [begin for begin, _ in arrived[i]]
        (summed,) = call(
            functools.partial(sum_body, begins),
            [shape(mine, wide, BF16)],
            pos,
            [owns[i]] + [moved for _, moved in arrived[i]],
            [pltpu.VMEM((mine, wide), F32)],
        )
        finished.append(summed)
        for j in range(1, copies):
            links = [(a, mate(a, j, copies)) for a in range(copies)]
            finished.append(lax.ppermute(summed, "dp", links))
    spots = []
    begin = 0
    for i in range(len(outputs)):
        spots += [(j, begin) for j in range(copies)]
        begin += owns[i].shape[1]
    early = len(finished) - copies + 1
    last = copies - 1
    (result,) = call(
        functools.partial(lay_body, dims, spots[:early]),
        [shape(shard, hidden, BF16)],
        pos,
        finished[:early],
        [pltpu.SemaphoreType.DMA((early,))],
        target=pltpu.HBM,
    )
    (result,) = call(
        functools.partial(lay_body, dims, spots[early:]),
        [shape(shard, hidden, BF16)],
        pos,
        finished[early:] + [result],
        [pltpu.SemaphoreType.DMA((last,))],
        space=[pltpu.VMEM] * last + [pltpu.HBM],
        target=pltpu.HBM,
        aliases={last + 1: 0},
    )
    return result[None]


def solution(mesh):
    rows = P(("dp", "node", "local"), None)
    weights = P("local", "node", None)
    return jax.shard_map(
        on_device,
        mesh=mesh,
        in_specs=(rows, rows, rows, weights, weights),
        out_specs=weights,
        check_vma=False,
    )
```

```python
import functools
import jax
import jax.numpy as jnp
from jax import lax
from jax.experimental import pallas as pl
from jax.experimental.pallas import tpu as pltpu
from jax.sharding import PartitionSpec as P

QB = 32
SPLITS = ((1, 2, 1),)
F32 = jnp.float32
BF16 = jnp.bfloat16


def mate(i, k, size):
    return i ^ k if size & (size - 1) == 0 else (i + k) % size


def traced_mate(i, k, size):
    return lax.bitwise_xor(i, jnp.int32(k)) if size & (size - 1) == 0 else lax.rem(i + k, size)


def traced_origin(i, k, size):
    if size & (size - 1) == 0:
        return lax.bitwise_xor(i, jnp.int32(k))
    return lax.rem(i + (size - k), size)


def call(body, outs, scalars, args, scratch=(), flops=0, space=pltpu.VMEM, target=pltpu.VMEM, aliases=None):
    moved = sum(a.size * a.dtype.itemsize for a in args)
    moved += sum(o.size * o.dtype.itemsize for o in outs)
    spaces = space if isinstance(space, list) else [space] * len(args)
    room = 2 * moved + (8 << 20)
    return pl.pallas_call(
        body,
        out_shape=outs,
        in_specs=[pl.BlockSpec(memory_space=pltpu.SMEM)]
        + [pl.BlockSpec(memory_space=kind) for kind in spaces],
        out_specs=[pl.BlockSpec(memory_space=target)] * len(outs),
        scratch_shapes=list(scratch),
        input_output_aliases=aliases or {},
        compiler_params=pltpu.CompilerParams(vmem_limit_bytes=min(room, 60 << 20)),
        cost_estimate=pl.CostEstimate(flops=flops, bytes_accessed=moved, transcendentals=0),
    )(scalars, *args)


def node_order(nodes):
    return [s for s in (3, 1, 2) if s < nodes] + list(range(4, nodes))


def plan_of(nodes):
    every = node_order(nodes) + [0]
    chunks = range(sum(len(split) for split in SPLITS))
    return [every], [([i], every) for i in chunks], [[i] for i in chunks]


def slots_of(copies, pairs):
    slots = [(j, k) for k in reversed(range(pairs)) for j in reversed(range(copies))]
    return [slot for slot in slots if slot != (0, 0)]


def shape(rows, cols, dtype):
    return jax.ShapeDtypeStruct((rows, cols), dtype)


def dequant_body(pos, codes, scales, *refs):
    outs, (raw, steps, wide, sems) = refs[:-4], refs[-4:]
    mine, ff = raw.shape
    at = pl.multiple_of(pos[0] * mine, 16)
    first = pltpu.make_async_copy(codes.at[pl.ds(at, mine), :], raw, sems.at[0])
    second = pltpu.make_async_copy(scales, steps, sems.at[1])
    first.start()
    second.start()
    second.wait()
    wide[...] = steps[...].astype(F32)
    used = max(1, mine // QB)
    begin = lax.div(pos[0] * mine, jnp.int32(QB))
    if used % 8 == 0:
        begin = pl.multiple_of(begin, 8)
    factors = wide[pl.ds(begin, used), :]
    first.wait()
    blocks = raw[...].astype(F32).reshape(used, mine // used, ff)
    kept = (blocks * factors[:, None, :]).astype(BF16).reshape(mine, ff)
    begin = 0
    for out in outs:
        end = begin + out.shape[1]
        out[...] = kept[:, begin:end]
        begin = end


def select_body(dims, stride, pos, ids, ids_pair, *picks):
    _, _, locals_ = dims
    pairs = locals_ // 2
    count = ids.shape[1]
    high = max(16, pairs)
    first = lax.broadcasted_iota(jnp.int32, (count, count), 0)
    second = lax.broadcasted_iota(jnp.int32, (count, count), 1)
    earlier = (first < second).astype(F32).astype(BF16)
    places = lax.broadcasted_iota(jnp.int32, (pairs * stride, count), 0)
    owner = lax.shift_right_logical(pos[2], 1)
    held = jnp.zeros((high, 1), F32)
    for chosen, pick in zip((ids[...], ids_pair[...]), picks):
        group = lax.shift_right_logical(chosen, 1)
        if pairs & (pairs - 1) == 0:
            relative = lax.bitwise_xor(group, owner)
        else:
            relative = lax.rem(group - owner + pairs, pairs)
        mine = lax.bitwise_and(chosen, 1) == lax.bitwise_and(pos[2], 1)
        relative = jnp.where(mine, relative, high)
        onehot = relative == lax.broadcasted_iota(jnp.int32, (high, count), 0)
        marks = onehot.astype(F32)
        ranks = held + jnp.dot(marks.astype(BF16), earlier, preferred_element_type=F32)
        rank = jnp.sum(jnp.where(onehot, ranks, 0.0), axis=0, keepdims=True)
        slot = jnp.where(mine, relative * stride + rank.astype(jnp.int32), -1)
        pick[...] = (slot == places).astype(F32).astype(BF16)
        held = held + jnp.sum(marks, axis=1, keepdims=True)


def place_rows(dims, stride, columns, pos, picks, sources, outs):
    copies, nodes, locals_ = dims
    pairs = locals_ // 2
    rows, width = outs[0].shape[0], outs[0].shape[1] // len(columns[0])
    for g, group in enumerate(columns):
        for j in reversed(range(copies)):
            which = traced_mate(pos[0], j, copies)
            for b, (relative, block) in enumerate(group):
                if relative:
                    block = traced_mate(pos[1], block, nodes)
                at = pl.multiple_of((block * copies + which) * width, 128)
                got = sum(
                    jnp.dot(pick[...], source[:, pl.ds(at, width)], preferred_element_type=F32)
                    for pick, source in zip(picks, sources)
                ).astype(BF16)
                for k in range(pairs):
                    out = outs[(g * copies + j) * pairs + k]
                    out[:, b * width : (b + 1) * width] = got[k * stride : k * stride + rows]


def choose_body(dims, stride, pos, ids, ids_pair, rows, *refs):
    picks, near, sem = refs[:2], refs[2], refs[3]
    move = pltpu.make_async_copy(rows, near, sem)
    move.start()
    select_body(dims, stride, pos, ids, ids_pair, *picks)
    move.wait()


def route_body(dims, stride, columns, pos, pick, pick_pair, rows, rows_pair, *outs):
    place_rows(dims, stride, columns, pos, (pick, pick_pair), (rows, rows_pair), outs)


def join_body(dims, stride, pos, *refs):
    copies, _, locals_ = dims
    pairs = locals_ // 2
    pieces, out = refs[:-1], refs[-1]
    rows, width = pieces[0].shape
    for j in range(copies):
        base = traced_origin(pos[0], j, copies) * (pairs * stride)
        for k in range(pairs):
            at = pl.multiple_of(base + k * stride, 16)
            block = pieces[j * pairs + k][...]
            if rows < stride:
                blank = jnp.zeros((stride - rows, width), block.dtype)
                block = jnp.concatenate([block, blank], axis=0)
            out[pl.ds(at, stride), :] = block


def turn_body(dims, stride, pos, *refs):
    pieces, out, held = refs[:-2], refs[-2], refs[-1]
    join_body(dims, stride, pos, *pieces, held)
    out[...] = jnp.transpose(held[...])


def up_body(dims, pos, rows, *refs):
    _, nodes, _ = dims
    weights, outs, held = refs[:nodes], refs[nodes:-1], refs[-1]
    mine = weights[0].shape[0]
    for s in range(nodes):
        at = pl.multiple_of(traced_origin(pos[1], s, nodes) * mine, 16)
        held[pl.ds(at, mine), :] = weights[s][...]
    begin = 0
    for kept, sent in zip(outs[::2], outs[1::2]):
        end = begin + kept.shape[1]
        pre = jnp.dot(rows[...], held[:, begin:end], preferred_element_type=F32)
        kept[...] = pre
        sent[...] = pre.astype(BF16)
        begin = end


def down_body(dims, factor, spots, sources, emits, pos, *refs):
    nodes = dims[1]
    tables = 1 + max(table for _, table, _ in spots)
    turned, rest, act = refs[:tables], list(refs[tables:-1]), refs[-1]
    begin = 0
    used = sum(sources)
    outs, kept_acts = rest[used : used + len(spots)], rest[used + len(spots) :]
    for held, emit in zip(sources, emits):
        if held and rest[0].dtype == F32:
            pre = rest[0][...]
            for part in rest[1:held]:
                pre = pre + part[...].astype(F32)
            value = (pre * jax.nn.sigmoid(pre)).astype(BF16)
        else:
            value = rest[0][...]
        rest = rest[held:]
        end = begin + value.shape[1]
        act[:, begin:end] = value
        if emit:
            kept_acts[0][...] = value
            kept_acts = kept_acts[1:]
        begin = end
    mine = outs[0].shape[0]
    for (s, table, place), out in zip(spots, outs):
        at = place * mine
        if place < 0:
            at = pl.multiple_of(traced_mate(pos[1], s, nodes) * mine, 16)
        term = jnp.dot(turned[table][pl.ds(at, mine), :], act[...], preferred_element_type=F32)
        out[...] = (term * factor).astype(out.dtype)


def sum_body(begins, pos, own, *refs):
    total, out = refs[-1], refs[-2]
    total[...] = own[...]
    for begin, part in zip(begins, refs[:-2]):
        end = begin + part.shape[1]
        total[:, begin:end] += part[...].astype(F32)
    out[...] = total[...].astype(BF16)


def lay_body(dims, spots, pos, *refs):
    copies = dims[0]
    parts, out, sems = refs[: len(spots)], refs[-2], refs[-1]
    moves = []
    for i, (part, (j, begin)) in enumerate(zip(parts, spots)):
        mine, width = part.shape
        at = pl.multiple_of(traced_origin(pos[0], j, copies) * mine, 16)
        spot = out.at[pl.ds(at, mine), pl.ds(begin, width)]
        moves.append(pltpu.make_async_copy(part, spot, sems.at[i]))
    for move in moves:
        move.start()
    for move in moves:
        move.wait()


def on_device(tokens, cotangent, expert_of, w1_codes, w1_scales):
    copies, nodes, locals_ = (lax.axis_size(a) for a in ("dp", "node", "local"))
    dims = (copies, nodes, locals_)
    count, features = tokens.shape
    capacity = 5 * count // (4 * locals_)
    pairs = locals_ // 2
    sent_rows = -(-2 * capacity // 8) * 8
    stride = -(-sent_rows // 16) * 16
    shard, hidden = w1_codes.shape[1:]
    mine = shard // copies
    part = features // copies
    unit = hidden // sum(sum(split) for split in SPLITS)
    gathered = [unit * sum(split) for split in SPLITS]
    everyone = copies * pairs * stride
    pos = jnp.stack([lax.axis_index(a) for a in ("dp", "node", "local")]).astype(jnp.int32)

    aligned = mine % 128 == 0
    halves, jobs, outputs = plan_of(nodes)
    if aligned:
        columns_x = [[(False, b) for b in range(nodes)]]
        columns_y = [[(True, s) for s in half] for half in halves]
    else:
        columns_x = columns_y = [[(False, 0)]]
        tokens, cotangent = (
            a.reshape(count, nodes, copies, mine).swapaxes(1, 2).reshape(count, features)
            for a in (tokens, cotangent)
        )
    chosen = expert_of.reshape(1, count)
    swap = [(i, i ^ 1) for i in range(locals_)]
    tokens_pair = lax.ppermute(tokens, "local", swap)
    chosen_pair = lax.ppermute(chosen, "local", swap)
    cotangent_pair = lax.ppermute(cotangent, "local", swap)

    weights = call(
        dequant_body,
        [shape(mine, w, BF16) for w in gathered],
        pos,
        [pltpu.with_memory_space_constraint(a[0], pltpu.HBM) for a in (w1_codes, w1_scales)],
        [
            pltpu.VMEM((mine, hidden), BF16),
            pltpu.VMEM((shard // QB, hidden), BF16),
            pltpu.VMEM((shard // QB, hidden), F32),
            pltpu.SemaphoreType.DMA((2,)),
        ],
        space=pltpu.HBM,
    )
    order = node_order(nodes)
    held = []
    for chunk in weights:
        got = {0: chunk}
        for s in order:
            got[s] = lax.ppermute(chunk, "node", [(a, mate(a, s, nodes)) for a in range(nodes)])
        held.append([got[s] for s in range(nodes)])

    *picks, tokens = call(
        functools.partial(choose_body, dims, stride),
        [shape(pairs * stride, count, BF16)] * 2 + [shape(count, features, BF16)],
        pos,
        [chosen, chosen_pair, pltpu.with_memory_space_constraint(tokens, pltpu.HBM)],
        [pltpu.SemaphoreType.DMA],
        space=[pltpu.VMEM, pltpu.VMEM, pltpu.HBM],
    )

    def route(columns, rows, rows_pair):
        pieces = call(
            functools.partial(route_body, dims, stride, columns),
            [shape(sent_rows, part // len(columns), BF16)] * (len(columns) * copies * pairs),
            pos,
            [*picks, rows, rows_pair],
            flops=4 * pairs * stride * count * features,
        )
        step = copies * pairs
        return [pieces[g * step : (g + 1) * step] for g in range(len(columns))]

    (pieces_x,) = route(columns_x, tokens, tokens_pair)
    pieces_y = route(columns_y, cotangent, cotangent_pair)

    def exchange(pieces):
        moved = list(pieces)
        for j, k in slots_of(copies, pairs):
            links = [
                (a * locals_ + b, mate(a, j, copies) * locals_ + 2 * mate(b // 2, k, pairs) + b % 2)
                for a in range(copies)
                for b in range(locals_)
            ]
            at = j * pairs + k
            moved[at] = lax.ppermute(pieces[at], ("dp", "local"), links)
        return moved

    (rows_x,) = call(
        functools.partial(join_body, dims, stride),
        [shape(everyone, part, BF16)],
        pos,
        exchange(pieces_x),
    )
    turned = []
    for h, pieces in enumerate(pieces_y):
        cols = part // len(pieces_y)
        got_dy = exchange(pieces)
        turned += call(
            functools.partial(turn_body, dims, stride),
            [shape(cols, everyone, BF16)],
            pos,
            got_dy,
            [pltpu.VMEM((everyone, cols), BF16)],
        )
    factor = float(count * copies * nodes) ** (-0.5)
    groups = []
    for i, split in enumerate(SPLITS):
        widths = [unit * share for share in split]
        parts = call(
            functools.partial(up_body, dims),
            [shape(everyone, w, kind) for w in widths for kind in (F32, BF16)],
            pos,
            [rows_x] + held[i],
            [pltpu.VMEM((part, gathered[i]), BF16)],
            flops=2 * everyone * part * gathered[i],
        )
        groups += list(zip(widths, parts[::2], parts[1::2]))
    acts = []
    for wide, kept, sent in groups:
        if copies == 2:
            acts.append([kept, lax.ppermute(sent, "dp", [(0, 1), (1, 0)])])
        else:
            acts.append([lax.psum(kept, "dp")])
    owns, arrived = {}, {}
    for n, (chunks, targets) in enumerate(jobs):
        wide = sum(groups[i][0] for i in chunks)
        tables = [h for h, half in enumerate(halves) if set(half) & set(targets)]
        spots = []
        for s in targets:
            (h,) = [h for h in tables if s in halves[h]]
            spots.append((s, tables.index(h), halves[h].index(s) if aligned else -1))
        again = [any(i in other for other, _ in jobs[n + 1 :]) for i in chunks]
        emits = [more and acts[i][0].dtype == F32 for i, more in zip(chunks, again)]
        kinds = [shape(mine, wide, BF16 if s else F32) for s in targets]
        kinds += [shape(everyone, groups[i][0], BF16) for i, emit in zip(chunks, emits) if emit]
        terms = call(
            functools.partial(down_body, dims, factor, spots, [len(acts[i]) for i in chunks], emits),
            kinds,
            pos,
            [turned[h] for h in tables] + sum((acts[i] for i in chunks), []),
            [pltpu.VMEM((everyone, wide), BF16)],
            flops=2 * everyone * len(targets) * mine * wide,
        )
        extra = list(terms[len(targets) :])
        for i, emit in zip(chunks, emits):
            if emit:
                acts[i] = [extra.pop(0)]
        (group,) = [g for g, members in enumerate(outputs) if chunks[0] in members]
        begin = sum(groups[i][0] for i in outputs[group] if i < chunks[0])
        for s, term in zip(targets, terms):
            if s == 0:
                owns[group] = term
                continue
            links = [(a, mate(a, s, nodes)) for a in range(nodes)]
            moved = lax.ppermute(term, "node", links)
            arrived.setdefault(group, []).append((begin, moved))
    finished = []
    for i in range(len(outputs)):
        wide = owns[i].shape[1]
        begins = [begin for begin, _ in arrived[i]]
        (summed,) = call(
            functools.partial(sum_body, begins),
            [shape(mine, wide, BF16)],
            pos,
            [owns[i]] + [moved for _, moved in arrived[i]],
            [pltpu.VMEM((mine, wide), F32)],
        )
        finished.append(summed)
        for j in range(1, copies):
            links = [(a, mate(a, j, copies)) for a in range(copies)]
            finished.append(lax.ppermute(summed, "dp", links))
    spots = []
    begin = 0
    for i in range(len(outputs)):
        spots += [(j, begin) for j in range(copies)]
        begin += owns[i].shape[1]
    early = len(finished) - copies + 1
    last = copies - 1
    (result,) = call(
        functools.partial(lay_body, dims, spots[:early]),
        [shape(shard, hidden, BF16)],
        pos,
        finished[:early],
        [pltpu.SemaphoreType.DMA((early,))],
        target=pltpu.HBM,
    )
    (result,) = call(
        functools.partial(lay_body, dims, spots[early:]),
        [shape(shard, hidden, BF16)],
        pos,
        finished[early:] + [result],
        [pltpu.SemaphoreType.DMA((last,))],
        space=[pltpu.VMEM] * last + [pltpu.HBM],
        target=pltpu.HBM,
        aliases={last + 1: 0},
    )
    return result[None]


def solution(mesh):
    rows = P(("dp", "node", "local"), None)
    weights = P("local", "node", None)
    return jax.shard_map(
        on_device,
        mesh=mesh,
        in_specs=(rows, rows, rows, weights, weights),
        out_specs=weights,
        check_vma=False,
    )
```

```python
import functools
import jax
import jax.numpy as jnp
from jax import lax
from jax.experimental import pallas as pl
from jax.experimental.pallas import tpu as pltpu
from jax.sharding import PartitionSpec as P

QB = 32
SPLITS = ((2,), (1, 1))
F32 = jnp.float32
BF16 = jnp.bfloat16


def mate(i, k, size):
    return i ^ k if size & (size - 1) == 0 else (i + k) % size


def traced_mate(i, k, size):
    return lax.bitwise_xor(i, jnp.int32(k)) if size & (size - 1) == 0 else lax.rem(i + k, size)


def traced_origin(i, k, size):
    if size & (size - 1) == 0:
        return lax.bitwise_xor(i, jnp.int32(k))
    return lax.rem(i + (size - k), size)


def call(body, outs, scalars, args, scratch=(), flops=0, space=pltpu.VMEM, target=pltpu.VMEM, aliases=None):
    moved = sum(a.size * a.dtype.itemsize for a in args)
    moved += sum(o.size * o.dtype.itemsize for o in outs)
    spaces = space if isinstance(space, list) else [space] * len(args)
    room = 2 * moved + (8 << 20)
    return pl.pallas_call(
        body,
        out_shape=outs,
        in_specs=[pl.BlockSpec(memory_space=pltpu.SMEM)]
        + [pl.BlockSpec(memory_space=kind) for kind in spaces],
        out_specs=[pl.BlockSpec(memory_space=target)] * len(outs),
        scratch_shapes=list(scratch),
        input_output_aliases=aliases or {},
        compiler_params=pltpu.CompilerParams(vmem_limit_bytes=min(room, 60 << 20)),
        cost_estimate=pl.CostEstimate(flops=flops, bytes_accessed=moved, transcendentals=0),
    )(scalars, *args)


def node_order(nodes):
    return [s for s in (3, 1, 2) if s < nodes] + list(range(4, nodes))


def plan_of(nodes, aligned):
    order = node_order(nodes)
    every = order + [0]
    chunks = sum(len(split) for split in SPLITS)
    if not aligned:
        return [every], [([i], every) for i in range(chunks)], [[i] for i in range(chunks)]
    early, late = order[: nodes // 2], order[nodes // 2 :] + [0]
    jobs = [([0], early), ([0], late)] + [([i], every) for i in range(1, chunks)]
    return [early, late], jobs, [[i] for i in range(chunks)]


def slots_of(copies, pairs):
    slots = [(j, k) for k in range(pairs) for j in range(copies) if j or k]
    return sorted(slots, key=lambda slot: -(slot[0] > 0) - (slot[1] > 0))


def shape(rows, cols, dtype):
    return jax.ShapeDtypeStruct((rows, cols), dtype)


def dequant_body(pos, codes, scales, *refs):
    outs, (raw, steps, wide, sems) = refs[:-4], refs[-4:]
    mine, ff = raw.shape
    at = pl.multiple_of(pos[0] * mine, 16)
    first = pltpu.make_async_copy(codes.at[pl.ds(at, mine), :], raw, sems.at[0])
    second = pltpu.make_async_copy(scales, steps, sems.at[1])
    first.start()
    second.start()
    second.wait()
    wide[...] = steps[...].astype(F32)
    used = max(1, mine // QB)
    begin = lax.div(pos[0] * mine, jnp.int32(QB))
    if used % 8 == 0:
        begin = pl.multiple_of(begin, 8)
    factors = wide[pl.ds(begin, used), :]
    first.wait()
    blocks = raw[...].astype(F32).reshape(used, mine // used, ff)
    kept = (blocks * factors[:, None, :]).astype(BF16).reshape(mine, ff)
    begin = 0
    for out in outs:
        end = begin + out.shape[1]
        out[...] = kept[:, begin:end]
        begin = end


def select_body(dims, stride, pos, ids, ids_pair, *picks):
    _, _, locals_ = dims
    pairs = locals_ // 2
    count = ids.shape[1]
    high = max(16, pairs)
    first = lax.broadcasted_iota(jnp.int32, (count, count), 0)
    second = lax.broadcasted_iota(jnp.int32, (count, count), 1)
    earlier = (first < second).astype(F32).astype(BF16)
    places = lax.broadcasted_iota(jnp.int32, (pairs * stride, count), 0)
    owner = lax.shift_right_logical(pos[2], 1)
    held = jnp.zeros((high, 1), F32)
    for chosen, pick in zip((ids[...], ids_pair[...]), picks):
        group = lax.shift_right_logical(chosen, 1)
        if pairs & (pairs - 1) == 0:
            relative = lax.bitwise_xor(group, owner)
        else:
            relative = lax.rem(group - owner + pairs, pairs)
        mine = lax.bitwise_and(chosen, 1) == lax.bitwise_and(pos[2], 1)
        relative = jnp.where(mine, relative, high)
        onehot = relative == lax.broadcasted_iota(jnp.int32, (high, count), 0)
        marks = onehot.astype(F32)
        ranks = held + jnp.dot(marks.astype(BF16), earlier, preferred_element_type=F32)
        rank = jnp.sum(jnp.where(onehot, ranks, 0.0), axis=0, keepdims=True)
        slot = jnp.where(mine, relative * stride + rank.astype(jnp.int32), -1)
        pick[...] = (slot == places).astype(F32).astype(BF16)
        held = held + jnp.sum(marks, axis=1, keepdims=True)


def place_rows(dims, stride, columns, pos, picks, sources, outs):
    copies, nodes, locals_ = dims
    pairs = locals_ // 2
    rows, width = outs[0].shape[0], outs[0].shape[1] // len(columns[0])
    for g, group in enumerate(columns):
        for j in reversed(range(copies)):
            which = traced_mate(pos[0], j, copies)
            for b, (relative, block) in enumerate(group):
                if relative:
                    block = traced_mate(pos[1], block, nodes)
                at = pl.multiple_of((block * copies + which) * width, 128)
                got = sum(
                    jnp.dot(pick[...], source[:, pl.ds(at, width)], preferred_element_type=F32)
                    for pick, source in zip(picks, sources)
                ).astype(BF16)
                for k in range(pairs):
                    out = outs[(g * copies + j) * pairs + k]
                    out[:, b * width : (b + 1) * width] = got[k * stride : k * stride + rows]


def choose_body(dims, stride, pos, ids, ids_pair, rows, *refs):
    picks, near, sem = refs[:2], refs[2], refs[3]
    move = pltpu.make_async_copy(rows, near, sem)
    move.start()
    select_body(dims, stride, pos, ids, ids_pair, *picks)
    move.wait()


def route_body(dims, stride, columns, pos, pick, pick_pair, rows, rows_pair, *outs):
    place_rows(dims, stride, columns, pos, (pick, pick_pair), (rows, rows_pair), outs)


def join_body(dims, stride, pos, *refs):
    copies, _, locals_ = dims
    pairs = locals_ // 2
    pieces, out = refs[:-1], refs[-1]
    rows, width = pieces[0].shape
    for j in range(copies):
        base = traced_origin(pos[0], j, copies) * (pairs * stride)
        for k in range(pairs):
            at = pl.multiple_of(base + k * stride, 16)
            block = pieces[j * pairs + k][...]
            if rows < stride:
                blank = jnp.zeros((stride - rows, width), block.dtype)
                block = jnp.concatenate([block, blank], axis=0)
            out[pl.ds(at, stride), :] = block


def turn_body(dims, stride, pos, *refs):
    pieces, out, held = refs[:-2], refs[-2], refs[-1]
    join_body(dims, stride, pos, *pieces, held)
    out[...] = jnp.transpose(held[...])


def up_body(dims, pos, rows, *refs):
    _, nodes, _ = dims
    weights, outs, held = refs[:nodes], refs[nodes:-1], refs[-1]
    mine = weights[0].shape[0]
    for s in range(nodes):
        at = pl.multiple_of(traced_origin(pos[1], s, nodes) * mine, 16)
        held[pl.ds(at, mine), :] = weights[s][...]
    begin = 0
    for kept, sent in zip(outs[::2], outs[1::2]):
        end = begin + kept.shape[1]
        pre = jnp.dot(rows[...], held[:, begin:end], preferred_element_type=F32)
        kept[...] = pre
        sent[...] = pre.astype(BF16)
        begin = end


def down_body(dims, factor, spots, sources, emits, pos, *refs):
    nodes = dims[1]
    tables = 1 + max(table for _, table, _ in spots)
    turned, rest, act = refs[:tables], list(refs[tables:-1]), refs[-1]
    begin = 0
    used = sum(sources)
    outs, kept_acts = rest[used : used + len(spots)], rest[used + len(spots) :]
    for held, emit in zip(sources, emits):
        if held and rest[0].dtype == F32:
            pre = rest[0][...]
            for part in rest[1:held]:
                pre = pre + part[...].astype(F32)
            value = (pre * jax.nn.sigmoid(pre)).astype(BF16)
        else:
            value = rest[0][...]
        rest = rest[held:]
        end = begin + value.shape[1]
        act[:, begin:end] = value
        if emit:
            kept_acts[0][...] = value
            kept_acts = kept_acts[1:]
        begin = end
    mine = outs[0].shape[0]
    for (s, table, place), out in zip(spots, outs):
        at = place * mine
        if place < 0:
            at = pl.multiple_of(traced_mate(pos[1], s, nodes) * mine, 16)
        term = jnp.dot(turned[table][pl.ds(at, mine), :], act[...], preferred_element_type=F32)
        out[...] = (term * factor).astype(out.dtype)


def sum_body(begins, pos, own, *refs):
    total, out = refs[-1], refs[-2]
    total[...] = own[...]
    for begin, part in zip(begins, refs[:-2]):
        end = begin + part.shape[1]
        total[:, begin:end] += part[...].astype(F32)
    out[...] = total[...].astype(BF16)


def lay_body(dims, spots, pos, *refs):
    copies = dims[0]
    parts, out, sems = refs[: len(spots)], refs[-2], refs[-1]
    moves = []
    for i, (part, (j, begin)) in enumerate(zip(parts, spots)):
        mine, width = part.shape
        at = pl.multiple_of(traced_origin(pos[0], j, copies) * mine, 16)
        spot = out.at[pl.ds(at, mine), pl.ds(begin, width)]
        moves.append(pltpu.make_async_copy(part, spot, sems.at[i]))
    for move in moves:
        move.start()
    for move in moves:
        move.wait()


def on_device(tokens, cotangent, expert_of, w1_codes, w1_scales):
    copies, nodes, locals_ = (lax.axis_size(a) for a in ("dp", "node", "local"))
    dims = (copies, nodes, locals_)
    count, features = tokens.shape
    capacity = 5 * count // (4 * locals_)
    pairs = locals_ // 2
    sent_rows = -(-2 * capacity // 8) * 8
    stride = -(-sent_rows // 16) * 16
    shard, hidden = w1_codes.shape[1:]
    mine = shard // copies
    part = features // copies
    unit = hidden // sum(sum(split) for split in SPLITS)
    gathered = [unit * sum(split) for split in SPLITS]
    everyone = copies * pairs * stride
    pos = jnp.stack([lax.axis_index(a) for a in ("dp", "node", "local")]).astype(jnp.int32)

    aligned = mine % 128 == 0
    halves, jobs, outputs = plan_of(nodes, aligned)
    if aligned:
        columns_x = [[(False, b) for b in range(nodes)]]
        columns_y = [[(True, s) for s in half] for half in halves]
    else:
        columns_x = columns_y = [[(False, 0)]]
        tokens, cotangent = (
            a.reshape(count, nodes, copies, mine).swapaxes(1, 2).reshape(count, features)
            for a in (tokens, cotangent)
        )
    chosen = expert_of.reshape(1, count)
    swap = [(i, i ^ 1) for i in range(locals_)]
    tokens_pair = lax.ppermute(tokens, "local", swap)
    chosen_pair = lax.ppermute(chosen, "local", swap)
    cotangent_pair = lax.ppermute(cotangent, "local", swap)

    weights = call(
        dequant_body,
        [shape(mine, w, BF16) for w in gathered],
        pos,
        [pltpu.with_memory_space_constraint(a[0], pltpu.HBM) for a in (w1_codes, w1_scales)],
        [
            pltpu.VMEM((mine, hidden), BF16),
            pltpu.VMEM((shard // QB, hidden), BF16),
            pltpu.VMEM((shard // QB, hidden), F32),
            pltpu.SemaphoreType.DMA((2,)),
        ],
        space=pltpu.HBM,
    )
    order = node_order(nodes)
    held = []
    for chunk in weights:
        got = {0: chunk}
        for s in order:
            got[s] = lax.ppermute(chunk, "node", [(a, mate(a, s, nodes)) for a in range(nodes)])
        held.append([got[s] for s in range(nodes)])

    *picks, tokens = call(
        functools.partial(choose_body, dims, stride),
        [shape(pairs * stride, count, BF16)] * 2 + [shape(count, features, BF16)],
        pos,
        [chosen, chosen_pair, pltpu.with_memory_space_constraint(tokens, pltpu.HBM)],
        [pltpu.SemaphoreType.DMA],
        space=[pltpu.VMEM, pltpu.VMEM, pltpu.HBM],
    )

    def route(columns, rows, rows_pair):
        pieces = call(
            functools.partial(route_body, dims, stride, columns),
            [shape(sent_rows, part // len(columns), BF16)] * (len(columns) * copies * pairs),
            pos,
            [*picks, rows, rows_pair],
            flops=4 * pairs * stride * count * features,
        )
        step = copies * pairs
        return [pieces[g * step : (g + 1) * step] for g in range(len(columns))]

    (pieces_x,) = route(columns_x, tokens, tokens_pair)
    pieces_y = route(columns_y, cotangent, cotangent_pair)

    def exchange(pieces):
        moved = list(pieces)
        for j, k in slots_of(copies, pairs):
            links = [
                (a * locals_ + b, mate(a, j, copies) * locals_ + 2 * mate(b // 2, k, pairs) + b % 2)
                for a in range(copies)
                for b in range(locals_)
            ]
            at = j * pairs + k
            moved[at] = lax.ppermute(pieces[at], ("dp", "local"), links)
        return moved

    (rows_x,) = call(
        functools.partial(join_body, dims, stride),
        [shape(everyone, part, BF16)],
        pos,
        exchange(pieces_x),
    )
    turned = []
    for h, pieces in enumerate(pieces_y):
        cols = part // len(pieces_y)
        got_dy = exchange(pieces)
        turned += call(
            functools.partial(turn_body, dims, stride),
            [shape(cols, everyone, BF16)],
            pos,
            got_dy,
            [pltpu.VMEM((everyone, cols), BF16)],
        )
    factor = float(count * copies * nodes) ** (-0.5)
    groups = []
    for i, split in enumerate(SPLITS):
        widths = [unit * share for share in split]
        parts = call(
            functools.partial(up_body, dims),
            [shape(everyone, w, kind) for w in widths for kind in (F32, BF16)],
            pos,
            [rows_x] + held[i],
            [pltpu.VMEM((part, gathered[i]), BF16)],
            flops=2 * everyone * part * gathered[i],
        )
        groups += list(zip(widths, parts[::2], parts[1::2]))
    acts = []
    for wide, kept, sent in groups:
        if copies == 2:
            acts.append([kept, lax.ppermute(sent, "dp", [(0, 1), (1, 0)])])
        else:
            acts.append([lax.psum(kept, "dp")])
    owns, arrived = {}, {}
    for n, (chunks, targets) in enumerate(jobs):
        wide = sum(groups[i][0] for i in chunks)
        tables = [h for h, half in enumerate(halves) if set(half) & set(targets)]
        spots = []
        for s in targets:
            (h,) = [h for h in tables if s in halves[h]]
            spots.append((s, tables.index(h), halves[h].index(s) if aligned else -1))
        again = [any(i in other for other, _ in jobs[n + 1 :]) for i in chunks]
        emits = [more and acts[i][0].dtype == F32 for i, more in zip(chunks, again)]
        kinds = [shape(mine, wide, BF16 if s else F32) for s in targets]
        kinds += [shape(everyone, groups[i][0], BF16) for i, emit in zip(chunks, emits) if emit]
        terms = call(
            functools.partial(down_body, dims, factor, spots, [len(acts[i]) for i in chunks], emits),
            kinds,
            pos,
            [turned[h] for h in tables] + sum((acts[i] for i in chunks), []),
            [pltpu.VMEM((everyone, wide), BF16)],
            flops=2 * everyone * len(targets) * mine * wide,
        )
        extra = list(terms[len(targets) :])
        for i, emit in zip(chunks, emits):
            if emit:
                acts[i] = [extra.pop(0)]
        (group,) = [g for g, members in enumerate(outputs) if chunks[0] in members]
        begin = sum(groups[i][0] for i in outputs[group] if i < chunks[0])
        for s, term in zip(targets, terms):
            if s == 0:
                owns[group] = term
                continue
            links = [(a, mate(a, s, nodes)) for a in range(nodes)]
            moved = lax.ppermute(term, "node", links)
            arrived.setdefault(group, []).append((begin, moved))
    finished = []
    for i in range(len(outputs)):
        wide = owns[i].shape[1]
        begins = [begin for begin, _ in arrived[i]]
        (summed,) = call(
            functools.partial(sum_body, begins),
            [shape(mine, wide, BF16)],
            pos,
            [owns[i]] + [moved for _, moved in arrived[i]],
            [pltpu.VMEM((mine, wide), F32)],
        )
        finished.append(summed)
        for j in range(1, copies):
            links = [(a, mate(a, j, copies)) for a in range(copies)]
            finished.append(lax.ppermute(summed, "dp", links))
    spots = []
    begin = 0
    for i in range(len(outputs)):
        spots += [(j, begin) for j in range(copies)]
        begin += owns[i].shape[1]
    items = list(zip(finished, spots))
    sure = copies * max(0, len(outputs) - 2)
    soon = [item for i, item in enumerate(items) if i < sure or item[1][0] == 0]
    late = [item for i, item in enumerate(items) if i >= sure and item[1][0] > 0]
    (result,) = call(
        functools.partial(lay_body, dims, [spot for _, spot in soon]),
        [shape(shard, hidden, BF16)],
        pos,
        [value for value, _ in soon],
        [pltpu.SemaphoreType.DMA((len(soon),))],
        target=pltpu.HBM,
    )
    (result,) = call(
        functools.partial(lay_body, dims, [spot for _, spot in late]),
        [shape(shard, hidden, BF16)],
        pos,
        [value for value, _ in late] + [result],
        [pltpu.SemaphoreType.DMA((len(late),))],
        space=[pltpu.VMEM] * len(late) + [pltpu.HBM],
        target=pltpu.HBM,
        aliases={len(late) + 1: 0},
    )
    return result[None]


def solution(mesh):
    rows = P(("dp", "node", "local"), None)
    weights = P("local", "node", None)
    return jax.shard_map(
        on_device,
        mesh=mesh,
        in_specs=(rows, rows, rows, weights, weights),
        out_specs=weights,
        check_vma=False,
    )
```

```python
import functools
import jax
import jax.numpy as jnp
from jax import lax
from jax.experimental import pallas as pl
from jax.experimental.pallas import tpu as pltpu
from jax.sharding import PartitionSpec as P

QB = 32
SPLITS = ((2,), (1, 1))
F32 = jnp.float32
BF16 = jnp.bfloat16


def mate(i, k, size):
    return i ^ k if size & (size - 1) == 0 else (i + k) % size


def traced_mate(i, k, size):
    return lax.bitwise_xor(i, jnp.int32(k)) if size & (size - 1) == 0 else lax.rem(i + k, size)


def traced_origin(i, k, size):
    if size & (size - 1) == 0:
        return lax.bitwise_xor(i, jnp.int32(k))
    return lax.rem(i + (size - k), size)


def call(body, outs, scalars, args, scratch=(), flops=0, space=pltpu.VMEM, target=pltpu.VMEM, aliases=None):
    moved = sum(a.size * a.dtype.itemsize for a in args)
    moved += sum(o.size * o.dtype.itemsize for o in outs)
    spaces = space if isinstance(space, list) else [space] * len(args)
    room = 2 * moved + (8 << 20)
    return pl.pallas_call(
        body,
        out_shape=outs,
        in_specs=[pl.BlockSpec(memory_space=pltpu.SMEM)]
        + [pl.BlockSpec(memory_space=kind) for kind in spaces],
        out_specs=[pl.BlockSpec(memory_space=target)] * len(outs),
        scratch_shapes=list(scratch),
        input_output_aliases=aliases or {},
        compiler_params=pltpu.CompilerParams(vmem_limit_bytes=min(room, 60 << 20)),
        cost_estimate=pl.CostEstimate(flops=flops, bytes_accessed=moved, transcendentals=0),
    )(scalars, *args)


def node_order(nodes):
    return [s for s in (3, 1, 2) if s < nodes] + list(range(4, nodes))


def plan_of(nodes, aligned):
    order = node_order(nodes)
    every = order + [0]
    chunks = sum(len(split) for split in SPLITS)
    if not aligned:
        return [every], [([i], every) for i in range(chunks)], [[i] for i in range(chunks)]
    early, late = order[: nodes // 2], order[nodes // 2 :] + [0]
    jobs = [([0], early), ([0], late)] + [([i], every) for i in range(1, chunks)]
    return [early, late], jobs, [[i] for i in range(chunks)]


def slots_of(copies, pairs):
    slots = [(j, k) for k in range(pairs) for j in range(copies) if j or k]
    return sorted(slots, key=lambda slot: -(slot[0] > 0) - (slot[1] > 0))


def shape(rows, cols, dtype):
    return jax.ShapeDtypeStruct((rows, cols), dtype)


def prep_body(dims, stride, pos, ids, ids_pair, rows, codes, scales, *refs):
    picks, near, outs = refs[:2], refs[2], refs[3:-4]
    raw, steps, wide, sems = refs[-4:]
    mine, ff = raw.shape
    at = pl.multiple_of(pos[0] * mine, 16)
    moves = [
        pltpu.make_async_copy(scales, steps, sems.at[0]),
        pltpu.make_async_copy(codes.at[pl.ds(at, mine), :], raw, sems.at[1]),
        pltpu.make_async_copy(rows, near, sems.at[2]),
    ]
    for move in moves:
        move.start()
    select_body(dims, stride, pos, ids, ids_pair, *picks)
    moves[0].wait()
    wide[...] = steps[...].astype(F32)
    used = max(1, mine // QB)
    begin = lax.div(pos[0] * mine, jnp.int32(QB))
    if used % 8 == 0:
        begin = pl.multiple_of(begin, 8)
    factors = wide[pl.ds(begin, used), :]
    moves[1].wait()
    blocks = raw[...].astype(F32).reshape(used, mine // used, ff)
    kept = (blocks * factors[:, None, :]).astype(BF16).reshape(mine, ff)
    begin = 0
    for out in outs:
        end = begin + out.shape[1]
        out[...] = kept[:, begin:end]
        begin = end
    moves[2].wait()


def select_body(dims, stride, pos, ids, ids_pair, *picks):
    _, _, locals_ = dims
    pairs = locals_ // 2
    count = ids.shape[1]
    high = max(16, pairs)
    first = lax.broadcasted_iota(jnp.int32, (count, count), 0)
    second = lax.broadcasted_iota(jnp.int32, (count, count), 1)
    earlier = (first < second).astype(F32).astype(BF16)
    places = lax.broadcasted_iota(jnp.int32, (pairs * stride, count), 0)
    owner = lax.shift_right_logical(pos[2], 1)
    held = jnp.zeros((high, 1), F32)
    for chosen, pick in zip((ids[...], ids_pair[...]), picks):
        group = lax.shift_right_logical(chosen, 1)
        if pairs & (pairs - 1) == 0:
            relative = lax.bitwise_xor(group, owner)
        else:
            relative = lax.rem(group - owner + pairs, pairs)
        mine = lax.bitwise_and(chosen, 1) == lax.bitwise_and(pos[2], 1)
        relative = jnp.where(mine, relative, high)
        onehot = relative == lax.broadcasted_iota(jnp.int32, (high, count), 0)
        marks = onehot.astype(F32)
        ranks = held + jnp.dot(marks.astype(BF16), earlier, preferred_element_type=F32)
        rank = jnp.sum(jnp.where(onehot, ranks, 0.0), axis=0, keepdims=True)
        slot = jnp.where(mine, relative * stride + rank.astype(jnp.int32), -1)
        pick[...] = (slot == places).astype(F32).astype(BF16)
        held = held + jnp.sum(marks, axis=1, keepdims=True)


def place_rows(dims, stride, columns, pos, picks, sources, outs):
    copies, nodes, locals_ = dims
    pairs = locals_ // 2
    rows, width = outs[0].shape[0], outs[0].shape[1] // len(columns[0])
    for g, group in enumerate(columns):
        for j in reversed(range(copies)):
            which = traced_mate(pos[0], j, copies)
            for b, (relative, block) in enumerate(group):
                if relative:
                    block = traced_mate(pos[1], block, nodes)
                at = pl.multiple_of((block * copies + which) * width, 128)
                got = sum(
                    jnp.dot(pick[...], source[:, pl.ds(at, width)], preferred_element_type=F32)
                    for pick, source in zip(picks, sources)
                ).astype(BF16)
                for k in range(pairs):
                    out = outs[(g * copies + j) * pairs + k]
                    out[:, b * width : (b + 1) * width] = got[k * stride : k * stride + rows]


def route_body(dims, stride, columns, pos, pick, pick_pair, rows, rows_pair, *outs):
    place_rows(dims, stride, columns, pos, (pick, pick_pair), (rows, rows_pair), outs)


def join_body(dims, stride, pos, *refs):
    copies, _, locals_ = dims
    pairs = locals_ // 2
    pieces, out = refs[:-1], refs[-1]
    rows, width = pieces[0].shape
    for j in range(copies):
        base = traced_origin(pos[0], j, copies) * (pairs * stride)
        for k in range(pairs):
            at = pl.multiple_of(base + k * stride, 16)
            block = pieces[j * pairs + k][...]
            if rows < stride:
                blank = jnp.zeros((stride - rows, width), block.dtype)
                block = jnp.concatenate([block, blank], axis=0)
            out[pl.ds(at, stride), :] = block


def turn_body(dims, stride, pos, *refs):
    pieces, out, held = refs[:-2], refs[-2], refs[-1]
    join_body(dims, stride, pos, *pieces, held)
    out[...] = jnp.transpose(held[...])


def up_body(dims, stride, given, pos, *refs):
    nodes = dims[1]
    pieces, weights, held = refs[:given], refs[given : given + nodes], refs[-1]
    outs = refs[given + nodes : -1]
    rows = pieces[0]
    if given > 1:
        rows, outs = outs[0], outs[1:]
        join_body(dims, stride, pos, *pieces, rows)
    mine = weights[0].shape[0]
    for s in range(nodes):
        at = pl.multiple_of(traced_origin(pos[1], s, nodes) * mine, 16)
        held[pl.ds(at, mine), :] = weights[s][...]
    begin = 0
    for kept, sent in zip(outs[::2], outs[1::2]):
        end = begin + kept.shape[1]
        pre = jnp.dot(rows[...], held[:, begin:end], preferred_element_type=F32)
        kept[...] = pre
        sent[...] = pre.astype(BF16)
        begin = end


def down_body(dims, factor, spots, sources, emits, pos, *refs):
    nodes = dims[1]
    tables = 1 + max(table for _, table, _ in spots)
    turned, rest, act = refs[:tables], list(refs[tables:-1]), refs[-1]
    begin = 0
    used = sum(sources)
    outs, kept_acts = rest[used : used + len(spots)], rest[used + len(spots) :]
    for held, emit in zip(sources, emits):
        if held and rest[0].dtype == F32:
            pre = rest[0][...]
            for part in rest[1:held]:
                pre = pre + part[...].astype(F32)
            value = (pre * jax.nn.sigmoid(pre)).astype(BF16)
        else:
            value = rest[0][...]
        rest = rest[held:]
        end = begin + value.shape[1]
        act[:, begin:end] = value
        if emit:
            kept_acts[0][...] = value
            kept_acts = kept_acts[1:]
        begin = end
    mine = outs[0].shape[0]
    for (s, table, place), out in zip(spots, outs):
        at = place * mine
        if place < 0:
            at = pl.multiple_of(traced_mate(pos[1], s, nodes) * mine, 16)
        term = jnp.dot(turned[table][pl.ds(at, mine), :], act[...], preferred_element_type=F32)
        out[...] = (term * factor).astype(out.dtype)


def sum_body(begins, pos, own, *refs):
    total, out = refs[-1], refs[-2]
    total[...] = own[...]
    for begin, part in zip(begins, refs[:-2]):
        end = begin + part.shape[1]
        total[:, begin:end] += part[...].astype(F32)
    out[...] = total[...].astype(BF16)


def lay_body(dims, spots, pos, *refs):
    copies = dims[0]
    parts, out, sems = refs[: len(spots)], refs[-2], refs[-1]
    moves = []
    for i, (part, (j, begin)) in enumerate(zip(parts, spots)):
        mine, width = part.shape
        at = pl.multiple_of(traced_origin(pos[0], j, copies) * mine, 16)
        spot = out.at[pl.ds(at, mine), pl.ds(begin, width)]
        moves.append(pltpu.make_async_copy(part, spot, sems.at[i]))
    for move in moves:
        move.start()
    for move in moves:
        move.wait()


def on_device(tokens, cotangent, expert_of, w1_codes, w1_scales):
    copies, nodes, locals_ = (lax.axis_size(a) for a in ("dp", "node", "local"))
    dims = (copies, nodes, locals_)
    count, features = tokens.shape
    capacity = 5 * count // (4 * locals_)
    pairs = locals_ // 2
    sent_rows = -(-2 * capacity // 8) * 8
    stride = -(-sent_rows // 16) * 16
    shard, hidden = w1_codes.shape[1:]
    mine = shard // copies
    part = features // copies
    unit = hidden // sum(sum(split) for split in SPLITS)
    gathered = [unit * sum(split) for split in SPLITS]
    everyone = copies * pairs * stride
    pos = jnp.stack([lax.axis_index(a) for a in ("dp", "node", "local")]).astype(jnp.int32)

    aligned = mine % 128 == 0
    halves, jobs, outputs = plan_of(nodes, aligned)
    if aligned:
        columns_x = [[(False, b) for b in range(nodes)]]
        columns_y = [[(True, s) for s in half] for half in halves]
    else:
        columns_x = columns_y = [[(False, 0)]]
        tokens, cotangent = (
            a.reshape(count, nodes, copies, mine).swapaxes(1, 2).reshape(count, features)
            for a in (tokens, cotangent)
        )
    chosen = expert_of.reshape(1, count)
    swap = [(i, i ^ 1) for i in range(locals_)]
    tokens_pair = lax.ppermute(tokens, "local", swap)
    chosen_pair = lax.ppermute(chosen, "local", swap)
    cotangent_pair = lax.ppermute(cotangent, "local", swap)

    far = [pltpu.with_memory_space_constraint(a, pltpu.HBM) for a in (tokens, w1_codes[0], w1_scales[0])]
    near = [shape(pairs * stride, count, BF16)] * 2 + [shape(count, features, BF16)]
    first, second, tokens, *weights = call(
        functools.partial(prep_body, dims, stride),
        near + [shape(mine, w, BF16) for w in gathered],
        pos,
        [chosen, chosen_pair] + far,
        [
            pltpu.VMEM((mine, hidden), BF16),
            pltpu.VMEM((shard // QB, hidden), BF16),
            pltpu.VMEM((shard // QB, hidden), F32),
            pltpu.SemaphoreType.DMA((3,)),
        ],
        space=[pltpu.VMEM] * 2 + [pltpu.HBM] * 3,
    )
    picks = [first, second]
    order = node_order(nodes)
    held = []
    for chunk in weights:
        got = {0: chunk}
        for s in order:
            got[s] = lax.ppermute(chunk, "node", [(a, mate(a, s, nodes)) for a in range(nodes)])
        held.append([got[s] for s in range(nodes)])

    def route(columns, rows, rows_pair):
        pieces = call(
            functools.partial(route_body, dims, stride, columns),
            [shape(sent_rows, part // len(columns), BF16)] * (len(columns) * copies * pairs),
            pos,
            [*picks, rows, rows_pair],
            flops=4 * pairs * stride * count * features,
        )
        step = copies * pairs
        return [pieces[g * step : (g + 1) * step] for g in range(len(columns))]

    (pieces_x,) = route(columns_x, tokens, tokens_pair)
    pieces_y = route(columns_y, cotangent, cotangent_pair)

    def exchange(pieces):
        moved = list(pieces)
        for j, k in slots_of(copies, pairs):
            links = [
                (a * locals_ + b, mate(a, j, copies) * locals_ + 2 * mate(b // 2, k, pairs) + b % 2)
                for a in range(copies)
                for b in range(locals_)
            ]
            at = j * pairs + k
            moved[at] = lax.ppermute(pieces[at], ("dp", "local"), links)
        return moved

    rows_x = exchange(pieces_x)
    turned = []
    for h, pieces in enumerate(pieces_y):
        cols = part // len(pieces_y)
        got_dy = exchange(pieces)
        turned += call(
            functools.partial(turn_body, dims, stride),
            [shape(cols, everyone, BF16)],
            pos,
            got_dy,
            [pltpu.VMEM((everyone, cols), BF16)],
        )
    factor = float(count * copies * nodes) ** (-0.5)
    groups = []
    for i, split in enumerate(SPLITS):
        widths = [unit * share for share in split]
        joined = [shape(everyone, part, BF16)] if len(rows_x) > 1 else []
        parts = call(
            functools.partial(up_body, dims, stride, len(rows_x)),
            joined + [shape(everyone, w, kind) for w in widths for kind in (F32, BF16)],
            pos,
            list(rows_x) + held[i],
            [pltpu.VMEM((part, gathered[i]), BF16)],
            flops=2 * everyone * part * gathered[i],
        )
        if joined:
            rows_x, parts = parts[:1], parts[1:]
        groups += list(zip(widths, parts[::2], parts[1::2]))
    acts = []
    for wide, kept, sent in groups:
        if copies == 2:
            acts.append([kept, lax.ppermute(sent, "dp", [(0, 1), (1, 0)])])
        else:
            acts.append([lax.psum(kept, "dp")])
    owns, arrived = {}, {}
    for n, (chunks, targets) in enumerate(jobs):
        wide = sum(groups[i][0] for i in chunks)
        tables = [h for h, half in enumerate(halves) if set(half) & set(targets)]
        spots = []
        for s in targets:
            (h,) = [h for h in tables if s in halves[h]]
            spots.append((s, tables.index(h), halves[h].index(s) if aligned else -1))
        again = [any(i in other for other, _ in jobs[n + 1 :]) for i in chunks]
        emits = [more and acts[i][0].dtype == F32 for i, more in zip(chunks, again)]
        kinds = [shape(mine, wide, BF16 if s else F32) for s in targets]
        kinds += [shape(everyone, groups[i][0], BF16) for i, emit in zip(chunks, emits) if emit]
        terms = call(
            functools.partial(down_body, dims, factor, spots, [len(acts[i]) for i in chunks], emits),
            kinds,
            pos,
            [turned[h] for h in tables] + sum((acts[i] for i in chunks), []),
            [pltpu.VMEM((everyone, wide), BF16)],
            flops=2 * everyone * len(targets) * mine * wide,
        )
        extra = list(terms[len(targets) :])
        for i, emit in zip(chunks, emits):
            if emit:
                acts[i] = [extra.pop(0)]
        (group,) = [g for g, members in enumerate(outputs) if chunks[0] in members]
        begin = sum(groups[i][0] for i in outputs[group] if i < chunks[0])
        for s, term in zip(targets, terms):
            if s == 0:
                owns[group] = term
                continue
            links = [(a, mate(a, s, nodes)) for a in range(nodes)]
            moved = lax.ppermute(term, "node", links)
            arrived.setdefault(group, []).append((begin, moved))
    finished = []
    for i in range(len(outputs)):
        wide = owns[i].shape[1]
        begins = [begin for begin, _ in arrived[i]]
        (summed,) = call(
            functools.partial(sum_body, begins),
            [shape(mine, wide, BF16)],
            pos,
            [owns[i]] + [moved for _, moved in arrived[i]],
            [pltpu.VMEM((mine, wide), F32)],
        )
        finished.append(summed)
        for j in range(1, copies):
            links = [(a, mate(a, j, copies)) for a in range(copies)]
            finished.append(lax.ppermute(summed, "dp", links))
    spots = []
    begin = 0
    for i in range(len(outputs)):
        spots += [(j, begin) for j in range(copies)]
        begin += owns[i].shape[1]
    items = list(zip(finished, spots))
    sure = copies * max(0, len(outputs) - 2)
    soon = [item for i, item in enumerate(items) if i < sure or item[1][0] == 0]
    late = [item for i, item in enumerate(items) if i >= sure and item[1][0] > 0]
    (result,) = call(
        functools.partial(lay_body, dims, [spot for _, spot in soon]),
        [shape(shard, hidden, BF16)],
        pos,
        [value for value, _ in soon],
        [pltpu.SemaphoreType.DMA((len(soon),))],
        target=pltpu.HBM,
    )
    (result,) = call(
        functools.partial(lay_body, dims, [spot for _, spot in late]),
        [shape(shard, hidden, BF16)],
        pos,
        [value for value, _ in late] + [result],
        [pltpu.SemaphoreType.DMA((len(late),))],
        space=[pltpu.VMEM] * len(late) + [pltpu.HBM],
        target=pltpu.HBM,
        aliases={len(late) + 1: 0},
    )
    return result[None]


def solution(mesh):
    rows = P(("dp", "node", "local"), None)
    weights = P("local", "node", None)
    return jax.shard_map(
        on_device,
        mesh=mesh,
        in_specs=(rows, rows, rows, weights, weights),
        out_specs=weights,
        check_vma=False,
    )
```

```python
import functools
import jax
import jax.numpy as jnp
from jax import lax
from jax.experimental import pallas as pl
from jax.experimental.pallas import tpu as pltpu
from jax.sharding import PartitionSpec as P

QB = 32
SPLITS = ((2,), (1, 1))
F32 = jnp.float32
BF16 = jnp.bfloat16


def mate(i, k, size):
    return i ^ k if size & (size - 1) == 0 else (i + k) % size


def traced_mate(i, k, size):
    return lax.bitwise_xor(i, jnp.int32(k)) if size & (size - 1) == 0 else lax.rem(i + k, size)


def traced_origin(i, k, size):
    if size & (size - 1) == 0:
        return lax.bitwise_xor(i, jnp.int32(k))
    return lax.rem(i + (size - k), size)


def call(body, outs, args, scratch=(), flops=0, space=pltpu.VMEM, target=pltpu.VMEM, aliases=None):
    moved = sum(a.size * a.dtype.itemsize for a in args)
    moved += sum(o.size * o.dtype.itemsize for o in outs)
    spaces = space if isinstance(space, list) else [space] * len(args)
    room = 2 * moved + (8 << 20)

    def kernel(*refs):
        body([lax.axis_index(name) for name in ("dp", "node", "local")], *refs)

    return pl.pallas_call(
        kernel,
        out_shape=outs,
        in_specs=[pl.BlockSpec(memory_space=kind) for kind in spaces],
        out_specs=[pl.BlockSpec(memory_space=target)] * len(outs),
        scratch_shapes=list(scratch),
        input_output_aliases=aliases or {},
        compiler_params=pltpu.CompilerParams(vmem_limit_bytes=min(room, 60 << 20)),
        cost_estimate=pl.CostEstimate(flops=flops, bytes_accessed=moved, transcendentals=0),
    )(*args)


def node_order(nodes):
    return [s for s in (3, 1, 2) if s < nodes] + list(range(4, nodes))


def plan_of(nodes, aligned):
    order = node_order(nodes)
    every = order + [0]
    chunks = sum(len(split) for split in SPLITS)
    if not aligned:
        return [every], [([i], every) for i in range(chunks)], [[i] for i in range(chunks)]
    early, late = order[: nodes // 2], order[nodes // 2 :] + [0]
    jobs = [([0], early), ([0], late)] + [([i], every) for i in range(1, chunks)]
    return [early, late], jobs, [[i] for i in range(chunks)]


def slots_of(copies, pairs):
    slots = [(j, k) for k in range(pairs) for j in range(copies) if j or k]
    return sorted(slots, key=lambda slot: -(slot[0] > 0) - (slot[1] > 0))


def shape(rows, cols, dtype):
    return jax.ShapeDtypeStruct((rows, cols), dtype)


def prep_body(dims, stride, pos, ids, ids_pair, rows, codes, scales, *refs):
    picks, near, outs = refs[:2], refs[2], refs[3:-4]
    raw, steps, wide, sems = refs[-4:]
    mine, ff = raw.shape
    at = pl.multiple_of(pos[0] * mine, 16)
    moves = [
        pltpu.make_async_copy(scales, steps, sems.at[0]),
        pltpu.make_async_copy(codes.at[pl.ds(at, mine), :], raw, sems.at[1]),
        pltpu.make_async_copy(rows, near, sems.at[2]),
    ]
    for move in moves:
        move.start()
    select_body(dims, stride, pos, ids, ids_pair, *picks)
    moves[0].wait()
    wide[...] = steps[...].astype(F32)
    used = max(1, mine // QB)
    begin = lax.div(pos[0] * mine, jnp.int32(QB))
    if used % 8 == 0:
        begin = pl.multiple_of(begin, 8)
    factors = wide[pl.ds(begin, used), :]
    moves[1].wait()
    blocks = raw[...].astype(F32).reshape(used, mine // used, ff)
    kept = (blocks * factors[:, None, :]).astype(BF16).reshape(mine, ff)
    begin = 0
    for out in outs:
        end = begin + out.shape[1]
        out[...] = kept[:, begin:end]
        begin = end
    moves[2].wait()


def select_body(dims, stride, pos, ids, ids_pair, *picks):
    _, _, locals_ = dims
    pairs = locals_ // 2
    count = ids.shape[1]
    high = max(16, pairs)
    first = lax.broadcasted_iota(jnp.int32, (count, count), 0)
    second = lax.broadcasted_iota(jnp.int32, (count, count), 1)
    earlier = (first < second).astype(F32).astype(BF16)
    places = lax.broadcasted_iota(jnp.int32, (pairs * stride, count), 0)
    owner = lax.shift_right_logical(pos[2], 1)
    held = jnp.zeros((high, 1), F32)
    for chosen, pick in zip((ids[...], ids_pair[...]), picks):
        group = lax.shift_right_logical(chosen, 1)
        if pairs & (pairs - 1) == 0:
            relative = lax.bitwise_xor(group, owner)
        else:
            relative = lax.rem(group - owner + pairs, pairs)
        mine = lax.bitwise_and(chosen, 1) == lax.bitwise_and(pos[2], 1)
        relative = jnp.where(mine, relative, high)
        onehot = relative == lax.broadcasted_iota(jnp.int32, (high, count), 0)
        marks = onehot.astype(F32)
        ranks = held + jnp.dot(marks.astype(BF16), earlier, preferred_element_type=F32)
        rank = jnp.sum(jnp.where(onehot, ranks, 0.0), axis=0, keepdims=True)
        slot = jnp.where(mine, relative * stride + rank.astype(jnp.int32), -1)
        pick[...] = (slot == places).astype(F32).astype(BF16)
        held = held + jnp.sum(marks, axis=1, keepdims=True)


def place_rows(dims, stride, columns, pos, picks, sources, outs):
    copies, nodes, locals_ = dims
    pairs = locals_ // 2
    rows, width = outs[0].shape[0], outs[0].shape[1] // len(columns[0])
    for g, group in enumerate(columns):
        for j in reversed(range(copies)):
            which = traced_mate(pos[0], j, copies)
            for b, (relative, block) in enumerate(group):
                if relative:
                    block = traced_mate(pos[1], block, nodes)
                at = pl.multiple_of((block * copies + which) * width, 128)
                got = sum(
                    jnp.dot(pick[...], source[:, pl.ds(at, width)], preferred_element_type=F32)
                    for pick, source in zip(picks, sources)
                ).astype(BF16)
                for k in range(pairs):
                    out = outs[(g * copies + j) * pairs + k]
                    out[:, b * width : (b + 1) * width] = got[k * stride : k * stride + rows]


def route_body(dims, stride, columns, pos, pick, pick_pair, rows, rows_pair, *outs):
    place_rows(dims, stride, columns, pos, (pick, pick_pair), (rows, rows_pair), outs)


def join_body(dims, stride, pos, *refs):
    copies, _, locals_ = dims
    pairs = locals_ // 2
    pieces, out = refs[:-1], refs[-1]
    rows, width = pieces[0].shape
    for j in range(copies):
        base = traced_origin(pos[0], j, copies) * (pairs * stride)
        for k in range(pairs):
            at = pl.multiple_of(base + k * stride, 16)
            block = pieces[j * pairs + k][...]
            if rows < stride:
                blank = jnp.zeros((stride - rows, width), block.dtype)
                block = jnp.concatenate([block, blank], axis=0)
            out[pl.ds(at, stride), :] = block


def turn_body(dims, stride, pos, *refs):
    pieces, out, held = refs[:-2], refs[-2], refs[-1]
    join_body(dims, stride, pos, *pieces, held)
    out[...] = jnp.transpose(held[...])


def up_body(dims, stride, given, pos, *refs):
    nodes = dims[1]
    pieces, weights, held = refs[:given], refs[given : given + nodes], refs[-1]
    outs = refs[given + nodes : -1]
    rows = pieces[0]
    if given > 1:
        rows, outs = outs[0], outs[1:]
        join_body(dims, stride, pos, *pieces, rows)
    mine = weights[0].shape[0]
    for s in range(nodes):
        at = pl.multiple_of(traced_origin(pos[1], s, nodes) * mine, 16)
        held[pl.ds(at, mine), :] = weights[s][...]
    begin = 0
    for kept, sent in zip(outs[::2], outs[1::2]):
        end = begin + kept.shape[1]
        pre = jnp.dot(rows[...], held[:, begin:end], preferred_element_type=F32)
        kept[...] = pre
        sent[...] = pre.astype(BF16)
        begin = end


def down_body(dims, factor, spots, sources, emits, pos, *refs):
    nodes = dims[1]
    tables = 1 + max(table for _, table, _ in spots)
    turned, rest, act = refs[:tables], list(refs[tables:-1]), refs[-1]
    begin = 0
    used = sum(sources)
    outs, kept_acts = rest[used : used + len(spots)], rest[used + len(spots) :]
    for held, emit in zip(sources, emits):
        if held and rest[0].dtype == F32:
            pre = rest[0][...]
            for part in rest[1:held]:
                pre = pre + part[...].astype(F32)
            value = (pre * jax.nn.sigmoid(pre)).astype(BF16)
        else:
            value = rest[0][...]
        rest = rest[held:]
        end = begin + value.shape[1]
        act[:, begin:end] = value
        if emit:
            kept_acts[0][...] = value
            kept_acts = kept_acts[1:]
        begin = end
    mine = outs[0].shape[0]
    for (s, table, place), out in zip(spots, outs):
        at = place * mine
        if place < 0:
            at = pl.multiple_of(traced_mate(pos[1], s, nodes) * mine, 16)
        term = jnp.dot(turned[table][pl.ds(at, mine), :], act[...], preferred_element_type=F32)
        out[...] = (term * factor).astype(out.dtype)


def sum_body(begins, pos, own, *refs):
    total, out = refs[-1], refs[-2]
    total[...] = own[...]
    for begin, part in zip(begins, refs[:-2]):
        end = begin + part.shape[1]
        total[:, begin:end] += part[...].astype(F32)
    out[...] = total[...].astype(BF16)


def lay_body(dims, spots, pos, *refs):
    copies = dims[0]
    parts, out, sems = refs[: len(spots)], refs[-2], refs[-1]
    moves = []
    for i, (part, (j, begin)) in enumerate(zip(parts, spots)):
        mine, width = part.shape
        at = pl.multiple_of(traced_origin(pos[0], j, copies) * mine, 16)
        spot = out.at[pl.ds(at, mine), pl.ds(begin, width)]
        moves.append(pltpu.make_async_copy(part, spot, sems.at[i]))
    for move in moves:
        move.start()
    for move in moves:
        move.wait()


def on_device(tokens, cotangent, expert_of, w1_codes, w1_scales):
    copies, nodes, locals_ = (lax.axis_size(a) for a in ("dp", "node", "local"))
    dims = (copies, nodes, locals_)
    count, features = tokens.shape
    capacity = 5 * count // (4 * locals_)
    pairs = locals_ // 2
    sent_rows = -(-2 * capacity // 8) * 8
    stride = -(-sent_rows // 16) * 16
    shard, hidden = w1_codes.shape[1:]
    mine = shard // copies
    part = features // copies
    unit = hidden // sum(sum(split) for split in SPLITS)
    gathered = [unit * sum(split) for split in SPLITS]
    everyone = copies * pairs * stride

    aligned = mine % 128 == 0
    halves, jobs, outputs = plan_of(nodes, aligned)
    if aligned:
        columns_x = [[(False, b) for b in range(nodes)]]
        columns_y = [[(True, s) for s in half] for half in halves]
    else:
        columns_x = columns_y = [[(False, 0)]]
        tokens, cotangent = (
            a.reshape(count, nodes, copies, mine).swapaxes(1, 2).reshape(count, features)
            for a in (tokens, cotangent)
        )
    chosen = expert_of.reshape(1, count)
    swap = [(i, i ^ 1) for i in range(locals_)]
    tokens_pair = lax.ppermute(tokens, "local", swap)
    chosen_pair = lax.ppermute(chosen, "local", swap)
    cotangent_pair = lax.ppermute(cotangent, "local", swap)

    far = [pltpu.with_memory_space_constraint(a, pltpu.HBM) for a in (tokens, w1_codes[0], w1_scales[0])]
    near = [shape(pairs * stride, count, BF16)] * 2 + [shape(count, features, BF16)]
    first, second, tokens, *weights = call(
        functools.partial(prep_body, dims, stride),
        near + [shape(mine, w, BF16) for w in gathered],
        [chosen, chosen_pair] + far,
        [
            pltpu.VMEM((mine, hidden), BF16),
            pltpu.VMEM((shard // QB, hidden), BF16),
            pltpu.VMEM((shard // QB, hidden), F32),
            pltpu.SemaphoreType.DMA((3,)),
        ],
        space=[pltpu.VMEM] * 2 + [pltpu.HBM] * 3,
    )
    picks = [first, second]
    order = node_order(nodes)
    held = []
    for chunk in weights:
        got = {0: chunk}
        for s in order:
            got[s] = lax.ppermute(chunk, "node", [(a, mate(a, s, nodes)) for a in range(nodes)])
        held.append([got[s] for s in range(nodes)])

    def route(columns, rows, rows_pair):
        pieces = call(
            functools.partial(route_body, dims, stride, columns),
            [shape(sent_rows, part // len(columns), BF16)] * (len(columns) * copies * pairs),
            [*picks, rows, rows_pair],
            flops=4 * pairs * stride * count * features,
        )
        step = copies * pairs
        return [pieces[g * step : (g + 1) * step] for g in range(len(columns))]

    (pieces_x,) = route(columns_x, tokens, tokens_pair)
    pieces_y = route(columns_y, cotangent, cotangent_pair)

    def exchange(pieces):
        moved = list(pieces)
        for j, k in slots_of(copies, pairs):
            links = [
                (a * locals_ + b, mate(a, j, copies) * locals_ + 2 * mate(b // 2, k, pairs) + b % 2)
                for a in range(copies)
                for b in range(locals_)
            ]
            at = j * pairs + k
            moved[at] = lax.ppermute(pieces[at], ("dp", "local"), links)
        return moved

    rows_x = exchange(pieces_x)
    turned = []
    for h, pieces in enumerate(pieces_y):
        cols = part // len(pieces_y)
        got_dy = exchange(pieces)
        turned += call(
            functools.partial(turn_body, dims, stride),
            [shape(cols, everyone, BF16)],
            got_dy,
            [pltpu.VMEM((everyone, cols), BF16)],
        )
    factor = float(count * copies * nodes) ** (-0.5)
    groups = []
    for i, split in enumerate(SPLITS):
        widths = [unit * share for share in split]
        joined = [shape(everyone, part, BF16)] if len(rows_x) > 1 else []
        parts = call(
            functools.partial(up_body, dims, stride, len(rows_x)),
            joined + [shape(everyone, w, kind) for w in widths for kind in (F32, BF16)],
            list(rows_x) + held[i],
            [pltpu.VMEM((part, gathered[i]), BF16)],
            flops=2 * everyone * part * gathered[i],
        )
        if joined:
            rows_x, parts = parts[:1], parts[1:]
        groups += list(zip(widths, parts[::2], parts[1::2]))
    acts = []
    for wide, kept, sent in groups:
        if copies == 2:
            acts.append([kept, lax.ppermute(sent, "dp", [(0, 1), (1, 0)])])
        else:
            acts.append([lax.psum(kept, "dp")])
    owns, arrived = {}, {}
    for n, (chunks, targets) in enumerate(jobs):
        wide = sum(groups[i][0] for i in chunks)
        tables = [h for h, half in enumerate(halves) if set(half) & set(targets)]
        spots = []
        for s in targets:
            (h,) = [h for h in tables if s in halves[h]]
            spots.append((s, tables.index(h), halves[h].index(s) if aligned else -1))
        again = [any(i in other for other, _ in jobs[n + 1 :]) for i in chunks]
        emits = [more and acts[i][0].dtype == F32 for i, more in zip(chunks, again)]
        kinds = [shape(mine, wide, BF16 if s else F32) for s in targets]
        kinds += [shape(everyone, groups[i][0], BF16) for i, emit in zip(chunks, emits) if emit]
        terms = call(
            functools.partial(down_body, dims, factor, spots, [len(acts[i]) for i in chunks], emits),
            kinds,
            [turned[h] for h in tables] + sum((acts[i] for i in chunks), []),
            [pltpu.VMEM((everyone, wide), BF16)],
            flops=2 * everyone * len(targets) * mine * wide,
        )
        extra = list(terms[len(targets) :])
        for i, emit in zip(chunks, emits):
            if emit:
                acts[i] = [extra.pop(0)]
        (group,) = [g for g, members in enumerate(outputs) if chunks[0] in members]
        begin = sum(groups[i][0] for i in outputs[group] if i < chunks[0])
        for s, term in zip(targets, terms):
            if s == 0:
                owns[group] = term
                continue
            links = [(a, mate(a, s, nodes)) for a in range(nodes)]
            moved = lax.ppermute(term, "node", links)
            arrived.setdefault(group, []).append((begin, moved))
    finished = []
    for i in range(len(outputs)):
        wide = owns[i].shape[1]
        begins = [begin for begin, _ in arrived[i]]
        (summed,) = call(
            functools.partial(sum_body, begins),
            [shape(mine, wide, BF16)],
            [owns[i]] + [moved for _, moved in arrived[i]],
            [pltpu.VMEM((mine, wide), F32)],
        )
        finished.append(summed)
        for j in range(1, copies):
            links = [(a, mate(a, j, copies)) for a in range(copies)]
            finished.append(lax.ppermute(summed, "dp", links))
    spots = []
    begin = 0
    for i in range(len(outputs)):
        spots += [(j, begin) for j in range(copies)]
        begin += owns[i].shape[1]
    items = list(zip(finished, spots))
    sure = copies * max(0, len(outputs) - 2)
    soon = [item for i, item in enumerate(items) if i < sure or item[1][0] == 0]
    late = [item for i, item in enumerate(items) if i >= sure and item[1][0] > 0]
    (result,) = call(
        functools.partial(lay_body, dims, [spot for _, spot in soon]),
        [shape(shard, hidden, BF16)],
        [value for value, _ in soon],
        [pltpu.SemaphoreType.DMA((len(soon),))],
        target=pltpu.HBM,
    )
    (result,) = call(
        functools.partial(lay_body, dims, [spot for _, spot in late]),
        [shape(shard, hidden, BF16)],
        [value for value, _ in late] + [result],
        [pltpu.SemaphoreType.DMA((len(late),))],
        space=[pltpu.VMEM] * len(late) + [pltpu.HBM],
        target=pltpu.HBM,
        aliases={len(late): 0},
    )
    return result[None]


def solution(mesh):
    rows = P(("dp", "node", "local"), None)
    weights = P("local", "node", None)
    return jax.shard_map(
        on_device,
        mesh=mesh,
        in_specs=(rows, rows, rows, weights, weights),
        out_specs=weights,
        check_vma=False,
    )
```

```python
import functools
import jax
import jax.numpy as jnp
from jax import lax
from jax.experimental import pallas as pl
from jax.experimental.pallas import tpu as pltpu
from jax.sharding import PartitionSpec as P

QB = 32
SPLITS = ((1, 1), (1, 1))
F32 = jnp.float32
BF16 = jnp.bfloat16


def mate(i, k, size):
    return i ^ k if size & (size - 1) == 0 else (i + k) % size


def traced_mate(i, k, size):
    return lax.bitwise_xor(i, jnp.int32(k)) if size & (size - 1) == 0 else lax.rem(i + k, size)


def traced_origin(i, k, size):
    if size & (size - 1) == 0:
        return lax.bitwise_xor(i, jnp.int32(k))
    return lax.rem(i + (size - k), size)


def call(body, outs, args, scratch=(), flops=0, space=pltpu.VMEM, target=pltpu.VMEM, aliases=None):
    moved = sum(a.size * a.dtype.itemsize for a in args)
    moved += sum(o.size * o.dtype.itemsize for o in outs)
    spaces = space if isinstance(space, list) else [space] * len(args)
    room = 2 * moved + (8 << 20)

    def kernel(*refs):
        body([lax.axis_index(name) for name in ("dp", "node", "local")], *refs)

    return pl.pallas_call(
        kernel,
        out_shape=outs,
        in_specs=[pl.BlockSpec(memory_space=kind) for kind in spaces],
        out_specs=[pl.BlockSpec(memory_space=target)] * len(outs),
        scratch_shapes=list(scratch),
        input_output_aliases=aliases or {},
        compiler_params=pltpu.CompilerParams(vmem_limit_bytes=min(room, 60 << 20)),
        cost_estimate=pl.CostEstimate(flops=flops, bytes_accessed=moved, transcendentals=0),
    )(*args)


def node_order(nodes):
    return [s for s in (3, 1, 2) if s < nodes] + list(range(4, nodes))


def plan_of(nodes, aligned):
    order = node_order(nodes)
    every = order + [0]
    chunks = sum(len(split) for split in SPLITS)
    if not aligned:
        return [every], [([i], every) for i in range(chunks)], [[i] for i in range(chunks)]
    early, late = order[: nodes // 2], order[nodes // 2 :] + [0]
    jobs = [([0], early), ([1], early), ([0, 1], late)]
    jobs += [([i], every) for i in range(2, chunks)]
    return [early, late], jobs, [[0, 1]] + [[i] for i in range(2, chunks)]


def slots_of(copies, pairs):
    slots = [(j, k) for k in range(pairs) for j in range(copies) if j or k]
    return sorted(slots, key=lambda slot: -(slot[0] > 0) - (slot[1] > 0))


def shape(rows, cols, dtype):
    return jax.ShapeDtypeStruct((rows, cols), dtype)


def prep_body(dims, stride, pos, ids, ids_pair, rows, codes, scales, *refs):
    picks, near, outs = refs[:2], refs[2], refs[3:-4]
    raw, steps, wide, sems = refs[-4:]
    mine, ff = raw.shape
    at = pl.multiple_of(pos[0] * mine, 16)
    moves = [
        pltpu.make_async_copy(scales, steps, sems.at[0]),
        pltpu.make_async_copy(codes.at[pl.ds(at, mine), :], raw, sems.at[1]),
        pltpu.make_async_copy(rows, near, sems.at[2]),
    ]
    for move in moves:
        move.start()
    select_body(dims, stride, pos, ids, ids_pair, *picks)
    moves[0].wait()
    wide[...] = steps[...].astype(F32)
    used = max(1, mine // QB)
    begin = lax.div(pos[0] * mine, jnp.int32(QB))
    if used % 8 == 0:
        begin = pl.multiple_of(begin, 8)
    factors = wide[pl.ds(begin, used), :]
    moves[1].wait()
    blocks = raw[...].astype(F32).reshape(used, mine // used, ff)
    kept = (blocks * factors[:, None, :]).astype(BF16).reshape(mine, ff)
    begin = 0
    for out in outs:
        end = begin + out.shape[1]
        out[...] = kept[:, begin:end]
        begin = end
    moves[2].wait()


def select_body(dims, stride, pos, ids, ids_pair, *picks):
    _, _, locals_ = dims
    pairs = locals_ // 2
    count = ids.shape[1]
    high = max(16, pairs)
    first = lax.broadcasted_iota(jnp.int32, (count, count), 0)
    second = lax.broadcasted_iota(jnp.int32, (count, count), 1)
    earlier = (first < second).astype(F32).astype(BF16)
    places = lax.broadcasted_iota(jnp.int32, (pairs * stride, count), 0)
    owner = lax.shift_right_logical(pos[2], 1)
    held = jnp.zeros((high, 1), F32)
    for chosen, pick in zip((ids[...], ids_pair[...]), picks):
        group = lax.shift_right_logical(chosen, 1)
        if pairs & (pairs - 1) == 0:
            relative = lax.bitwise_xor(group, owner)
        else:
            relative = lax.rem(group - owner + pairs, pairs)
        mine = lax.bitwise_and(chosen, 1) == lax.bitwise_and(pos[2], 1)
        relative = jnp.where(mine, relative, high)
        onehot = relative == lax.broadcasted_iota(jnp.int32, (high, count), 0)
        marks = onehot.astype(F32)
        ranks = held + jnp.dot(marks.astype(BF16), earlier, preferred_element_type=F32)
        rank = jnp.sum(jnp.where(onehot, ranks, 0.0), axis=0, keepdims=True)
        slot = jnp.where(mine, relative * stride + rank.astype(jnp.int32), -1)
        pick[...] = (slot == places).astype(F32).astype(BF16)
        held = held + jnp.sum(marks, axis=1, keepdims=True)


def place_rows(dims, stride, columns, pos, picks, sources, outs):
    copies, nodes, locals_ = dims
    pairs = locals_ // 2
    rows, width = outs[0].shape[0], outs[0].shape[1] // len(columns[0])
    for g, group in enumerate(columns):
        for j in reversed(range(copies)):
            which = traced_mate(pos[0], j, copies)
            for b, (relative, block) in enumerate(group):
                if relative:
                    block = traced_mate(pos[1], block, nodes)
                at = pl.multiple_of((block * copies + which) * width, 128)
                got = sum(
                    jnp.dot(pick[...], source[:, pl.ds(at, width)], preferred_element_type=F32)
                    for pick, source in zip(picks, sources)
                ).astype(BF16)
                for k in range(pairs):
                    out = outs[(g * copies + j) * pairs + k]
                    out[:, b * width : (b + 1) * width] = got[k * stride : k * stride + rows]


def route_body(dims, stride, columns, pos, pick, pick_pair, rows, rows_pair, *outs):
    place_rows(dims, stride, columns, pos, (pick, pick_pair), (rows, rows_pair), outs)


def join_body(dims, stride, pos, *refs):
    copies, _, locals_ = dims
    pairs = locals_ // 2
    pieces, out = refs[:-1], refs[-1]
    rows, width = pieces[0].shape
    for j in range(copies):
        base = traced_origin(pos[0], j, copies) * (pairs * stride)
        for k in range(pairs):
            at = pl.multiple_of(base + k * stride, 16)
            block = pieces[j * pairs + k][...]
            if rows < stride:
                blank = jnp.zeros((stride - rows, width), block.dtype)
                block = jnp.concatenate([block, blank], axis=0)
            out[pl.ds(at, stride), :] = block


def turn_body(dims, stride, pos, *refs):
    pieces, out, held = refs[:-2], refs[-2], refs[-1]
    join_body(dims, stride, pos, *pieces, held)
    out[...] = jnp.transpose(held[...])


def up_body(dims, stride, given, pos, *refs):
    nodes = dims[1]
    pieces, weights, held = refs[:given], refs[given : given + nodes], refs[-1]
    outs = refs[given + nodes : -1]
    rows = pieces[0]
    if given > 1:
        rows, outs = outs[0], outs[1:]
        join_body(dims, stride, pos, *pieces, rows)
    mine = weights[0].shape[0]
    for s in range(nodes):
        at = pl.multiple_of(traced_origin(pos[1], s, nodes) * mine, 16)
        held[pl.ds(at, mine), :] = weights[s][...]
    begin = 0
    for kept, sent in zip(outs[::2], outs[1::2]):
        end = begin + kept.shape[1]
        pre = jnp.dot(rows[...], held[:, begin:end], preferred_element_type=F32)
        kept[...] = pre
        sent[...] = pre.astype(BF16)
        begin = end


def down_body(dims, factor, spots, sources, emits, pos, *refs):
    nodes = dims[1]
    tables = 1 + max(table for _, table, _ in spots)
    turned, rest, act = refs[:tables], list(refs[tables:-1]), refs[-1]
    begin = 0
    used = sum(sources)
    outs, kept_acts = rest[used : used + len(spots)], rest[used + len(spots) :]
    for held, emit in zip(sources, emits):
        if held and rest[0].dtype == F32:
            pre = rest[0][...]
            for part in rest[1:held]:
                pre = pre + part[...].astype(F32)
            value = (pre * jax.nn.sigmoid(pre)).astype(BF16)
        else:
            value = rest[0][...]
        rest = rest[held:]
        end = begin + value.shape[1]
        act[:, begin:end] = value
        if emit:
            kept_acts[0][...] = value
            kept_acts = kept_acts[1:]
        begin = end
    mine = outs[0].shape[0]
    for (s, table, place), out in zip(spots, outs):
        at = place * mine
        if place < 0:
            at = pl.multiple_of(traced_mate(pos[1], s, nodes) * mine, 16)
        term = jnp.dot(turned[table][pl.ds(at, mine), :], act[...], preferred_element_type=F32)
        out[...] = (term * factor).astype(out.dtype)


def sum_body(begins, pos, own, *refs):
    total, out = refs[-1], refs[-2]
    total[...] = own[...]
    for begin, part in zip(begins, refs[:-2]):
        end = begin + part.shape[1]
        total[:, begin:end] += part[...].astype(F32)
    out[...] = total[...].astype(BF16)


def lay_body(dims, spots, pos, *refs):
    copies = dims[0]
    parts, out, sems = refs[: len(spots)], refs[-2], refs[-1]
    moves = []
    for i, (part, (j, begin)) in enumerate(zip(parts, spots)):
        mine, width = part.shape
        at = pl.multiple_of(traced_origin(pos[0], j, copies) * mine, 16)
        spot = out.at[pl.ds(at, mine), pl.ds(begin, width)]
        moves.append(pltpu.make_async_copy(part, spot, sems.at[i]))
    for move in moves:
        move.start()
    for move in moves:
        move.wait()


def on_device(tokens, cotangent, expert_of, w1_codes, w1_scales):
    copies, nodes, locals_ = (lax.axis_size(a) for a in ("dp", "node", "local"))
    dims = (copies, nodes, locals_)
    count, features = tokens.shape
    capacity = 5 * count // (4 * locals_)
    pairs = locals_ // 2
    sent_rows = -(-2 * capacity // 8) * 8
    stride = -(-sent_rows // 16) * 16
    shard, hidden = w1_codes.shape[1:]
    mine = shard // copies
    part = features // copies
    unit = hidden // sum(sum(split) for split in SPLITS)
    gathered = [unit * sum(split) for split in SPLITS]
    everyone = copies * pairs * stride

    aligned = mine % 128 == 0
    halves, jobs, outputs = plan_of(nodes, aligned)
    if aligned:
        columns_x = [[(False, b) for b in range(nodes)]]
        columns_y = [[(True, s) for s in half] for half in halves]
    else:
        columns_x = columns_y = [[(False, 0)]]
        tokens, cotangent = (
            a.reshape(count, nodes, copies, mine).swapaxes(1, 2).reshape(count, features)
            for a in (tokens, cotangent)
        )
    chosen = expert_of.reshape(1, count)
    swap = [(i, i ^ 1) for i in range(locals_)]
    tokens_pair = lax.ppermute(tokens, "local", swap)
    chosen_pair = lax.ppermute(chosen, "local", swap)
    cotangent_pair = lax.ppermute(cotangent, "local", swap)

    far = [pltpu.with_memory_space_constraint(a, pltpu.HBM) for a in (tokens, w1_codes[0], w1_scales[0])]
    near = [shape(pairs * stride, count, BF16)] * 2 + [shape(count, features, BF16)]
    first, second, tokens, *weights = call(
        functools.partial(prep_body, dims, stride),
        near + [shape(mine, w, BF16) for w in gathered],
        [chosen, chosen_pair] + far,
        [
            pltpu.VMEM((mine, hidden), BF16),
            pltpu.VMEM((shard // QB, hidden), BF16),
            pltpu.VMEM((shard // QB, hidden), F32),
            pltpu.SemaphoreType.DMA((3,)),
        ],
        space=[pltpu.VMEM] * 2 + [pltpu.HBM] * 3,
    )
    picks = [first, second]
    order = node_order(nodes)
    held = []
    for chunk in weights:
        got = {0: chunk}
        for s in order:
            got[s] = lax.ppermute(chunk, "node", [(a, mate(a, s, nodes)) for a in range(nodes)])
        held.append([got[s] for s in range(nodes)])

    def route(columns, rows, rows_pair):
        pieces = call(
            functools.partial(route_body, dims, stride, columns),
            [shape(sent_rows, part // len(columns), BF16)] * (len(columns) * copies * pairs),
            [*picks, rows, rows_pair],
            flops=4 * pairs * stride * count * features,
        )
        step = copies * pairs
        return [pieces[g * step : (g + 1) * step] for g in range(len(columns))]

    (pieces_x,) = route(columns_x, tokens, tokens_pair)
    pieces_y = route(columns_y, cotangent, cotangent_pair)

    def exchange(pieces):
        moved = list(pieces)
        for j, k in slots_of(copies, pairs):
            links = [
                (a * locals_ + b, mate(a, j, copies) * locals_ + 2 * mate(b // 2, k, pairs) + b % 2)
                for a in range(copies)
                for b in range(locals_)
            ]
            at = j * pairs + k
            moved[at] = lax.ppermute(pieces[at], ("dp", "local"), links)
        return moved

    rows_x = exchange(pieces_x)
    turned = []
    for h, pieces in enumerate(pieces_y):
        cols = part // len(pieces_y)
        got_dy = exchange(pieces)
        turned += call(
            functools.partial(turn_body, dims, stride),
            [shape(cols, everyone, BF16)],
            got_dy,
            [pltpu.VMEM((everyone, cols), BF16)],
        )
    factor = float(count * copies * nodes) ** (-0.5)
    groups = []
    for i, split in enumerate(SPLITS):
        widths = [unit * share for share in split]
        joined = [shape(everyone, part, BF16)] if len(rows_x) > 1 else []
        parts = call(
            functools.partial(up_body, dims, stride, len(rows_x)),
            joined + [shape(everyone, w, kind) for w in widths for kind in (F32, BF16)],
            list(rows_x) + held[i],
            [pltpu.VMEM((part, gathered[i]), BF16)],
            flops=2 * everyone * part * gathered[i],
        )
        if joined:
            rows_x, parts = parts[:1], parts[1:]
        groups += list(zip(widths, parts[::2], parts[1::2]))
    acts = []
    for wide, kept, sent in groups:
        if copies == 2:
            acts.append([kept, lax.ppermute(sent, "dp", [(0, 1), (1, 0)])])
        else:
            acts.append([lax.psum(kept, "dp")])
    owns, arrived = {}, {}
    for n, (chunks, targets) in enumerate(jobs):
        wide = sum(groups[i][0] for i in chunks)
        tables = [h for h, half in enumerate(halves) if set(half) & set(targets)]
        spots = []
        for s in targets:
            (h,) = [h for h in tables if s in halves[h]]
            spots.append((s, tables.index(h), halves[h].index(s) if aligned else -1))
        again = [any(i in other for other, _ in jobs[n + 1 :]) for i in chunks]
        emits = [more and acts[i][0].dtype == F32 for i, more in zip(chunks, again)]
        kinds = [shape(mine, wide, BF16 if s else F32) for s in targets]
        kinds += [shape(everyone, groups[i][0], BF16) for i, emit in zip(chunks, emits) if emit]
        terms = call(
            functools.partial(down_body, dims, factor, spots, [len(acts[i]) for i in chunks], emits),
            kinds,
            [turned[h] for h in tables] + sum((acts[i] for i in chunks), []),
            [pltpu.VMEM((everyone, wide), BF16)],
            flops=2 * everyone * len(targets) * mine * wide,
        )
        extra = list(terms[len(targets) :])
        for i, emit in zip(chunks, emits):
            if emit:
                acts[i] = [extra.pop(0)]
        (group,) = [g for g, members in enumerate(outputs) if chunks[0] in members]
        begin = sum(groups[i][0] for i in outputs[group] if i < chunks[0])
        for s, term in zip(targets, terms):
            if s == 0:
                owns[group] = term
                continue
            links = [(a, mate(a, s, nodes)) for a in range(nodes)]
            moved = lax.ppermute(term, "node", links)
            arrived.setdefault(group, []).append((begin, moved))
    finished = []
    for i in range(len(outputs)):
        wide = owns[i].shape[1]
        begins = [begin for begin, _ in arrived[i]]
        (summed,) = call(
            functools.partial(sum_body, begins),
            [shape(mine, wide, BF16)],
            [owns[i]] + [moved for _, moved in arrived[i]],
            [pltpu.VMEM((mine, wide), F32)],
        )
        finished.append(summed)
        for j in range(1, copies):
            links = [(a, mate(a, j, copies)) for a in range(copies)]
            finished.append(lax.ppermute(summed, "dp", links))
    spots = []
    begin = 0
    for i in range(len(outputs)):
        spots += [(j, begin) for j in range(copies)]
        begin += owns[i].shape[1]
    items = list(zip(finished, spots))
    sure = copies * max(0, len(outputs) - 2)
    soon = [item for i, item in enumerate(items) if i < sure or item[1][0] == 0]
    late = [item for i, item in enumerate(items) if i >= sure and item[1][0] > 0]
    (result,) = call(
        functools.partial(lay_body, dims, [spot for _, spot in soon]),
        [shape(shard, hidden, BF16)],
        [value for value, _ in soon],
        [pltpu.SemaphoreType.DMA((len(soon),))],
        target=pltpu.HBM,
    )
    (result,) = call(
        functools.partial(lay_body, dims, [spot for _, spot in late]),
        [shape(shard, hidden, BF16)],
        [value for value, _ in late] + [result],
        [pltpu.SemaphoreType.DMA((len(late),))],
        space=[pltpu.VMEM] * len(late) + [pltpu.HBM],
        target=pltpu.HBM,
        aliases={len(late): 0},
    )
    return result[None]


def solution(mesh):
    rows = P(("dp", "node", "local"), None)
    weights = P("local", "node", None)
    return jax.shard_map(
        on_device,
        mesh=mesh,
        in_specs=(rows, rows, rows, weights, weights),
        out_specs=weights,
        check_vma=False,
    )
```

```python
import functools
import jax
import jax.numpy as jnp
from jax import lax
from jax.experimental import pallas as pl
from jax.experimental.pallas import tpu as pltpu
from jax.sharding import PartitionSpec as P

QB = 32
SPLITS = ((2,), (1, 1))
F32 = jnp.float32
BF16 = jnp.bfloat16


def mate(i, k, size):
    return i ^ k if size & (size - 1) == 0 else (i + k) % size


def traced_mate(i, k, size):
    return lax.bitwise_xor(i, jnp.int32(k)) if size & (size - 1) == 0 else lax.rem(i + k, size)


def traced_origin(i, k, size):
    if size & (size - 1) == 0:
        return lax.bitwise_xor(i, jnp.int32(k))
    return lax.rem(i + (size - k), size)


def call(body, outs, args, scratch=(), flops=0, space=pltpu.VMEM, target=pltpu.VMEM, aliases=None):
    moved = sum(a.size * a.dtype.itemsize for a in args)
    moved += sum(o.size * o.dtype.itemsize for o in outs)
    spaces = space if isinstance(space, list) else [space] * len(args)
    room = 2 * moved + (8 << 20)

    def kernel(*refs):
        body([lax.axis_index(name) for name in ("dp", "node", "local")], *refs)

    return pl.pallas_call(
        kernel,
        out_shape=outs,
        in_specs=[pl.BlockSpec(memory_space=kind) for kind in spaces],
        out_specs=[pl.BlockSpec(memory_space=target)] * len(outs),
        scratch_shapes=list(scratch),
        input_output_aliases=aliases or {},
        compiler_params=pltpu.CompilerParams(vmem_limit_bytes=min(room, 60 << 20)),
        cost_estimate=pl.CostEstimate(flops=flops, bytes_accessed=moved, transcendentals=0),
    )(*args)


def node_order(nodes):
    return [s for s in (3, 1, 2) if s < nodes] + list(range(4, nodes))


def plan_of(nodes, aligned):
    order = node_order(nodes)
    every = order + [0]
    chunks = sum(len(split) for split in SPLITS)
    if not aligned:
        return [every], [([i], every) for i in range(chunks)], [[i] for i in range(chunks)]
    early, late = order[: nodes // 2], order[nodes // 2 :] + [0]
    jobs = [([0], early), ([0], late)] + [([i], every) for i in range(1, chunks)]
    return [early, late], jobs, [[i] for i in range(chunks)]


def slots_of(copies, pairs):
    slots = [(j, k) for k in range(pairs) for j in range(copies) if j or k]
    return sorted(slots, key=lambda slot: -(slot[0] > 0) - (slot[1] > 0))


def shape(rows, cols, dtype):
    return jax.ShapeDtypeStruct((rows, cols), dtype)


def prep_body(pos, rows, codes, scales, *refs):
    near, outs = refs[0], refs[1:-4]
    raw, steps, wide, sems = refs[-4:]
    mine, ff = raw.shape
    at = pl.multiple_of(pos[0] * mine, 16)
    moves = [
        pltpu.make_async_copy(scales, steps, sems.at[0]),
        pltpu.make_async_copy(codes.at[pl.ds(at, mine), :], raw, sems.at[1]),
        pltpu.make_async_copy(rows, near, sems.at[2]),
    ]
    for move in moves:
        move.start()
    moves[0].wait()
    wide[...] = steps[...].astype(F32)
    used = max(1, mine // QB)
    begin = lax.div(pos[0] * mine, jnp.int32(QB))
    if used % 8 == 0:
        begin = pl.multiple_of(begin, 8)
    factors = wide[pl.ds(begin, used), :]
    moves[1].wait()
    blocks = raw[...].astype(F32).reshape(used, mine // used, ff)
    kept = (blocks * factors[:, None, :]).astype(BF16).reshape(mine, ff)
    begin = 0
    for out in outs:
        end = begin + out.shape[1]
        out[...] = kept[:, begin:end]
        begin = end
    moves[2].wait()


def select_body(dims, stride, pos, ids, ids_pair, *picks):
    _, _, locals_ = dims
    pairs = locals_ // 2
    count = ids.shape[1]
    high = max(16, pairs)
    first = lax.broadcasted_iota(jnp.int32, (count, count), 0)
    second = lax.broadcasted_iota(jnp.int32, (count, count), 1)
    earlier = (first < second).astype(F32).astype(BF16)
    places = lax.broadcasted_iota(jnp.int32, (pairs * stride, count), 0)
    owner = lax.shift_right_logical(pos[2], 1)
    held = jnp.zeros((high, 1), F32)
    for chosen, pick in zip((ids[...], ids_pair[...]), picks):
        group = lax.shift_right_logical(chosen, 1)
        if pairs & (pairs - 1) == 0:
            relative = lax.bitwise_xor(group, owner)
        else:
            relative = lax.rem(group - owner + pairs, pairs)
        mine = lax.bitwise_and(chosen, 1) == lax.bitwise_and(pos[2], 1)
        relative = jnp.where(mine, relative, high)
        onehot = relative == lax.broadcasted_iota(jnp.int32, (high, count), 0)
        marks = onehot.astype(F32)
        ranks = held + jnp.dot(marks.astype(BF16), earlier, preferred_element_type=F32)
        rank = jnp.sum(jnp.where(onehot, ranks, 0.0), axis=0, keepdims=True)
        slot = jnp.where(mine, relative * stride + rank.astype(jnp.int32), -1)
        pick[...] = (slot == places).astype(F32).astype(BF16)
        held = held + jnp.sum(marks, axis=1, keepdims=True)


def place_rows(dims, stride, columns, pos, picks, sources, outs):
    copies, nodes, locals_ = dims
    pairs = locals_ // 2
    rows, width = outs[0].shape[0], outs[0].shape[1] // len(columns[0])
    for g, group in enumerate(columns):
        for j in reversed(range(copies)):
            which = traced_mate(pos[0], j, copies)
            for b, (relative, block) in enumerate(group):
                if relative:
                    block = traced_mate(pos[1], block, nodes)
                at = pl.multiple_of((block * copies + which) * width, 128)
                got = sum(
                    jnp.dot(pick[...], source[:, pl.ds(at, width)], preferred_element_type=F32)
                    for pick, source in zip(picks, sources)
                ).astype(BF16)
                for k in range(pairs):
                    out = outs[(g * copies + j) * pairs + k]
                    out[:, b * width : (b + 1) * width] = got[k * stride : k * stride + rows]


def route_body(dims, stride, columns, pos, pick, pick_pair, rows, rows_pair, *outs):
    place_rows(dims, stride, columns, pos, (pick, pick_pair), (rows, rows_pair), outs)


def join_body(dims, stride, pos, *refs):
    copies, _, locals_ = dims
    pairs = locals_ // 2
    pieces, out = refs[:-1], refs[-1]
    rows, width = pieces[0].shape
    for j in range(copies):
        base = traced_origin(pos[0], j, copies) * (pairs * stride)
        for k in range(pairs):
            at = pl.multiple_of(base + k * stride, 16)
            block = pieces[j * pairs + k][...]
            if rows < stride:
                blank = jnp.zeros((stride - rows, width), block.dtype)
                block = jnp.concatenate([block, blank], axis=0)
            out[pl.ds(at, stride), :] = block


def turn_body(dims, stride, pos, *refs):
    pieces, out, held = refs[:-2], refs[-2], refs[-1]
    join_body(dims, stride, pos, *pieces, held)
    out[...] = jnp.transpose(held[...])


def up_body(dims, stride, given, pos, *refs):
    nodes = dims[1]
    pieces, weights, held = refs[:given], refs[given : given + nodes], refs[-1]
    outs = refs[given + nodes : -1]
    rows = pieces[0]
    if given > 1:
        rows, outs = outs[0], outs[1:]
        join_body(dims, stride, pos, *pieces, rows)
    mine = weights[0].shape[0]
    for s in range(nodes):
        at = pl.multiple_of(traced_origin(pos[1], s, nodes) * mine, 16)
        held[pl.ds(at, mine), :] = weights[s][...]
    begin = 0
    for kept, sent in zip(outs[::2], outs[1::2]):
        end = begin + kept.shape[1]
        pre = jnp.dot(rows[...], held[:, begin:end], preferred_element_type=F32)
        kept[...] = pre
        sent[...] = pre.astype(BF16)
        begin = end


def down_body(dims, factor, spots, sources, emits, pos, *refs):
    nodes = dims[1]
    tables = 1 + max(table for _, table, _ in spots)
    turned, rest, act = refs[:tables], list(refs[tables:-1]), refs[-1]
    begin = 0
    used = sum(sources)
    outs, kept_acts = rest[used : used + len(spots)], rest[used + len(spots) :]
    for held, emit in zip(sources, emits):
        if held and rest[0].dtype == F32:
            pre = rest[0][...]
            for part in rest[1:held]:
                pre = pre + part[...].astype(F32)
            value = (pre * jax.nn.sigmoid(pre)).astype(BF16)
        else:
            value = rest[0][...]
        rest = rest[held:]
        end = begin + value.shape[1]
        act[:, begin:end] = value
        if emit:
            kept_acts[0][...] = value
            kept_acts = kept_acts[1:]
        begin = end
    mine = outs[0].shape[0]
    for (s, table, place), out in zip(spots, outs):
        at = place * mine
        if place < 0:
            at = pl.multiple_of(traced_mate(pos[1], s, nodes) * mine, 16)
        term = jnp.dot(turned[table][pl.ds(at, mine), :], act[...], preferred_element_type=F32)
        out[...] = (term * factor).astype(out.dtype)


def sum_body(begins, pos, own, *refs):
    total, out = refs[-1], refs[-2]
    total[...] = own[...]
    for begin, part in zip(begins, refs[:-2]):
        end = begin + part.shape[1]
        total[:, begin:end] += part[...].astype(F32)
    out[...] = total[...].astype(BF16)


def lay_body(dims, spots, pos, *refs):
    copies = dims[0]
    parts, out, sems = refs[: len(spots)], refs[-2], refs[-1]
    moves = []
    for i, (part, (j, begin)) in enumerate(zip(parts, spots)):
        mine, width = part.shape
        at = pl.multiple_of(traced_origin(pos[0], j, copies) * mine, 16)
        spot = out.at[pl.ds(at, mine), pl.ds(begin, width)]
        moves.append(pltpu.make_async_copy(part, spot, sems.at[i]))
    for move in moves:
        move.start()
    for move in moves:
        move.wait()


def on_device(tokens, cotangent, expert_of, w1_codes, w1_scales):
    copies, nodes, locals_ = (lax.axis_size(a) for a in ("dp", "node", "local"))
    dims = (copies, nodes, locals_)
    count, features = tokens.shape
    capacity = 5 * count // (4 * locals_)
    pairs = locals_ // 2
    sent_rows = -(-2 * capacity // 8) * 8
    stride = -(-sent_rows // 16) * 16
    shard, hidden = w1_codes.shape[1:]
    mine = shard // copies
    part = features // copies
    unit = hidden // sum(sum(split) for split in SPLITS)
    gathered = [unit * sum(split) for split in SPLITS]
    everyone = copies * pairs * stride

    aligned = mine % 128 == 0
    halves, jobs, outputs = plan_of(nodes, aligned)
    if aligned:
        columns_x = [[(False, b) for b in range(nodes)]]
        columns_y = [[(True, s) for s in half] for half in halves]
    else:
        columns_x = columns_y = [[(False, 0)]]
        tokens, cotangent = (
            a.reshape(count, nodes, copies, mine).swapaxes(1, 2).reshape(count, features)
            for a in (tokens, cotangent)
        )
    chosen = expert_of.reshape(1, count)
    swap = [(i, i ^ 1) for i in range(locals_)]
    tokens_pair = lax.ppermute(tokens, "local", swap)
    chosen_pair = lax.ppermute(chosen, "local", swap)
    cotangent_pair = lax.ppermute(cotangent, "local", swap)

    far = [pltpu.with_memory_space_constraint(a, pltpu.HBM) for a in (tokens, w1_codes[0], w1_scales[0])]
    tokens, *weights = call(
        prep_body,
        [shape(count, features, BF16)] + [shape(mine, w, BF16) for w in gathered],
        far,
        [
            pltpu.VMEM((mine, hidden), BF16),
            pltpu.VMEM((shard // QB, hidden), BF16),
            pltpu.VMEM((shard // QB, hidden), F32),
            pltpu.SemaphoreType.DMA((3,)),
        ],
        space=pltpu.HBM,
    )
    picks = call(
        functools.partial(select_body, dims, stride),
        [shape(pairs * stride, count, BF16)] * 2,
        [chosen, chosen_pair],
    )
    order = node_order(nodes)
    held = []
    for chunk in weights:
        got = {0: chunk}
        for s in order:
            got[s] = lax.ppermute(chunk, "node", [(a, mate(a, s, nodes)) for a in range(nodes)])
        held.append([got[s] for s in range(nodes)])

    def route(columns, rows, rows_pair):
        pieces = call(
            functools.partial(route_body, dims, stride, columns),
            [shape(sent_rows, part // len(columns), BF16)] * (len(columns) * copies * pairs),
            [*picks, rows, rows_pair],
            flops=4 * pairs * stride * count * features,
        )
        step = copies * pairs
        return [pieces[g * step : (g + 1) * step] for g in range(len(columns))]

    (pieces_x,) = route(columns_x, tokens, tokens_pair)
    pieces_y = route(columns_y, cotangent, cotangent_pair)

    def exchange(pieces):
        moved = list(pieces)
        for j, k in slots_of(copies, pairs):
            links = [
                (a * locals_ + b, mate(a, j, copies) * locals_ + 2 * mate(b // 2, k, pairs) + b % 2)
                for a in range(copies)
                for b in range(locals_)
            ]
            at = j * pairs + k
            moved[at] = lax.ppermute(pieces[at], ("dp", "local"), links)
        return moved

    rows_x = exchange(pieces_x)
    turned = []
    for h, pieces in enumerate(pieces_y):
        cols = part // len(pieces_y)
        got_dy = exchange(pieces)
        turned += call(
            functools.partial(turn_body, dims, stride),
            [shape(cols, everyone, BF16)],
            got_dy,
            [pltpu.VMEM((everyone, cols), BF16)],
        )
    factor = float(count * copies * nodes) ** (-0.5)
    groups = []
    for i, split in enumerate(SPLITS):
        widths = [unit * share for share in split]
        joined = [shape(everyone, part, BF16)] if len(rows_x) > 1 else []
        parts = call(
            functools.partial(up_body, dims, stride, len(rows_x)),
            joined + [shape(everyone, w, kind) for w in widths for kind in (F32, BF16)],
            list(rows_x) + held[i],
            [pltpu.VMEM((part, gathered[i]), BF16)],
            flops=2 * everyone * part * gathered[i],
        )
        if joined:
            rows_x, parts = parts[:1], parts[1:]
        groups += list(zip(widths, parts[::2], parts[1::2]))
    acts = []
    for wide, kept, sent in groups:
        if copies == 2:
            acts.append([kept, lax.ppermute(sent, "dp", [(0, 1), (1, 0)])])
        else:
            acts.append([lax.psum(kept, "dp")])
    owns, arrived = {}, {}
    for n, (chunks, targets) in enumerate(jobs):
        wide = sum(groups[i][0] for i in chunks)
        tables = [h for h, half in enumerate(halves) if set(half) & set(targets)]
        spots = []
        for s in targets:
            (h,) = [h for h in tables if s in halves[h]]
            spots.append((s, tables.index(h), halves[h].index(s) if aligned else -1))
        again = [any(i in other for other, _ in jobs[n + 1 :]) for i in chunks]
        emits = [more and acts[i][0].dtype == F32 for i, more in zip(chunks, again)]
        kinds = [shape(mine, wide, BF16 if s else F32) for s in targets]
        kinds += [shape(everyone, groups[i][0], BF16) for i, emit in zip(chunks, emits) if emit]
        terms = call(
            functools.partial(down_body, dims, factor, spots, [len(acts[i]) for i in chunks], emits),
            kinds,
            [turned[h] for h in tables] + sum((acts[i] for i in chunks), []),
            [pltpu.VMEM((everyone, wide), BF16)],
            flops=2 * everyone * len(targets) * mine * wide,
        )
        extra = list(terms[len(targets) :])
        for i, emit in zip(chunks, emits):
            if emit:
                acts[i] = [extra.pop(0)]
        (group,) = [g for g, members in enumerate(outputs) if chunks[0] in members]
        begin = sum(groups[i][0] for i in outputs[group] if i < chunks[0])
        for s, term in zip(targets, terms):
            if s == 0:
                owns[group] = term
                continue
            links = [(a, mate(a, s, nodes)) for a in range(nodes)]
            moved = lax.ppermute(term, "node", links)
            arrived.setdefault(group, []).append((begin, moved))
    finished = []
    for i in range(len(outputs)):
        wide = owns[i].shape[1]
        begins = [begin for begin, _ in arrived[i]]
        (summed,) = call(
            functools.partial(sum_body, begins),
            [shape(mine, wide, BF16)],
            [owns[i]] + [moved for _, moved in arrived[i]],
            [pltpu.VMEM((mine, wide), F32)],
        )
        finished.append(summed)
        for j in range(1, copies):
            links = [(a, mate(a, j, copies)) for a in range(copies)]
            finished.append(lax.ppermute(summed, "dp", links))
    spots = []
    begin = 0
    for i in range(len(outputs)):
        spots += [(j, begin) for j in range(copies)]
        begin += owns[i].shape[1]
    items = list(zip(finished, spots))
    sure = copies * max(0, len(outputs) - 2)
    soon = [item for i, item in enumerate(items) if i < sure or item[1][0] == 0]
    late = [item for i, item in enumerate(items) if i >= sure and item[1][0] > 0]
    (result,) = call(
        functools.partial(lay_body, dims, [spot for _, spot in soon]),
        [shape(shard, hidden, BF16)],
        [value for value, _ in soon],
        [pltpu.SemaphoreType.DMA((len(soon),))],
        target=pltpu.HBM,
    )
    (result,) = call(
        functools.partial(lay_body, dims, [spot for _, spot in late]),
        [shape(shard, hidden, BF16)],
        [value for value, _ in late] + [result],
        [pltpu.SemaphoreType.DMA((len(late),))],
        space=[pltpu.VMEM] * len(late) + [pltpu.HBM],
        target=pltpu.HBM,
        aliases={len(late): 0},
    )
    return result[None]


def solution(mesh):
    rows = P(("dp", "node", "local"), None)
    weights = P("local", "node", None)
    return jax.shard_map(
        on_device,
        mesh=mesh,
        in_specs=(rows, rows, rows, weights, weights),
        out_specs=weights,
        check_vma=False,
    )
```
